512 devices in a mesh: blk: 8 (over z_lo), stripe: 64 (over y, x, z_hi, core).
Axes of the slice: x: 4, y: 4, z: 16 (z_hi: 2, z_lo: 8; z = z_hi * 8 + z_lo), core: 2. Of those that a mesh axis runs over, the one named last changes fastest.
Arguments:
- points: bfloat16 [262144, 64], P(('blk', 'stripe')), may hold values from -6 to 6
- coefficients: float32 [262144], P(('blk', 'stripe')), may hold values from -0.0234375 to 0.0234375
- velocity: float32 [262144], P(('blk', 'stripe')), may hold values from -0.0234375 to 0.0234375
- targets: float32 [262144], P(('blk', 'stripe')), may hold values from -6 to 6
- batch_rows: int32 [32768], P(('blk', 'stripe')), may hold values from 0 to 511
- counts: int32 [8, 64], P('blk', 'stripe'), may hold values from 1 to 64, 2048 in all within a row
Outputs:
- new_coefficients: float32 [262144], P(('blk', 'stripe'))
- new_velocity: float32 [262144], P(('blk', 'stripe'))
The draws below stay inside these ranges and needn't reach their ends.
Inputs may be any that keep to these rules, and one draw needn't show every extreme that they name: In every index of blk, the counts of its 64 devices sum to exactly 2048, and some device's count is exactly 64. Only the first count entries of a device's slots are live. `batch_rows`: every entry, live or not, indexes the points of the device that holds it; rows may repeat.
All inputs are finite; a program needn't handle non-finite values.
Results may differ from the reference program's by a relative error of at most 0.0003.
Values may be sent and summed in bfloat16 or wider, within the bound.
A program may use at most 64 MiB of HBM per device.

```python
import math
import jax
import jax.numpy as jnp
import numpy as np
from jax import lax

D = 64
PTS_DEV = 512
SLOTS = 64
NPTS = 262144
ROWS = 32768
N_BLK = 8
N_STRIPE = 64
DEVICES = 512


def plant(values, own_key, smallest, top_value):
    longest = values.shape.index(max(values.shape))
    spots = []
    for shift in (0, 1):
        where = [jax.random.randint(jax.random.fold_in(own_key, axis), (), 0, length) for axis, length in enumerate(values.shape)]
        where[longest] = (where[longest] + shift) % values.shape[longest]
        spots.append(tuple(where))
    return values.at[spots[0]].set(smallest).at[spots[1]].set(top_value)


def block_scale(own_key, shape, cuts, low, top_value):
    def one(dim, blocks):
        draws = jax.random.uniform(jax.random.fold_in(jax.random.fold_in(own_key, 6), dim), (blocks,), jnp.float32, low / len(cuts), top_value / len(cuts))
        return jnp.repeat(jnp.exp(draws), shape[dim] // blocks).reshape((-1,) + (1,) * (len(shape) - dim - 1))

    gain = one(*cuts[0])
    for cut in cuts[1:]:
        gain = gain * one(*cut)
    return gain


def length_profile(amount, total, reach, lean):
    weights = [(1 << 20) // math.isqrt(rank ** lean) + 1 for rank in range(2, amount + 1)]
    spare, given = total - reach - (amount - 1), [1] * (amount - 1)
    while spare > 0:
        candidates = [i for i in range(amount - 1) if given[i] < reach]
        pool, remaining = sum([weights[i] for i in candidates]), spare
        for i in candidates:
            extra = min(reach - given[i], max(1, remaining * weights[i] // pool), spare)
            given[i] = given[i] + extra
            spare = spare - extra
    return np.array([reach] + given)


def ragged(rng, number_of, total, most, skew):
    if number_of == 2:
        one = jax.random.randint(rng, (), max(1, total - most), min(most, total - 1) + 1)
        return jnp.stack([one, total - one])
    lengths = jnp.asarray(length_profile(number_of, total, most, skew), jnp.int32)
    twos = (number_of - 1) // 2
    donor, sink = lengths[1:1 + 2 * twos:2], lengths[2:2 + 2 * twos:2]
    room = jnp.minimum(donor - 1, most - sink)
    moved = jax.random.randint(jax.random.fold_in(rng, 1), (twos,), 0, 1 << 20) % (room + 1)
    lengths = lengths.at[1:1 + 2 * twos:2].set(donor - moved).at[2:2 + 2 * twos:2].set(sink + moved)
    return lengths[jax.random.permutation(jax.random.fold_in(rng, 2), number_of)]


def gaussian(own_key, dims, scale, reach, shards=(), held_as=jnp.bfloat16):
    values = jax.random.normal(own_key, dims, jnp.float32) * scale
    if len(shards) > 0:
        values = block_scale(own_key, dims, shards, -0.22, 0.18) * values
    return jnp.clip(values, min=-reach, max=reach).astype(held_as)


def setup_inputs(seed: int = 0) -> dict:
    seeds = jax.random.split(jax.random.key(seed), 7)
    return {
        "points": gaussian(seeds[0], (NPTS, D), 1.0, 6.0, ((0, 512),)),
        "coefficients": gaussian(seeds[1], (NPTS,), (NPTS // 4) ** -0.5, 0.0234375, ((0, 512),), jnp.float32),
        "velocity": gaussian(seeds[2], (NPTS,), (NPTS // 4) ** -0.5, 0.0234375, ((0, 512),), jnp.float32),
        "targets": gaussian(seeds[3], (NPTS,), 1.0, 6.0, ((0, 512),), jnp.float32),
        "batch_rows": plant(jax.random.randint(seeds[4], (ROWS,), 0, PTS_DEV), jax.random.fold_in(seeds[4], 1), 0, PTS_DEV - 1).astype(jnp.int32),
        "counts": jax.vmap(lambda own: ragged(own, N_STRIPE, N_STRIPE * SLOTS // 2, SLOTS, 2))(jax.random.split(seeds[5], N_BLK)).reshape((N_BLK, N_STRIPE)).astype(jnp.int32),
    }


MOMENTUM = 0.9
STEP_SIZE = 1.0
NOISE_VAR = 8.0
KERNEL_RATE = 3.0 ** 0.5 / 6.0

def matern_sums(row_feats, row_sq, col_points, col_coef):
    col_sq = lax.optimization_barrier(jnp.sum(jnp.square(col_points.astype(jnp.float32)), axis=1))
    inner_prod = lax.dot_general(row_feats, col_points, (((1,), (1,)), ((), ())), preferred_element_type=jnp.float32)
    distance = jnp.sqrt(jnp.maximum(row_sq[:, None] + col_sq[None, :] - 2.0 * inner_prod, 0.0))
    scaled = KERNEL_RATE * distance
    kernel_tile = (1.0 + scaled) * jnp.exp(-scaled)
    return lax.optimization_barrier(jnp.sum(kernel_tile * col_coef[None, :], axis=1))

def reference(points, coefficients, velocity, targets, batch_rows, counts):
    preview = coefficients + MOMENTUM * velocity
    device_ids = jnp.arange(DEVICES, dtype=jnp.int32)
    slot_ids = jnp.arange(SLOTS, dtype=jnp.int32)
    point_of = (device_ids[:, None] * PTS_DEV + batch_rows.reshape(DEVICES, SLOTS)).reshape(-1).astype(jnp.int32)
    in_count = (slot_ids[None, :] < counts.reshape(DEVICES, 1)).reshape(-1)
    picked = points[point_of]
    picked_sq = lax.optimization_barrier(jnp.sum(jnp.square(picked.astype(jnp.float32)), axis=1))
    col_block = math.gcd(NPTS, 8192)
    point_blocks = points.reshape(-1, col_block, D)
    coef_blocks = preview.reshape(-1, col_block)
    row_block = math.gcd(ROWS, 2048)

    def block_sums(block_args):
        feat_block, sq_block = block_args

        def advance(partial_sum, column_block):
            return (partial_sum + matern_sums(feat_block, sq_block, column_block[0], column_block[1]), None)
        result, unused = lax.scan(advance, jnp.zeros((feat_block.shape[0],), jnp.float32), (point_blocks, coef_blocks))
        return result
    kernel_sums = lax.map(block_sums, (picked.reshape(-1, row_block, D), picked_sq.reshape(-1, row_block))).reshape(-1)
    residual = jnp.where(in_count, kernel_sums + NOISE_VAR * preview[point_of] - targets[point_of], 0.0)
    update_sum = jnp.zeros((NPTS,), jnp.float32).at[point_of].add(residual)
    new_velocity = MOMENTUM * velocity - STEP_SIZE * update_sum
    new_coefficients = coefficients + new_velocity
    return (new_coefficients, new_velocity)
```

```python
import functools
import math

import jax
import jax.numpy as jnp
from jax import lax
from jax.experimental import pallas as pl
from jax.experimental.pallas import tpu as pltpu
from jax.sharding import PartitionSpec as P

MOMENTUM = 0.9
STEP_SIZE = 1.0
NOISE_VAR = 8.0
KERNEL_RATE = 3.0**0.5 / 6.0

MESH_ID = pl.DeviceIdType.MESH
ANY = pl.BlockSpec(memory_space=pl.ANY)


def gather_kernel(n_blk, n_str, picked, pts, prev, rows_out, pts_out, prev_out,
                  row_send, row_recv, pt_send, pt_recv, pv_send, pv_recv, local_sem):
    b = lax.axis_index("blk")
    s = lax.axis_index("stripe")
    own = [
        pltpu.make_async_copy(picked, rows_out.at[s], local_sem.at[0]),
        pltpu.make_async_copy(pts, pts_out.at[b], local_sem.at[1]),
        pltpu.make_async_copy(prev, prev_out.at[b], local_sem.at[2]),
    ]
    for c in own:
        c.start()

    def row_copy(i, src):
        peer = lax.rem(s + 1 + i, n_str)
        return pltpu.make_async_remote_copy(
            src_ref=picked, dst_ref=rows_out.at[src], send_sem=row_send.at[i],
            recv_sem=row_recv.at[src], device_id=(b, peer), device_id_type=MESH_ID)

    def blk_copies(i, src):
        peer = lax.rem(b + 1 + i, n_blk)
        return (
            pltpu.make_async_remote_copy(
                src_ref=pts, dst_ref=pts_out.at[src], send_sem=pt_send.at[i],
                recv_sem=pt_recv.at[src], device_id=(peer, s), device_id_type=MESH_ID),
            pltpu.make_async_remote_copy(
                src_ref=prev, dst_ref=prev_out.at[src], send_sem=pv_send.at[i],
                recv_sem=pv_recv.at[src], device_id=(peer, s), device_id_type=MESH_ID),
        )

    def start_blk(i, carry):
        for c in blk_copies(i, b):
            c.start()
        return carry

    def start_row(i, carry):
        row_copy(i, s).start()
        return carry

    lax.fori_loop(0, n_blk - 1, start_blk, 0)
    lax.fori_loop(0, n_str - 1, start_row, 0)

    def wait_row(i, carry):
        row_copy(i, s).wait_send()
        src = lax.rem(s + 2 * n_str - 1 - i, n_str)
        row_copy(i, src).wait_recv()
        return carry

    def wait_blk(i, carry):
        for c in blk_copies(i, b):
            c.wait_send()
        src = lax.rem(b + 2 * n_blk - 1 - i, n_blk)
        for c in blk_copies(i, src):
            c.wait_recv()
        return carry

    lax.fori_loop(0, n_blk - 1, wait_blk, 0)
    lax.fori_loop(0, n_str - 1, wait_row, 0)
    for c in own:
        c.wait()


def gather_all(picked, pts, prev, n_blk, n_str):
    dma = pltpu.SemaphoreType.DMA
    return pl.pallas_call(
        functools.partial(gather_kernel, n_blk, n_str),
        out_shape=(
            jax.ShapeDtypeStruct((n_str,) + picked.shape, picked.dtype),
            jax.ShapeDtypeStruct((n_blk,) + pts.shape, pts.dtype),
            jax.ShapeDtypeStruct((n_blk,) + prev.shape, prev.dtype),
        ),
        in_specs=[ANY, ANY, ANY],
        out_specs=(ANY, ANY, ANY),
        scratch_shapes=[
            dma((n_str,)), dma((n_str,)), dma((n_blk,)), dma((n_blk,)),
            dma((n_blk,)), dma((n_blk,)), dma((3,)),
        ],
        compiler_params=pltpu.CompilerParams(has_side_effects=True),
    )(picked, pts, prev)


def scatter_kernel(n_str, part, recv_out, send_sem, recv_sem, local_sem):
    b = lax.axis_index("blk")
    s = lax.axis_index("stripe")
    own = pltpu.make_async_copy(part.at[s], recv_out.at[s], local_sem.at[0])
    own.start()

    def copy(i, src):
        peer = lax.rem(s + 1 + i, n_str)
        return pltpu.make_async_remote_copy(
            src_ref=part.at[peer], dst_ref=recv_out.at[src], send_sem=send_sem.at[i],
            recv_sem=recv_sem.at[src], device_id=(b, peer), device_id_type=MESH_ID)

    def start(i, carry):
        copy(i, s).start()
        return carry

    lax.fori_loop(0, n_str - 1, start, 0)

    def wait(i, carry):
        copy(i, s).wait_send()
        src = lax.rem(s + 2 * n_str - 1 - i, n_str)
        copy(i, src).wait_recv()
        return carry

    lax.fori_loop(0, n_str - 1, wait, 0)
    own.wait()


def scatter_all(part, n_str):
    dma = pltpu.SemaphoreType.DMA
    return pl.pallas_call(
        functools.partial(scatter_kernel, n_str),
        out_shape=jax.ShapeDtypeStruct(part.shape, part.dtype),
        in_specs=[ANY],
        out_specs=ANY,
        scratch_shapes=[dma((n_str,)), dma((n_str,)), dma((1,))],
        compiler_params=pltpu.CompilerParams(has_side_effects=True),
    )(part)


def matern_sums(row_feats, row_sq, col_points, col_coef):
    col_sq = jnp.sum(jnp.square(col_points.astype(jnp.float32)), axis=1)
    inner_prod = lax.dot_general(
        row_feats, col_points, (((1,), (1,)), ((), ())), preferred_element_type=jnp.float32
    )
    distance = jnp.sqrt(jnp.maximum(row_sq[:, None] + col_sq[None, :] - 2.0 * inner_prod, 0.0))
    scaled = KERNEL_RATE * distance
    kernel_tile = (1.0 + scaled) * jnp.exp(-scaled)
    return jnp.sum(kernel_tile * col_coef[None, :], axis=1)


def column_sums(row_feats, piece_points, every_coef):
    row_sq = jnp.sum(jnp.square(row_feats.astype(jnp.float32)), axis=1)
    zeros_init = jnp.zeros((row_feats.shape[0],), jnp.float32)
    piece_len = piece_points.shape[0]
    block_len = math.gcd(piece_len, 512)
    point_blocks = piece_points.reshape(-1, block_len, piece_points.shape[1])
    coef_blocks = every_coef.reshape(-1, block_len)

    def advance(partial_sum, column_block):
        return (
            partial_sum + matern_sums(row_feats, row_sq, column_block[0], column_block[1]),
            None,
        )

    result, unused = lax.scan(advance, zeros_init, (point_blocks, coef_blocks))
    return result


def per_device(n_blk, n_str, points, coefficients, velocity, targets, batch_rows, counts):
    preview = coefficients + MOMENTUM * velocity
    slot_total = batch_rows.shape[0]
    local_size = points.shape[0]
    slot_ids = jnp.arange(slot_total, dtype=jnp.int32)
    count_here = counts.reshape((1,))
    in_count = slot_ids < count_here[0]
    picked = jnp.take(points, batch_rows, axis=0)
    rows_all, pts_all, prev_all = gather_all(picked, points, preview.reshape(1, -1), n_blk, n_str)
    group_rows = rows_all.reshape(-1, points.shape[1])
    piece_points = pts_all.reshape(-1, points.shape[1])
    every_coef = prev_all.reshape(-1)
    partial_value = column_sums(group_rows, piece_points, every_coef)
    received = scatter_all(partial_value.reshape(n_str, 1, slot_total), n_str)
    kernel_rows = jnp.sum(received.reshape(n_str, slot_total), axis=0)
    residual = jnp.where(
        in_count,
        kernel_rows + NOISE_VAR * jnp.take(preview, batch_rows) - jnp.take(targets, batch_rows),
        0.0,
    )
    scatter_rows = (batch_rows[:, None] == jnp.arange(local_size, dtype=jnp.int32)[None, :]).astype(
        jnp.float32
    )
    update_sum = jnp.dot(residual, scatter_rows, precision=lax.Precision.HIGHEST)
    new_velocity = MOMENTUM * velocity - STEP_SIZE * update_sum
    new_coefficients = coefficients + new_velocity
    return (new_coefficients, new_velocity)


def solution(mesh):
    n_blk = mesh.shape["blk"]
    n_str = mesh.shape["stripe"]
    in_specs = (
        P(("blk", "stripe"), None),
        P(("blk", "stripe")),
        P(("blk", "stripe")),
        P(("blk", "stripe")),
        P(("blk", "stripe")),
        P("blk", "stripe"),
    )
    out_specs = (P(("blk", "stripe")), P(("blk", "stripe")))
    return jax.shard_map(
        functools.partial(per_device, n_blk, n_str), mesh=mesh, in_specs=in_specs,
        out_specs=out_specs, check_vma=False
    )
```

```python
import functools
import math

import jax
import jax.numpy as jnp
from jax import lax
from jax.experimental import pallas as pl
from jax.experimental.pallas import tpu as pltpu
from jax.sharding import PartitionSpec as P

MOMENTUM = 0.9
STEP_SIZE = 1.0
NOISE_VAR = 8.0
KERNEL_RATE = 3.0**0.5 / 6.0

MESH_ID = pl.DeviceIdType.MESH
ANY = pl.BlockSpec(memory_space=pl.ANY)


def gather_kernel(n_blk, n_in, n_out, picked, pts, prev, rows_out, pts_out, prev_out,
                  in_send, in_recv, out_send, out_recv, pt_send, pt_recv, pv_send, pv_recv,
                  local_sem):
    b = lax.axis_index("blk")
    s = lax.axis_index("stripe")
    u = s // n_in
    v = lax.rem(s, n_in)
    own = [
        pltpu.make_async_copy(picked, rows_out.at[u, v], local_sem.at[0]),
        pltpu.make_async_copy(pts, pts_out.at[b], local_sem.at[1]),
        pltpu.make_async_copy(prev, prev_out.at[b], local_sem.at[2]),
    ]
    for c in own:
        c.start()

    def inner_copy(i, src):
        peer = lax.rem(v + 1 + i, n_in)
        return pltpu.make_async_remote_copy(
            src_ref=picked, dst_ref=rows_out.at[u, src], send_sem=in_send.at[i],
            recv_sem=in_recv.at[src], device_id=(b, u * n_in + peer), device_id_type=MESH_ID)

    def outer_copy(i, src):
        peer = lax.rem(u + 1 + i, n_out)
        return pltpu.make_async_remote_copy(
            src_ref=rows_out.at[u], dst_ref=rows_out.at[src], send_sem=out_send.at[i],
            recv_sem=out_recv.at[src], device_id=(b, peer * n_in + v), device_id_type=MESH_ID)

    def blk_copies(i, src):
        peer = lax.rem(b + 1 + i, n_blk)
        return (
            pltpu.make_async_remote_copy(
                src_ref=pts, dst_ref=pts_out.at[src], send_sem=pt_send.at[i],
                recv_sem=pt_recv.at[src], device_id=(peer, s), device_id_type=MESH_ID),
            pltpu.make_async_remote_copy(
                src_ref=prev, dst_ref=prev_out.at[src], send_sem=pv_send.at[i],
                recv_sem=pv_recv.at[src], device_id=(peer, s), device_id_type=MESH_ID),
        )

    def start_inner(i, carry):
        inner_copy(i, v).start()
        return carry

    def start_blk(i, carry):
        for c in blk_copies(i, b):
            c.start()
        return carry

    lax.fori_loop(0, n_in - 1, start_inner, 0)
    lax.fori_loop(0, n_blk - 1, start_blk, 0)

    def wait_inner(i, carry):
        inner_copy(i, v).wait_send()
        inner_copy(i, lax.rem(v + 2 * n_in - 1 - i, n_in)).wait_recv()
        return carry

    lax.fori_loop(0, n_in - 1, wait_inner, 0)
    own[0].wait()

    def start_outer(i, carry):
        outer_copy(i, u).start()
        return carry

    lax.fori_loop(0, n_out - 1, start_outer, 0)

    def wait_blk(i, carry):
        for c in blk_copies(i, b):
            c.wait_send()
        src = lax.rem(b + 2 * n_blk - 1 - i, n_blk)
        for c in blk_copies(i, src):
            c.wait_recv()
        return carry

    def wait_outer(i, carry):
        outer_copy(i, u).wait_send()
        outer_copy(i, lax.rem(u + 2 * n_out - 1 - i, n_out)).wait_recv()
        return carry

    lax.fori_loop(0, n_blk - 1, wait_blk, 0)
    lax.fori_loop(0, n_out - 1, wait_outer, 0)
    own[1].wait()
    own[2].wait()


def gather_all(picked, pts, prev, n_blk, n_in, n_out):
    dma = pltpu.SemaphoreType.DMA
    return pl.pallas_call(
        functools.partial(gather_kernel, n_blk, n_in, n_out),
        out_shape=(
            jax.ShapeDtypeStruct((n_out, n_in) + picked.shape, picked.dtype),
            jax.ShapeDtypeStruct((n_blk,) + pts.shape, pts.dtype),
            jax.ShapeDtypeStruct((n_blk,) + prev.shape, prev.dtype),
        ),
        in_specs=[ANY, ANY, ANY],
        out_specs=(ANY, ANY, ANY),
        scratch_shapes=[
            dma((n_in,)), dma((n_in,)), dma((n_out,)), dma((n_out,)),
            dma((n_blk,)), dma((n_blk,)), dma((n_blk,)), dma((n_blk,)), dma((3,)),
        ],
        compiler_params=pltpu.CompilerParams(has_side_effects=True),
    )(picked, pts, prev)


def scatter_kernel(n_in, n_out, part, total_out, stage1, mid, stage2,
                   out_send, out_recv, in_send, in_recv, local_sem):
    b = lax.axis_index("blk")
    s = lax.axis_index("stripe")
    u = s // n_in
    v = lax.rem(s, n_in)
    own1 = pltpu.make_async_copy(part.at[u], stage1.at[u], local_sem.at[0])
    own1.start()

    def outer_copy(i, src):
        peer = lax.rem(u + 1 + i, n_out)
        return pltpu.make_async_remote_copy(
            src_ref=part.at[peer], dst_ref=stage1.at[src], send_sem=out_send.at[i],
            recv_sem=out_recv.at[src], device_id=(b, peer * n_in + v), device_id_type=MESH_ID)

    def inner_copy(i, src):
        peer = lax.rem(v + 1 + i, n_in)
        return pltpu.make_async_remote_copy(
            src_ref=mid.at[peer], dst_ref=stage2.at[src], send_sem=in_send.at[i],
            recv_sem=in_recv.at[src], device_id=(b, u * n_in + peer), device_id_type=MESH_ID)

    def start_outer(i, carry):
        outer_copy(i, u).start()
        return carry

    lax.fori_loop(0, n_out - 1, start_outer, 0)

    def wait_outer(i, carry):
        outer_copy(i, u).wait_send()
        outer_copy(i, lax.rem(u + 2 * n_out - 1 - i, n_out)).wait_recv()
        return carry

    lax.fori_loop(0, n_out - 1, wait_outer, 0)
    own1.wait()
    mid[...] = jnp.sum(stage1[...], axis=0)[:, None, :]
    own2 = pltpu.make_async_copy(mid.at[v], stage2.at[v], local_sem.at[1])
    own2.start()

    def start_inner(i, carry):
        inner_copy(i, v).start()
        return carry

    lax.fori_loop(0, n_in - 1, start_inner, 0)

    def wait_inner(i, carry):
        inner_copy(i, v).wait_send()
        inner_copy(i, lax.rem(v + 2 * n_in - 1 - i, n_in)).wait_recv()
        return carry

    lax.fori_loop(0, n_in - 1, wait_inner, 0)
    own2.wait()
    total_out[...] = jnp.sum(stage2[...], axis=0)


def scatter_all(part, n_in, n_out):
    dma = pltpu.SemaphoreType.DMA
    vmem = pl.BlockSpec(memory_space=pltpu.VMEM)
    width = part.shape[-1]
    return pl.pallas_call(
        functools.partial(scatter_kernel, n_in, n_out),
        out_shape=jax.ShapeDtypeStruct((1, width), part.dtype),
        in_specs=[vmem],
        out_specs=vmem,
        scratch_shapes=[
            pltpu.VMEM((n_out, n_in, width), jnp.float32),
            pltpu.VMEM((n_in, 1, width), jnp.float32),
            pltpu.VMEM((n_in, 1, width), jnp.float32),
            dma((n_out,)), dma((n_out,)), dma((n_in,)), dma((n_in,)), dma((2,)),
        ],
        compiler_params=pltpu.CompilerParams(has_side_effects=True),
    )(part)


def matern_sums(row_feats, row_sq, col_points, col_coef):
    col_sq = jnp.sum(jnp.square(col_points.astype(jnp.float32)), axis=1)
    inner_prod = lax.dot_general(
        row_feats, col_points, (((1,), (1,)), ((), ())), preferred_element_type=jnp.float32
    )
    distance = jnp.sqrt(jnp.maximum(row_sq[:, None] + col_sq[None, :] - 2.0 * inner_prod, 0.0))
    scaled = KERNEL_RATE * distance
    kernel_tile = (1.0 + scaled) * jnp.exp(-scaled)
    return jnp.sum(kernel_tile * col_coef[None, :], axis=1)


def column_sums(row_feats, piece_points, every_coef):
    row_sq = jnp.sum(jnp.square(row_feats.astype(jnp.float32)), axis=1)
    zeros_init = jnp.zeros((row_feats.shape[0],), jnp.float32)
    piece_len = piece_points.shape[0]
    block_len = math.gcd(piece_len, 512)
    point_blocks = piece_points.reshape(-1, block_len, piece_points.shape[1])
    coef_blocks = every_coef.reshape(-1, block_len)

    def advance(partial_sum, column_block):
        return (
            partial_sum + matern_sums(row_feats, row_sq, column_block[0], column_block[1]),
            None,
        )

    result, unused = lax.scan(advance, zeros_init, (point_blocks, coef_blocks))
    return result


def per_device(n_blk, n_str, points, coefficients, velocity, targets, batch_rows, counts):
    preview = coefficients + MOMENTUM * velocity
    slot_total = batch_rows.shape[0]
    local_size = points.shape[0]
    slot_ids = jnp.arange(slot_total, dtype=jnp.int32)
    count_here = counts.reshape((1,))
    in_count = slot_ids < count_here[0]
    picked = jnp.take(points, batch_rows, axis=0)
    n_in = math.gcd(n_str, 8)
    n_out = n_str // n_in
    rows_all, pts_all, prev_all = gather_all(picked, points, preview.reshape(1, -1), n_blk, n_in, n_out)
    group_rows = rows_all.reshape(-1, points.shape[1])
    piece_points = pts_all.reshape(-1, points.shape[1])
    every_coef = prev_all.reshape(-1)
    partial_value = column_sums(group_rows, piece_points, every_coef)
    kernel_rows = scatter_all(partial_value.reshape(n_out, n_in, slot_total), n_in, n_out).reshape(-1)
    residual = jnp.where(
        in_count,
        kernel_rows + NOISE_VAR * jnp.take(preview, batch_rows) - jnp.take(targets, batch_rows),
        0.0,
    )
    scatter_rows = (batch_rows[:, None] == jnp.arange(local_size, dtype=jnp.int32)[None, :]).astype(
        jnp.float32
    )
    update_sum = jnp.dot(residual, scatter_rows, precision=lax.Precision.HIGHEST)
    new_velocity = MOMENTUM * velocity - STEP_SIZE * update_sum
    new_coefficients = coefficients + new_velocity
    return (new_coefficients, new_velocity)


def solution(mesh):
    n_blk = mesh.shape["blk"]
    n_str = mesh.shape["stripe"]
    in_specs = (
        P(("blk", "stripe"), None),
        P(("blk", "stripe")),
        P(("blk", "stripe")),
        P(("blk", "stripe")),
        P(("blk", "stripe")),
        P("blk", "stripe"),
    )
    out_specs = (P(("blk", "stripe")), P(("blk", "stripe")))
    return jax.shard_map(
        functools.partial(per_device, n_blk, n_str), mesh=mesh, in_specs=in_specs,
        out_specs=out_specs, check_vma=False
    )
```

```python
import functools
import math

import jax
import jax.numpy as jnp
from jax import lax
from jax.experimental import pallas as pl
from jax.experimental.pallas import tpu as pltpu
from jax.sharding import PartitionSpec as P

MOMENTUM = 0.9
STEP_SIZE = 1.0
NOISE_VAR = 8.0
KERNEL_RATE = 3.0**0.5 / 6.0

MESH_ID = pl.DeviceIdType.MESH
ANY = pl.BlockSpec(memory_space=pl.ANY)


def gather_kernel(n_blk, n_in, n_out, picked, pts, prev, rows_out, pts_out, prev_out,
                  in_send, in_recv, out_send, out_recv, pt_send, pt_recv, pv_send, pv_recv,
                  local_sem):
    b = lax.axis_index("blk")
    s = lax.axis_index("stripe")
    u = s // n_in
    v = lax.rem(s, n_in)
    barrier = pltpu.get_barrier_semaphore()

    def greet(i, carry):
        pl.semaphore_signal(barrier, 1, device_id=(b, u * n_in + lax.rem(v + 1 + i, n_in)),
                            device_id_type=MESH_ID)
        return carry

    def greet_out(i, carry):
        pl.semaphore_signal(barrier, 1, device_id=(b, lax.rem(u + 1 + i, n_out) * n_in + v),
                            device_id_type=MESH_ID)
        return carry

    def greet_blk(i, carry):
        pl.semaphore_signal(barrier, 1, device_id=(lax.rem(b + 1 + i, n_blk), s),
                            device_id_type=MESH_ID)
        return carry

    lax.fori_loop(0, n_in - 1, greet, 0)
    lax.fori_loop(0, n_out - 1, greet_out, 0)
    lax.fori_loop(0, n_blk - 1, greet_blk, 0)
    pl.semaphore_wait(barrier, (n_in - 1) + (n_out - 1) + (n_blk - 1))
    own = [
        pltpu.make_async_copy(picked, rows_out.at[u, v], local_sem.at[0]),
        pltpu.make_async_copy(pts, pts_out.at[b], local_sem.at[1]),
        pltpu.make_async_copy(prev, prev_out.at[b], local_sem.at[2]),
    ]
    for c in own:
        c.start()

    def inner_copy(i, src):
        peer = lax.rem(v + 1 + i, n_in)
        return pltpu.make_async_remote_copy(
            src_ref=picked, dst_ref=rows_out.at[u, src], send_sem=in_send.at[i],
            recv_sem=in_recv.at[src], device_id=(b, u * n_in + peer), device_id_type=MESH_ID)

    def outer_copy(i, src):
        peer = lax.rem(u + 1 + i, n_out)
        return pltpu.make_async_remote_copy(
            src_ref=rows_out.at[u], dst_ref=rows_out.at[src], send_sem=out_send.at[i],
            recv_sem=out_recv.at[src], device_id=(b, peer * n_in + v), device_id_type=MESH_ID)

    def blk_copies(i, src):
        peer = lax.rem(b + 1 + i, n_blk)
        return (
            pltpu.make_async_remote_copy(
                src_ref=pts, dst_ref=pts_out.at[src], send_sem=pt_send.at[i],
                recv_sem=pt_recv.at[src], device_id=(peer, s), device_id_type=MESH_ID),
            pltpu.make_async_remote_copy(
                src_ref=prev, dst_ref=prev_out.at[src], send_sem=pv_send.at[i],
                recv_sem=pv_recv.at[src], device_id=(peer, s), device_id_type=MESH_ID),
        )

    def start_inner(i, carry):
        inner_copy(i, v).start()
        return carry

    def start_blk(i, carry):
        for c in blk_copies(i, b):
            c.start()
        return carry

    lax.fori_loop(0, n_in - 1, start_inner, 0)
    lax.fori_loop(0, n_blk - 1, start_blk, 0)

    def wait_inner(i, carry):
        inner_copy(i, v).wait_send()
        inner_copy(i, lax.rem(v + 2 * n_in - 1 - i, n_in)).wait_recv()
        return carry

    lax.fori_loop(0, n_in - 1, wait_inner, 0)
    own[0].wait()

    def start_outer(i, carry):
        outer_copy(i, u).start()
        return carry

    lax.fori_loop(0, n_out - 1, start_outer, 0)

    def wait_blk(i, carry):
        for c in blk_copies(i, b):
            c.wait_send()
        src = lax.rem(b + 2 * n_blk - 1 - i, n_blk)
        for c in blk_copies(i, src):
            c.wait_recv()
        return carry

    def wait_outer(i, carry):
        outer_copy(i, u).wait_send()
        outer_copy(i, lax.rem(u + 2 * n_out - 1 - i, n_out)).wait_recv()
        return carry

    lax.fori_loop(0, n_blk - 1, wait_blk, 0)
    lax.fori_loop(0, n_out - 1, wait_outer, 0)
    own[1].wait()
    own[2].wait()


def gather_all(picked, pts, prev, n_blk, n_in, n_out):
    dma = pltpu.SemaphoreType.DMA
    return pl.pallas_call(
        functools.partial(gather_kernel, n_blk, n_in, n_out),
        out_shape=(
            jax.ShapeDtypeStruct((n_out, n_in) + picked.shape, picked.dtype),
            jax.ShapeDtypeStruct((n_blk,) + pts.shape, pts.dtype),
            jax.ShapeDtypeStruct((n_blk,) + prev.shape, prev.dtype),
        ),
        in_specs=[ANY, ANY, ANY],
        out_specs=(ANY, ANY, ANY),
        scratch_shapes=[
            dma((n_in,)), dma((n_in,)), dma((n_out,)), dma((n_out,)),
            dma((n_blk,)), dma((n_blk,)), dma((n_blk,)), dma((n_blk,)), dma((3,)),
        ],
        compiler_params=pltpu.CompilerParams(has_side_effects=True, collective_id=0),
    )(picked, pts, prev)


def scatter_kernel(n_in, n_out, part, total_out, stage1, mid, stage2,
                   out_send, out_recv, in_send, in_recv, local_sem):
    b = lax.axis_index("blk")
    s = lax.axis_index("stripe")
    u = s // n_in
    v = lax.rem(s, n_in)
    barrier = pltpu.get_barrier_semaphore()

    def greet(i, carry):
        pl.semaphore_signal(barrier, 1, device_id=(b, u * n_in + lax.rem(v + 1 + i, n_in)),
                            device_id_type=MESH_ID)
        return carry

    def greet_out(i, carry):
        pl.semaphore_signal(barrier, 1, device_id=(b, lax.rem(u + 1 + i, n_out) * n_in + v),
                            device_id_type=MESH_ID)
        return carry

    lax.fori_loop(0, n_in - 1, greet, 0)
    lax.fori_loop(0, n_out - 1, greet_out, 0)
    pl.semaphore_wait(barrier, (n_in - 1) + (n_out - 1))
    own1 = pltpu.make_async_copy(part.at[u], stage1.at[u], local_sem.at[0])
    own1.start()

    def outer_copy(i, src):
        peer = lax.rem(u + 1 + i, n_out)
        return pltpu.make_async_remote_copy(
            src_ref=part.at[peer], dst_ref=stage1.at[src], send_sem=out_send.at[i],
            recv_sem=out_recv.at[src], device_id=(b, peer * n_in + v), device_id_type=MESH_ID)

    def inner_copy(i, src):
        peer = lax.rem(v + 1 + i, n_in)
        return pltpu.make_async_remote_copy(
            src_ref=mid.at[peer], dst_ref=stage2.at[src], send_sem=in_send.at[i],
            recv_sem=in_recv.at[src], device_id=(b, u * n_in + peer), device_id_type=MESH_ID)

    def start_outer(i, carry):
        outer_copy(i, u).start()
        return carry

    lax.fori_loop(0, n_out - 1, start_outer, 0)

    def wait_outer(i, carry):
        outer_copy(i, u).wait_send()
        outer_copy(i, lax.rem(u + 2 * n_out - 1 - i, n_out)).wait_recv()
        return carry

    lax.fori_loop(0, n_out - 1, wait_outer, 0)
    own1.wait()
    mid[...] = jnp.sum(stage1[...], axis=0)[:, None, :]
    own2 = pltpu.make_async_copy(mid.at[v], stage2.at[v], local_sem.at[1])
    own2.start()

    def start_inner(i, carry):
        inner_copy(i, v).start()
        return carry

    lax.fori_loop(0, n_in - 1, start_inner, 0)

    def wait_inner(i, carry):
        inner_copy(i, v).wait_send()
        inner_copy(i, lax.rem(v + 2 * n_in - 1 - i, n_in)).wait_recv()
        return carry

    lax.fori_loop(0, n_in - 1, wait_inner, 0)
    own2.wait()
    total_out[...] = jnp.sum(stage2[...], axis=0)


def scatter_all(part, n_in, n_out):
    dma = pltpu.SemaphoreType.DMA
    vmem = pl.BlockSpec(memory_space=pltpu.VMEM)
    width = part.shape[-1]
    return pl.pallas_call(
        functools.partial(scatter_kernel, n_in, n_out),
        out_shape=jax.ShapeDtypeStruct((1, width), part.dtype),
        in_specs=[vmem],
        out_specs=vmem,
        scratch_shapes=[
            pltpu.VMEM((n_out, n_in, width), jnp.float32),
            pltpu.VMEM((n_in, 1, width), jnp.float32),
            pltpu.VMEM((n_in, 1, width), jnp.float32),
            dma((n_out,)), dma((n_out,)), dma((n_in,)), dma((n_in,)), dma((2,)),
        ],
        compiler_params=pltpu.CompilerParams(has_side_effects=True, collective_id=1),
    )(part)


def matern_sums(row_feats, row_sq, col_points, col_coef):
    col_sq = jnp.sum(jnp.square(col_points.astype(jnp.float32)), axis=1)
    inner_prod = lax.dot_general(
        row_feats, col_points, (((1,), (1,)), ((), ())), preferred_element_type=jnp.float32
    )
    distance = jnp.sqrt(jnp.maximum(row_sq[:, None] + col_sq[None, :] - 2.0 * inner_prod, 0.0))
    scaled = KERNEL_RATE * distance
    kernel_tile = (1.0 + scaled) * jnp.exp(-scaled)
    return jnp.sum(kernel_tile * col_coef[None, :], axis=1)


def column_sums(row_feats, piece_points, every_coef):
    row_sq = jnp.sum(jnp.square(row_feats.astype(jnp.float32)), axis=1)
    zeros_init = jnp.zeros((row_feats.shape[0],), jnp.float32)
    piece_len = piece_points.shape[0]
    block_len = math.gcd(piece_len, 512)
    point_blocks = piece_points.reshape(-1, block_len, piece_points.shape[1])
    coef_blocks = every_coef.reshape(-1, block_len)

    def advance(partial_sum, column_block):
        return (
            partial_sum + matern_sums(row_feats, row_sq, column_block[0], column_block[1]),
            None,
        )

    result, unused = lax.scan(advance, zeros_init, (point_blocks, coef_blocks))
    return result


def per_device(n_blk, n_str, points, coefficients, velocity, targets, batch_rows, counts):
    preview = coefficients + MOMENTUM * velocity
    slot_total = batch_rows.shape[0]
    local_size = points.shape[0]
    slot_ids = jnp.arange(slot_total, dtype=jnp.int32)
    count_here = counts.reshape((1,))
    in_count = slot_ids < count_here[0]
    picked = jnp.take(points, batch_rows, axis=0)
    n_in = math.gcd(n_str, 8)
    n_out = n_str // n_in
    rows_all, pts_all, prev_all = gather_all(picked, points, preview.reshape(1, -1), n_blk, n_in, n_out)
    group_rows = rows_all.reshape(-1, points.shape[1])
    piece_points = pts_all.reshape(-1, points.shape[1])
    every_coef = prev_all.reshape(-1)
    partial_value = column_sums(group_rows, piece_points, every_coef)
    kernel_rows = scatter_all(partial_value.reshape(n_out, n_in, slot_total), n_in, n_out).reshape(-1)
    residual = jnp.where(
        in_count,
        kernel_rows + NOISE_VAR * jnp.take(preview, batch_rows) - jnp.take(targets, batch_rows),
        0.0,
    )
    scatter_rows = (batch_rows[:, None] == jnp.arange(local_size, dtype=jnp.int32)[None, :]).astype(
        jnp.float32
    )
    update_sum = jnp.dot(residual, scatter_rows, precision=lax.Precision.HIGHEST)
    new_velocity = MOMENTUM * velocity - STEP_SIZE * update_sum
    new_coefficients = coefficients + new_velocity
    return (new_coefficients, new_velocity)


def solution(mesh):
    n_blk = mesh.shape["blk"]
    n_str = mesh.shape["stripe"]
    in_specs = (
        P(("blk", "stripe"), None),
        P(("blk", "stripe")),
        P(("blk", "stripe")),
        P(("blk", "stripe")),
        P(("blk", "stripe")),
        P("blk", "stripe"),
    )
    out_specs = (P(("blk", "stripe")), P(("blk", "stripe")))
    return jax.shard_map(
        functools.partial(per_device, n_blk, n_str), mesh=mesh, in_specs=in_specs,
        out_specs=out_specs, check_vma=False
    )
```

```python
import functools
import math

import jax
import jax.numpy as jnp
from jax import lax
from jax.experimental import pallas as pl
from jax.experimental.pallas import tpu as pltpu
from jax.sharding import PartitionSpec as P

MOMENTUM = 0.9
STEP_SIZE = 1.0
NOISE_VAR = 8.0
KERNEL_RATE = 3.0**0.5 / 6.0

MESH_ID = pl.DeviceIdType.MESH
ANY = pl.BlockSpec(memory_space=pl.ANY)


def coords():
    b = lax.axis_index("blk")
    s = lax.axis_index("stripe")
    core = lax.rem(s, 2)
    z_hi = lax.rem(s // 2, 2)
    x = lax.rem(s // 4, 4)
    y = s // 16
    c = lax.rem(b, 2) * 4 + lax.rem(x, 2) * 2 + core
    q = y * 2 + x // 2
    w = (b // 2) * 2 + z_hi
    return c, q, w


def dev(c, q, w):
    b = (w // 2) * 2 + c // 4
    z_hi = lax.rem(w, 2)
    y = q // 2
    x = lax.rem(q, 2) * 2 + lax.rem(c // 2, 2)
    core = lax.rem(c, 2)
    return (b, ((y * 4 + x) * 2 + z_hi) * 2 + core)


def greet_all(barrier, peers_of, n, total):
    def greet(i, carry):
        pl.semaphore_signal(barrier, 1, device_id=peers_of(i), device_id_type=MESH_ID)
        return carry

    lax.fori_loop(0, n, greet, 0)
    return total + n


def gather_kernel(g, picked, pts, prev, rows_out, pts_out, prev_out,
                  in_send, in_recv, out_send, out_recv, pt_send, pt_recv, pv_send, pv_recv,
                  local_sem):
    c, q, w = coords()
    barrier = pltpu.get_barrier_semaphore()
    n = greet_all(barrier, lambda i: dev(c, q, lax.rem(w + 1 + i, g)), g - 1, 0)
    n = greet_all(barrier, lambda i: dev(c, lax.rem(q + 1 + i, g), w), g - 1, n)
    n = greet_all(barrier, lambda i: dev(lax.rem(c + 1 + i, g), q, w), g - 1, n)
    pl.semaphore_wait(barrier, n)
    own = [
        pltpu.make_async_copy(picked, rows_out.at[q, w], local_sem.at[0]),
        pltpu.make_async_copy(pts, pts_out.at[c], local_sem.at[1]),
        pltpu.make_async_copy(prev, prev_out.at[c], local_sem.at[2]),
    ]
    for cp in own:
        cp.start()

    def inner_copy(i, src):
        return pltpu.make_async_remote_copy(
            src_ref=picked, dst_ref=rows_out.at[q, src], send_sem=in_send.at[i],
            recv_sem=in_recv.at[src], device_id=dev(c, q, lax.rem(w + 1 + i, g)),
            device_id_type=MESH_ID)

    def outer_copy(i, src):
        return pltpu.make_async_remote_copy(
            src_ref=rows_out.at[q], dst_ref=rows_out.at[src], send_sem=out_send.at[i],
            recv_sem=out_recv.at[src], device_id=dev(c, lax.rem(q + 1 + i, g), w),
            device_id_type=MESH_ID)

    def group_copies(i, src):
        peer = dev(lax.rem(c + 1 + i, g), q, w)
        return (
            pltpu.make_async_remote_copy(
                src_ref=pts, dst_ref=pts_out.at[src], send_sem=pt_send.at[i],
                recv_sem=pt_recv.at[src], device_id=peer, device_id_type=MESH_ID),
            pltpu.make_async_remote_copy(
                src_ref=prev, dst_ref=prev_out.at[src], send_sem=pv_send.at[i],
                recv_sem=pv_recv.at[src], device_id=peer, device_id_type=MESH_ID),
        )

    def start_inner(i, carry):
        inner_copy(i, w).start()
        return carry

    def start_group(i, carry):
        for cp in group_copies(i, c):
            cp.start()
        return carry

    lax.fori_loop(0, g - 1, start_inner, 0)
    lax.fori_loop(0, g - 1, start_group, 0)

    def wait_inner(i, carry):
        inner_copy(i, w).wait_send()
        inner_copy(i, lax.rem(w + 2 * g - 1 - i, g)).wait_recv()
        return carry

    lax.fori_loop(0, g - 1, wait_inner, 0)
    own[0].wait()

    def start_outer(i, carry):
        outer_copy(i, q).start()
        return carry

    lax.fori_loop(0, g - 1, start_outer, 0)

    def wait_group(i, carry):
        for cp in group_copies(i, c):
            cp.wait_send()
        for cp in group_copies(i, lax.rem(c + 2 * g - 1 - i, g)):
            cp.wait_recv()
        return carry

    def wait_outer(i, carry):
        outer_copy(i, q).wait_send()
        outer_copy(i, lax.rem(q + 2 * g - 1 - i, g)).wait_recv()
        return carry

    lax.fori_loop(0, g - 1, wait_group, 0)
    lax.fori_loop(0, g - 1, wait_outer, 0)
    own[1].wait()
    own[2].wait()


def gather_all(picked, pts, prev, g):
    dma = pltpu.SemaphoreType.DMA
    return pl.pallas_call(
        functools.partial(gather_kernel, g),
        out_shape=(
            jax.ShapeDtypeStruct((g, g) + picked.shape, picked.dtype),
            jax.ShapeDtypeStruct((g,) + pts.shape, pts.dtype),
            jax.ShapeDtypeStruct((g,) + prev.shape, prev.dtype),
        ),
        in_specs=[ANY, ANY, ANY],
        out_specs=(ANY, ANY, ANY),
        scratch_shapes=[dma((g,)) for _ in range(8)] + [dma((3,))],
        compiler_params=pltpu.CompilerParams(has_side_effects=True, collective_id=0),
    )(picked, pts, prev)


def scatter_kernel(g, part, total_out, stage1, mid, stage2,
                   out_send, out_recv, in_send, in_recv, local_sem):
    c, q, w = coords()
    barrier = pltpu.get_barrier_semaphore()
    n = greet_all(barrier, lambda i: dev(c, q, lax.rem(w + 1 + i, g)), g - 1, 0)
    n = greet_all(barrier, lambda i: dev(c, lax.rem(q + 1 + i, g), w), g - 1, n)
    pl.semaphore_wait(barrier, n)
    own1 = pltpu.make_async_copy(part.at[q], stage1.at[q], local_sem.at[0])
    own1.start()

    def outer_copy(i, src):
        peer = lax.rem(q + 1 + i, g)
        return pltpu.make_async_remote_copy(
            src_ref=part.at[peer], dst_ref=stage1.at[src], send_sem=out_send.at[i],
            recv_sem=out_recv.at[src], device_id=dev(c, peer, w), device_id_type=MESH_ID)

    def inner_copy(i, src):
        peer = lax.rem(w + 1 + i, g)
        return pltpu.make_async_remote_copy(
            src_ref=mid.at[peer], dst_ref=stage2.at[src], send_sem=in_send.at[i],
            recv_sem=in_recv.at[src], device_id=dev(c, q, peer), device_id_type=MESH_ID)

    def start_outer(i, carry):
        outer_copy(i, q).start()
        return carry

    lax.fori_loop(0, g - 1, start_outer, 0)

    def wait_outer(i, carry):
        outer_copy(i, q).wait_send()
        outer_copy(i, lax.rem(q + 2 * g - 1 - i, g)).wait_recv()
        return carry

    lax.fori_loop(0, g - 1, wait_outer, 0)
    own1.wait()
    mid[...] = jnp.sum(stage1[...], axis=0)[:, None, :]
    own2 = pltpu.make_async_copy(mid.at[w], stage2.at[w], local_sem.at[1])
    own2.start()

    def start_inner(i, carry):
        inner_copy(i, w).start()
        return carry

    lax.fori_loop(0, g - 1, start_inner, 0)

    def wait_inner(i, carry):
        inner_copy(i, w).wait_send()
        inner_copy(i, lax.rem(w + 2 * g - 1 - i, g)).wait_recv()
        return carry

    lax.fori_loop(0, g - 1, wait_inner, 0)
    own2.wait()
    total_out[...] = jnp.sum(stage2[...], axis=0)


def scatter_all(part, g):
    dma = pltpu.SemaphoreType.DMA
    vmem = pl.BlockSpec(memory_space=pltpu.VMEM)
    width = part.shape[-1]
    return pl.pallas_call(
        functools.partial(scatter_kernel, g),
        out_shape=jax.ShapeDtypeStruct((1, width), part.dtype),
        in_specs=[vmem],
        out_specs=vmem,
        scratch_shapes=[
            pltpu.VMEM((g, g, width), jnp.float32),
            pltpu.VMEM((g, 1, width), jnp.float32),
            pltpu.VMEM((g, 1, width), jnp.float32),
            dma((g,)), dma((g,)), dma((g,)), dma((g,)), dma((2,)),
        ],
        compiler_params=pltpu.CompilerParams(has_side_effects=True, collective_id=1),
    )(part)


def matern_sums(row_feats, row_sq, col_points, col_coef):
    col_sq = jnp.sum(jnp.square(col_points.astype(jnp.float32)), axis=1)
    inner_prod = lax.dot_general(
        row_feats, col_points, (((1,), (1,)), ((), ())), preferred_element_type=jnp.float32
    )
    distance = jnp.sqrt(jnp.maximum(row_sq[:, None] + col_sq[None, :] - 2.0 * inner_prod, 0.0))
    scaled = KERNEL_RATE * distance
    kernel_tile = (1.0 + scaled) * jnp.exp(-scaled)
    return jnp.sum(kernel_tile * col_coef[None, :], axis=1)


def column_sums(row_feats, piece_points, every_coef):
    row_sq = jnp.sum(jnp.square(row_feats.astype(jnp.float32)), axis=1)
    zeros_init = jnp.zeros((row_feats.shape[0],), jnp.float32)
    piece_len = piece_points.shape[0]
    block_len = math.gcd(piece_len, 512)
    point_blocks = piece_points.reshape(-1, block_len, piece_points.shape[1])
    coef_blocks = every_coef.reshape(-1, block_len)

    def advance(partial_sum, column_block):
        return (
            partial_sum + matern_sums(row_feats, row_sq, column_block[0], column_block[1]),
            None,
        )

    result, unused = lax.scan(advance, zeros_init, (point_blocks, coef_blocks))
    return result


def per_device(n_blk, n_str, points, coefficients, velocity, targets, batch_rows, counts):
    preview = coefficients + MOMENTUM * velocity
    slot_total = batch_rows.shape[0]
    local_size = points.shape[0]
    slot_ids = jnp.arange(slot_total, dtype=jnp.int32)
    count_here = counts.reshape((1,))
    in_count = slot_ids < count_here[0]
    picked = jnp.take(points, batch_rows, axis=0)
    g = 8
    rows_all, pts_all, prev_all = gather_all(picked, points, preview.reshape(1, -1), g)
    group_rows = rows_all.reshape(-1, points.shape[1])
    piece_points = pts_all.reshape(-1, points.shape[1])
    every_coef = prev_all.reshape(-1)
    partial_value = column_sums(group_rows, piece_points, every_coef)
    kernel_rows = scatter_all(partial_value.reshape(g, g, slot_total), g).reshape(-1)
    residual = jnp.where(
        in_count,
        kernel_rows + NOISE_VAR * jnp.take(preview, batch_rows) - jnp.take(targets, batch_rows),
        0.0,
    )
    scatter_rows = (batch_rows[:, None] == jnp.arange(local_size, dtype=jnp.int32)[None, :]).astype(
        jnp.float32
    )
    update_sum = jnp.dot(residual, scatter_rows, precision=lax.Precision.HIGHEST)
    new_velocity = MOMENTUM * velocity - STEP_SIZE * update_sum
    new_coefficients = coefficients + new_velocity
    return (new_coefficients, new_velocity)


def solution(mesh):
    n_blk = mesh.shape["blk"]
    n_str = mesh.shape["stripe"]
    in_specs = (
        P(("blk", "stripe"), None),
        P(("blk", "stripe")),
        P(("blk", "stripe")),
        P(("blk", "stripe")),
        P(("blk", "stripe")),
        P("blk", "stripe"),
    )
    out_specs = (P(("blk", "stripe")), P(("blk", "stripe")))
    return jax.shard_map(
        functools.partial(per_device, n_blk, n_str), mesh=mesh, in_specs=in_specs,
        out_specs=out_specs, check_vma=False
    )
```

```python
import functools
import math

import jax
import jax.numpy as jnp
from jax import lax
from jax.experimental import pallas as pl
from jax.experimental.pallas import tpu as pltpu
from jax.sharding import PartitionSpec as P

MOMENTUM = 0.9
STEP_SIZE = 1.0
NOISE_VAR = 8.0
KERNEL_RATE = 3.0**0.5 / 6.0

MESH_ID = pl.DeviceIdType.MESH
ANY = pl.BlockSpec(memory_space=pl.ANY)


def coords():
    b = lax.axis_index("blk")
    s = lax.axis_index("stripe")
    core = lax.rem(s, 2)
    z_hi = lax.rem(s // 2, 2)
    x = lax.rem(s // 4, 4)
    y = s // 16
    c = lax.rem(b, 2) * 4 + lax.rem(x, 2) * 2 + core
    q = y * 2 + x // 2
    w = (b // 2) * 2 + z_hi
    return c, q, w


def dev(c, q, w):
    b = (w // 2) * 2 + c // 4
    z_hi = lax.rem(w, 2)
    y = q // 2
    x = lax.rem(q, 2) * 2 + lax.rem(c // 2, 2)
    core = lax.rem(c, 2)
    return (b, ((y * 4 + x) * 2 + z_hi) * 2 + core)


def greet_all(barrier, peers_of, n, total):
    def greet(i, carry):
        pl.semaphore_signal(barrier, 1, device_id=peers_of(i), device_id_type=MESH_ID)
        return carry

    lax.fori_loop(0, n, greet, 0)
    return total + n


def gather_kernel(g, picked, pts, prev, rows_out, pts_out, prev_out,
                  in_send, in_recv, out_send, out_recv, pt_send, pt_recv, pv_send, pv_recv,
                  local_sem):
    c, q, w = coords()
    barrier = pltpu.get_barrier_semaphore()
    n = greet_all(barrier, lambda i: dev(c, q, lax.rem(w + 1 + i, g)), g - 1, 0)
    n = greet_all(barrier, lambda i: dev(c, lax.rem(q + 1 + i, g), w), g - 1, n)
    n = greet_all(barrier, lambda i: dev(lax.rem(c + 1 + i, g), q, w), g - 1, n)
    pl.semaphore_wait(barrier, n)
    own = [
        pltpu.make_async_copy(picked, rows_out.at[q, w], local_sem.at[0]),
        pltpu.make_async_copy(pts, pts_out.at[c], local_sem.at[1]),
        pltpu.make_async_copy(prev, prev_out.at[c], local_sem.at[2]),
    ]
    for cp in own:
        cp.start()

    def inner_copy(i, src):
        return pltpu.make_async_remote_copy(
            src_ref=picked, dst_ref=rows_out.at[q, src], send_sem=in_send.at[i],
            recv_sem=in_recv.at[src], device_id=dev(c, q, lax.rem(w + 1 + i, g)),
            device_id_type=MESH_ID)

    def outer_copy(i, src):
        return pltpu.make_async_remote_copy(
            src_ref=rows_out.at[q], dst_ref=rows_out.at[src], send_sem=out_send.at[i],
            recv_sem=out_recv.at[src], device_id=dev(c, lax.rem(q + 1 + i, g), w),
            device_id_type=MESH_ID)

    def group_copies(i, src):
        peer = dev(lax.rem(c + 1 + i, g), q, w)
        return (
            pltpu.make_async_remote_copy(
                src_ref=pts, dst_ref=pts_out.at[src], send_sem=pt_send.at[i],
                recv_sem=pt_recv.at[src], device_id=peer, device_id_type=MESH_ID),
            pltpu.make_async_remote_copy(
                src_ref=prev, dst_ref=prev_out.at[src], send_sem=pv_send.at[i],
                recv_sem=pv_recv.at[src], device_id=peer, device_id_type=MESH_ID),
        )

    def start_inner(i, carry):
        inner_copy(i, w).start()
        return carry

    def start_group(i, carry):
        for cp in group_copies(i, c):
            cp.start()
        return carry

    lax.fori_loop(0, g - 1, start_inner, 0)
    lax.fori_loop(0, g - 1, start_group, 0)

    def wait_inner(i, carry):
        inner_copy(i, w).wait_send()
        inner_copy(i, lax.rem(w + 2 * g - 1 - i, g)).wait_recv()
        return carry

    lax.fori_loop(0, g - 1, wait_inner, 0)
    own[0].wait()

    def start_outer(i, carry):
        outer_copy(i, q).start()
        return carry

    lax.fori_loop(0, g - 1, start_outer, 0)

    def wait_group(i, carry):
        for cp in group_copies(i, c):
            cp.wait_send()
        for cp in group_copies(i, lax.rem(c + 2 * g - 1 - i, g)):
            cp.wait_recv()
        return carry

    def wait_outer(i, carry):
        outer_copy(i, q).wait_send()
        outer_copy(i, lax.rem(q + 2 * g - 1 - i, g)).wait_recv()
        return carry

    lax.fori_loop(0, g - 1, wait_group, 0)
    lax.fori_loop(0, g - 1, wait_outer, 0)
    own[1].wait()
    own[2].wait()


def gather_all(picked, pts, prev, g):
    dma = pltpu.SemaphoreType.DMA
    return pl.pallas_call(
        functools.partial(gather_kernel, g),
        out_shape=(
            jax.ShapeDtypeStruct((g, g) + picked.shape, picked.dtype),
            jax.ShapeDtypeStruct((g,) + pts.shape, pts.dtype),
            jax.ShapeDtypeStruct((g,) + prev.shape, prev.dtype),
        ),
        in_specs=[ANY, ANY, ANY],
        out_specs=(ANY, ANY, ANY),
        scratch_shapes=[dma((g,)) for _ in range(8)] + [dma((3,))],
        compiler_params=pltpu.CompilerParams(has_side_effects=True, collective_id=0),
    )(picked, pts, prev)


def scatter_kernel(g, part, total_out, stage1, mid, stage2,
                   out_send, out_recv, in_send, in_recv, local_sem):
    c, q, w = coords()
    barrier = pltpu.get_barrier_semaphore()
    n = greet_all(barrier, lambda i: dev(c, q, lax.rem(w + 1 + i, g)), g - 1, 0)
    n = greet_all(barrier, lambda i: dev(c, lax.rem(q + 1 + i, g), w), g - 1, n)
    pl.semaphore_wait(barrier, n)
    own1 = pltpu.make_async_copy(part.at[q], stage1.at[q], local_sem.at[0])
    own1.start()

    def outer_copy(i, src):
        peer = lax.rem(q + 1 + i, g)
        return pltpu.make_async_remote_copy(
            src_ref=part.at[peer], dst_ref=stage1.at[src], send_sem=out_send.at[i],
            recv_sem=out_recv.at[src], device_id=dev(c, peer, w), device_id_type=MESH_ID)

    def inner_copy(i, src):
        peer = lax.rem(w + 1 + i, g)
        return pltpu.make_async_remote_copy(
            src_ref=mid.at[peer], dst_ref=stage2.at[src], send_sem=in_send.at[i],
            recv_sem=in_recv.at[src], device_id=dev(c, q, peer), device_id_type=MESH_ID)

    def start_outer(i, carry):
        outer_copy(i, q).start()
        return carry

    lax.fori_loop(0, g - 1, start_outer, 0)

    def wait_outer(i, carry):
        outer_copy(i, q).wait_send()
        outer_copy(i, lax.rem(q + 2 * g - 1 - i, g)).wait_recv()
        return carry

    lax.fori_loop(0, g - 1, wait_outer, 0)
    own1.wait()
    mid[...] = jnp.sum(stage1[...], axis=0)[:, None, :]
    own2 = pltpu.make_async_copy(mid.at[w], stage2.at[w], local_sem.at[1])
    own2.start()

    def start_inner(i, carry):
        inner_copy(i, w).start()
        return carry

    lax.fori_loop(0, g - 1, start_inner, 0)

    def wait_inner(i, carry):
        inner_copy(i, w).wait_send()
        inner_copy(i, lax.rem(w + 2 * g - 1 - i, g)).wait_recv()
        return carry

    lax.fori_loop(0, g - 1, wait_inner, 0)
    own2.wait()
    total_out[...] = jnp.sum(stage2[...], axis=0)


def scatter_all(part, g):
    dma = pltpu.SemaphoreType.DMA
    vmem = pl.BlockSpec(memory_space=pltpu.VMEM)
    width = part.shape[-1]
    return pl.pallas_call(
        functools.partial(scatter_kernel, g),
        out_shape=jax.ShapeDtypeStruct((1, width), part.dtype),
        in_specs=[vmem],
        out_specs=vmem,
        scratch_shapes=[
            pltpu.VMEM((g, g, width), jnp.float32),
            pltpu.VMEM((g, 1, width), jnp.float32),
            pltpu.VMEM((g, 1, width), jnp.float32),
            dma((g,)), dma((g,)), dma((g,)), dma((g,)), dma((2,)),
        ],
        compiler_params=pltpu.CompilerParams(has_side_effects=True, collective_id=1),
    )(part)


def tile_kernel(rows_ref, pts_ref, rs_ref, cs_ref, coef_ref, out_ref):
    row_chunk, col_chunk, lanes = 64, 512, 128
    n_cols = pts_ref.shape[0]

    def body(r, carry):
        r0 = pl.multiple_of(r * row_chunk, row_chunk)
        rows = rows_ref[pl.ds(r0, row_chunk), :]
        rs = rs_ref[pl.ds(r0, row_chunk), :]
        acc = jnp.zeros((row_chunk, lanes), jnp.float32)
        for cj in range(n_cols // col_chunk):
            cols = slice(cj * col_chunk, (cj + 1) * col_chunk)
            neg_two_dot = lax.dot_general(
                rows, pts_ref[cols, :], (((1,), (1,)), ((), ())),
                preferred_element_type=jnp.float32)
            sq = (rs + cs_ref[:, cols]) + neg_two_dot
            m = jnp.sqrt(jnp.maximum(sq, 0.0)) * (-KERNEL_RATE)
            term = ((1.0 - m) * jnp.exp(m)) * coef_ref[:, cols]
            for l in range(col_chunk // lanes):
                acc = acc + term[:, l * lanes:(l + 1) * lanes]
        out_ref[pl.ds(r0, row_chunk), :] = jnp.sum(acc, axis=1, keepdims=True)
        return carry

    lax.fori_loop(0, rows_ref.shape[0] // row_chunk, body, 0)


def column_sums(row_feats, piece_points, every_coef):
    n_rows, n_cols = row_feats.shape[0], piece_points.shape[0]
    row_sq = jnp.sum(jnp.square(row_feats.astype(jnp.float32)), axis=1, keepdims=True)
    col_sq = jnp.sum(jnp.square(piece_points.astype(jnp.float32)), axis=1)[None, :]
    neg_two_rows = row_feats * jnp.asarray(-2.0, row_feats.dtype)
    block = math.gcd(n_rows, 512)
    full = lambda i: (0, 0)
    return pl.pallas_call(
        tile_kernel,
        out_shape=jax.ShapeDtypeStruct((n_rows, 1), jnp.float32),
        grid=(n_rows // block,),
        in_specs=[
            pl.BlockSpec((block, row_feats.shape[1]), lambda i: (i, 0)),
            pl.BlockSpec(piece_points.shape, full),
            pl.BlockSpec((block, 1), lambda i: (i, 0)),
            pl.BlockSpec((1, n_cols), full),
            pl.BlockSpec((1, n_cols), full),
        ],
        out_specs=pl.BlockSpec((block, 1), lambda i: (i, 0)),
        cost_estimate=pl.CostEstimate(
            flops=n_rows * n_cols * (2 * row_feats.shape[1] + 10),
            transcendentals=2 * n_rows * n_cols,
            bytes_accessed=2 * (n_rows + n_cols) * row_feats.shape[1] + 12 * (n_rows + n_cols)),
    )(neg_two_rows, piece_points, row_sq, col_sq, every_coef[None, :]).reshape(-1)


def per_device(n_blk, n_str, points, coefficients, velocity, targets, batch_rows, counts):
    preview = coefficients + MOMENTUM * velocity
    slot_total = batch_rows.shape[0]
    local_size = points.shape[0]
    slot_ids = jnp.arange(slot_total, dtype=jnp.int32)
    count_here = counts.reshape((1,))
    in_count = slot_ids < count_here[0]
    picked = jnp.take(points, batch_rows, axis=0)
    g = 8
    rows_all, pts_all, prev_all = gather_all(picked, points, preview.reshape(1, -1), g)
    group_rows = rows_all.reshape(-1, points.shape[1])
    piece_points = pts_all.reshape(-1, points.shape[1])
    every_coef = prev_all.reshape(-1)
    partial_value = column_sums(group_rows, piece_points, every_coef)
    kernel_rows = scatter_all(partial_value.reshape(g, g, slot_total), g).reshape(-1)
    residual = jnp.where(
        in_count,
        kernel_rows + NOISE_VAR * jnp.take(preview, batch_rows) - jnp.take(targets, batch_rows),
        0.0,
    )
    scatter_rows = (batch_rows[:, None] == jnp.arange(local_size, dtype=jnp.int32)[None, :]).astype(
        jnp.float32
    )
    update_sum = jnp.dot(residual, scatter_rows, precision=lax.Precision.HIGHEST)
    new_velocity = MOMENTUM * velocity - STEP_SIZE * update_sum
    new_coefficients = coefficients + new_velocity
    return (new_coefficients, new_velocity)


def solution(mesh):
    n_blk = mesh.shape["blk"]
    n_str = mesh.shape["stripe"]
    in_specs = (
        P(("blk", "stripe"), None),
        P(("blk", "stripe")),
        P(("blk", "stripe")),
        P(("blk", "stripe")),
        P(("blk", "stripe")),
        P("blk", "stripe"),
    )
    out_specs = (P(("blk", "stripe")), P(("blk", "stripe")))
    return jax.shard_map(
        functools.partial(per_device, n_blk, n_str), mesh=mesh, in_specs=in_specs,
        out_specs=out_specs, check_vma=False
    )
```

```python
import functools
import math

import jax
import jax.numpy as jnp
from jax import lax
from jax.experimental import pallas as pl
from jax.experimental.pallas import tpu as pltpu
from jax.sharding import PartitionSpec as P

MOMENTUM = 0.9
STEP_SIZE = 1.0
NOISE_VAR = 8.0
KERNEL_RATE = 3.0**0.5 / 6.0

MESH_ID = pl.DeviceIdType.MESH
ANY = pl.BlockSpec(memory_space=pl.ANY)


def coords():
    b = lax.axis_index("blk")
    s = lax.axis_index("stripe")
    core = lax.rem(s, 2)
    z_hi = lax.rem(s // 2, 2)
    x = lax.rem(s // 4, 4)
    y = s // 16
    c = lax.rem(b, 2) * 4 + lax.rem(x, 2) * 2 + core
    q = y * 2 + x // 2
    w = (b // 2) * 2 + z_hi
    return c, q, w


def dev(c, q, w):
    b = (w // 2) * 2 + c // 4
    z_hi = lax.rem(w, 2)
    y = q // 2
    x = lax.rem(q, 2) * 2 + lax.rem(c // 2, 2)
    core = lax.rem(c, 2)
    return (b, ((y * 4 + x) * 2 + z_hi) * 2 + core)


def greet_all(barrier, peers_of, n, total):
    def greet(i, carry):
        pl.semaphore_signal(barrier, 1, device_id=peers_of(i), device_id_type=MESH_ID)
        return carry

    lax.fori_loop(0, n, greet, 0)
    return total + n


def gather_kernel(g, picked, pts, prev, rows_out, pts_out, prev_out,
                  in_send, in_recv, out_send, out_recv, pt_send, pt_recv, pv_send, pv_recv,
                  local_sem):
    c, q, w = coords()
    barrier = pltpu.get_barrier_semaphore()
    n = greet_all(barrier, lambda i: dev(c, q, lax.rem(w + 1 + i, g)), g - 1, 0)
    n = greet_all(barrier, lambda i: dev(c, lax.rem(q + 1 + i, g), w), g - 1, n)
    n = greet_all(barrier, lambda i: dev(lax.rem(c + 1 + i, g), q, w), g - 1, n)
    pl.semaphore_wait(barrier, n)
    own = [
        pltpu.make_async_copy(picked, rows_out.at[q, w], local_sem.at[0]),
        pltpu.make_async_copy(pts, pts_out.at[c], local_sem.at[1]),
        pltpu.make_async_copy(prev, prev_out.at[c], local_sem.at[2]),
    ]
    for cp in own:
        cp.start()

    def inner_copy(i, src):
        return pltpu.make_async_remote_copy(
            src_ref=picked, dst_ref=rows_out.at[q, src], send_sem=in_send.at[i],
            recv_sem=in_recv.at[src], device_id=dev(c, q, lax.rem(w + 1 + i, g)),
            device_id_type=MESH_ID)

    def outer_copy(i, src):
        return pltpu.make_async_remote_copy(
            src_ref=rows_out.at[q], dst_ref=rows_out.at[src], send_sem=out_send.at[i],
            recv_sem=out_recv.at[src], device_id=dev(c, lax.rem(q + 1 + i, g), w),
            device_id_type=MESH_ID)

    def group_copies(i, src):
        peer = dev(lax.rem(c + 1 + i, g), q, w)
        return (
            pltpu.make_async_remote_copy(
                src_ref=pts, dst_ref=pts_out.at[src], send_sem=pt_send.at[i],
                recv_sem=pt_recv.at[src], device_id=peer, device_id_type=MESH_ID),
            pltpu.make_async_remote_copy(
                src_ref=prev, dst_ref=prev_out.at[src], send_sem=pv_send.at[i],
                recv_sem=pv_recv.at[src], device_id=peer, device_id_type=MESH_ID),
        )

    def start_inner(i, carry):
        inner_copy(i, w).start()
        return carry

    def start_group(i, carry):
        for cp in group_copies(i, c):
            cp.start()
        return carry

    lax.fori_loop(0, g - 1, start_inner, 0)
    lax.fori_loop(0, g - 1, start_group, 0)

    def wait_inner(i, carry):
        inner_copy(i, w).wait_send()
        inner_copy(i, lax.rem(w + 2 * g - 1 - i, g)).wait_recv()
        return carry

    lax.fori_loop(0, g - 1, wait_inner, 0)
    own[0].wait()

    def start_outer(i, carry):
        outer_copy(i, q).start()
        return carry

    lax.fori_loop(0, g - 1, start_outer, 0)

    def wait_group(i, carry):
        for cp in group_copies(i, c):
            cp.wait_send()
        for cp in group_copies(i, lax.rem(c + 2 * g - 1 - i, g)):
            cp.wait_recv()
        return carry

    def wait_outer(i, carry):
        outer_copy(i, q).wait_send()
        outer_copy(i, lax.rem(q + 2 * g - 1 - i, g)).wait_recv()
        return carry

    lax.fori_loop(0, g - 1, wait_group, 0)
    lax.fori_loop(0, g - 1, wait_outer, 0)
    own[1].wait()
    own[2].wait()


def gather_all(picked, pts, prev, g):
    dma = pltpu.SemaphoreType.DMA
    return pl.pallas_call(
        functools.partial(gather_kernel, g),
        out_shape=(
            jax.ShapeDtypeStruct((g, g) + picked.shape, picked.dtype),
            jax.ShapeDtypeStruct((g,) + pts.shape, pts.dtype),
            jax.ShapeDtypeStruct((g,) + prev.shape, prev.dtype),
        ),
        in_specs=[ANY, ANY, ANY],
        out_specs=(ANY, ANY, ANY),
        scratch_shapes=[dma((g,)) for _ in range(8)] + [dma((3,))],
        compiler_params=pltpu.CompilerParams(has_side_effects=True, collective_id=0),
    )(picked, pts, prev)


def scatter_kernel(g, part, total_out, stage1, mid, stage2,
                   out_send, out_recv, in_send, in_recv, local_sem):
    c, q, w = coords()
    barrier = pltpu.get_barrier_semaphore()
    n = greet_all(barrier, lambda i: dev(c, q, lax.rem(w + 1 + i, g)), g - 1, 0)
    n = greet_all(barrier, lambda i: dev(c, lax.rem(q + 1 + i, g), w), g - 1, n)
    pl.semaphore_wait(barrier, n)
    own1 = pltpu.make_async_copy(part.at[q], stage1.at[q], local_sem.at[0])
    own1.start()

    def outer_copy(i, src):
        peer = lax.rem(q + 1 + i, g)
        return pltpu.make_async_remote_copy(
            src_ref=part.at[peer], dst_ref=stage1.at[src], send_sem=out_send.at[i],
            recv_sem=out_recv.at[src], device_id=dev(c, peer, w), device_id_type=MESH_ID)

    def inner_copy(i, src):
        peer = lax.rem(w + 1 + i, g)
        return pltpu.make_async_remote_copy(
            src_ref=mid.at[peer], dst_ref=stage2.at[src], send_sem=in_send.at[i],
            recv_sem=in_recv.at[src], device_id=dev(c, q, peer), device_id_type=MESH_ID)

    def start_outer(i, carry):
        outer_copy(i, q).start()
        return carry

    lax.fori_loop(0, g - 1, start_outer, 0)

    def wait_outer(i, carry):
        outer_copy(i, q).wait_send()
        outer_copy(i, lax.rem(q + 2 * g - 1 - i, g)).wait_recv()
        return carry

    lax.fori_loop(0, g - 1, wait_outer, 0)
    own1.wait()
    mid[...] = jnp.sum(stage1[...], axis=0)[:, None, :]
    own2 = pltpu.make_async_copy(mid.at[w], stage2.at[w], local_sem.at[1])
    own2.start()

    def start_inner(i, carry):
        inner_copy(i, w).start()
        return carry

    lax.fori_loop(0, g - 1, start_inner, 0)

    def wait_inner(i, carry):
        inner_copy(i, w).wait_send()
        inner_copy(i, lax.rem(w + 2 * g - 1 - i, g)).wait_recv()
        return carry

    lax.fori_loop(0, g - 1, wait_inner, 0)
    own2.wait()
    total_out[...] = jnp.sum(stage2[...], axis=0)


def scatter_all(part, g):
    dma = pltpu.SemaphoreType.DMA
    vmem = pl.BlockSpec(memory_space=pltpu.VMEM)
    width = part.shape[-1]
    return pl.pallas_call(
        functools.partial(scatter_kernel, g),
        out_shape=jax.ShapeDtypeStruct((1, width), part.dtype),
        in_specs=[vmem],
        out_specs=vmem,
        scratch_shapes=[
            pltpu.VMEM((g, g, width), jnp.float32),
            pltpu.VMEM((g, 1, width), jnp.float32),
            pltpu.VMEM((g, 1, width), jnp.float32),
            dma((g,)), dma((g,)), dma((g,)), dma((g,)), dma((2,)),
        ],
        compiler_params=pltpu.CompilerParams(has_side_effects=True, collective_id=1),
    )(part)


def tile_kernel(pts_ref, rows_t_ref, rs_ref, cs_ref, coef_ref, out_ref):
    pt_chunk, lanes, sub = 256, 128, 8
    n_pts = pts_ref.shape[0]

    def lane_tile(t, carry):
        c0 = pl.multiple_of(t * lanes, lanes)
        rows_t = rows_t_ref[:, pl.ds(c0, lanes)]
        rs = jnp.broadcast_to(rs_ref[:, pl.ds(c0, lanes)], (pt_chunk, lanes))

        def chunk(p, acc):
            p0 = pl.multiple_of(p * pt_chunk, pt_chunk)
            neg_two_dot = jnp.dot(pts_ref[pl.ds(p0, pt_chunk), :], rows_t,
                                  preferred_element_type=jnp.float32)
            sq = (rs + cs_ref[pl.ds(p0, pt_chunk), :]) + neg_two_dot
            m = jnp.sqrt(jnp.maximum(sq, 0.0)) * (-KERNEL_RATE)
            term = ((1.0 - m) * jnp.exp(m)) * coef_ref[pl.ds(p0, pt_chunk), :]
            return acc + jnp.sum(term.reshape(pt_chunk // sub, sub, lanes), axis=0)

        acc = lax.fori_loop(0, n_pts // pt_chunk, chunk, jnp.zeros((sub, lanes), jnp.float32))
        out_ref[:, pl.ds(c0, lanes)] = jnp.sum(acc, axis=0, keepdims=True)
        return carry

    lax.fori_loop(0, out_ref.shape[1] // lanes, lane_tile, 0)


def column_sums(row_feats, piece_points, every_coef):
    n_rows, n_pts = row_feats.shape[0], piece_points.shape[0]
    lanes = 128
    row_sq = jnp.sum(jnp.square(row_feats.astype(jnp.float32)), axis=1)[None, :]
    col_sq = jnp.sum(jnp.square(piece_points.astype(jnp.float32)), axis=1)
    col_sq = jnp.broadcast_to(col_sq[:, None], (n_pts, lanes))
    coef = jnp.broadcast_to(every_coef[:, None], (n_pts, lanes))
    neg_two_rows_t = (row_feats * jnp.asarray(-2.0, row_feats.dtype)).T
    block = math.gcd(n_rows, 512)
    full = lambda i: (0, 0)
    return pl.pallas_call(
        tile_kernel,
        out_shape=jax.ShapeDtypeStruct((1, n_rows), jnp.float32),
        grid=(n_rows // block,),
        in_specs=[
            pl.BlockSpec(piece_points.shape, full),
            pl.BlockSpec((row_feats.shape[1], block), lambda i: (0, i)),
            pl.BlockSpec((1, block), lambda i: (0, i)),
            pl.BlockSpec((n_pts, lanes), full),
            pl.BlockSpec((n_pts, lanes), full),
        ],
        out_specs=pl.BlockSpec((1, block), lambda i: (0, i)),
        cost_estimate=pl.CostEstimate(
            flops=n_rows * n_pts * (2 * row_feats.shape[1] + 10),
            transcendentals=2 * n_rows * n_pts,
            bytes_accessed=2 * (n_rows + n_pts) * row_feats.shape[1] + 1024 * n_pts),
    )(piece_points, neg_two_rows_t, row_sq, col_sq, coef).reshape(-1)


def per_device(n_blk, n_str, points, coefficients, velocity, targets, batch_rows, counts):
    preview = coefficients + MOMENTUM * velocity
    slot_total = batch_rows.shape[0]
    local_size = points.shape[0]
    slot_ids = jnp.arange(slot_total, dtype=jnp.int32)
    count_here = counts.reshape((1,))
    in_count = slot_ids < count_here[0]
    picked = jnp.take(points, batch_rows, axis=0)
    g = 8
    rows_all, pts_all, prev_all = gather_all(picked, points, preview.reshape(1, -1), g)
    group_rows = rows_all.reshape(-1, points.shape[1])
    piece_points = pts_all.reshape(-1, points.shape[1])
    every_coef = prev_all.reshape(-1)
    partial_value = column_sums(group_rows, piece_points, every_coef)
    kernel_rows = scatter_all(partial_value.reshape(g, g, slot_total), g).reshape(-1)
    residual = jnp.where(
        in_count,
        kernel_rows + NOISE_VAR * jnp.take(preview, batch_rows) - jnp.take(targets, batch_rows),
        0.0,
    )
    scatter_rows = (batch_rows[:, None] == jnp.arange(local_size, dtype=jnp.int32)[None, :]).astype(
        jnp.float32
    )
    update_sum = jnp.dot(residual, scatter_rows, precision=lax.Precision.HIGHEST)
    new_velocity = MOMENTUM * velocity - STEP_SIZE * update_sum
    new_coefficients = coefficients + new_velocity
    return (new_coefficients, new_velocity)


def solution(mesh):
    n_blk = mesh.shape["blk"]
    n_str = mesh.shape["stripe"]
    in_specs = (
        P(("blk", "stripe"), None),
        P(("blk", "stripe")),
        P(("blk", "stripe")),
        P(("blk", "stripe")),
        P(("blk", "stripe")),
        P("blk", "stripe"),
    )
    out_specs = (P(("blk", "stripe")), P(("blk", "stripe")))
    return jax.shard_map(
        functools.partial(per_device, n_blk, n_str), mesh=mesh, in_specs=in_specs,
        out_specs=out_specs, check_vma=False
    )
```

```python
import functools
import math

import jax
import jax.numpy as jnp
from jax import lax
from jax.experimental import pallas as pl
from jax.experimental.pallas import tpu as pltpu
from jax.sharding import PartitionSpec as P

MOMENTUM = 0.9
STEP_SIZE = 1.0
NOISE_VAR = 8.0
KERNEL_RATE = 3.0**0.5 / 6.0

MESH_ID = pl.DeviceIdType.MESH
ANY = pl.BlockSpec(memory_space=pl.ANY)


def coords():
    b = lax.axis_index("blk")
    s = lax.axis_index("stripe")
    core = lax.rem(s, 2)
    z_hi = lax.rem(s // 2, 2)
    x = lax.rem(s // 4, 4)
    y = s // 16
    c = lax.rem(b, 2) * 4 + lax.rem(x, 2) * 2 + core
    q = y * 2 + x // 2
    w = (b // 2) * 2 + z_hi
    return c, q, w


def dev(c, q, w):
    b = (w // 2) * 2 + c // 4
    z_hi = lax.rem(w, 2)
    y = q // 2
    x = lax.rem(q, 2) * 2 + lax.rem(c // 2, 2)
    core = lax.rem(c, 2)
    return (b, ((y * 4 + x) * 2 + z_hi) * 2 + core)


def greet_all(barrier, peers_of, n, total):
    def greet(i, carry):
        pl.semaphore_signal(barrier, 1, device_id=peers_of(i), device_id_type=MESH_ID)
        return carry

    lax.fori_loop(0, n, greet, 0)
    return total + n


def gather_kernel(g, picked, pts, prev, rows_out, pts_out, prev_out,
                  in_send, in_recv, out_send, out_recv, pt_send, pt_recv, pv_send, pv_recv,
                  local_sem):
    c, q, w = coords()
    barrier = pltpu.get_barrier_semaphore()
    n = greet_all(barrier, lambda i: dev(c, q, lax.rem(w + 1 + i, g)), g - 1, 0)
    n = greet_all(barrier, lambda i: dev(c, lax.rem(q + 1 + i, g), w), g - 1, n)
    n = greet_all(barrier, lambda i: dev(lax.rem(c + 1 + i, g), q, w), g - 1, n)
    pl.semaphore_wait(barrier, n)
    own = [
        pltpu.make_async_copy(picked, rows_out.at[q, w], local_sem.at[0]),
        pltpu.make_async_copy(pts, pts_out.at[c], local_sem.at[1]),
        pltpu.make_async_copy(prev, prev_out.at[c], local_sem.at[2]),
    ]
    for cp in own:
        cp.start()

    def inner_copy(i, src):
        return pltpu.make_async_remote_copy(
            src_ref=picked, dst_ref=rows_out.at[q, src], send_sem=in_send.at[i],
            recv_sem=in_recv.at[src], device_id=dev(c, q, lax.rem(w + 1 + i, g)),
            device_id_type=MESH_ID)

    def outer_copy(i, src):
        return pltpu.make_async_remote_copy(
            src_ref=rows_out.at[q], dst_ref=rows_out.at[src], send_sem=out_send.at[i],
            recv_sem=out_recv.at[src], device_id=dev(c, lax.rem(q + 1 + i, g), w),
            device_id_type=MESH_ID)

    def group_copies(i, src):
        peer = dev(lax.rem(c + 1 + i, g), q, w)
        return (
            pltpu.make_async_remote_copy(
                src_ref=pts, dst_ref=pts_out.at[src], send_sem=pt_send.at[i],
                recv_sem=pt_recv.at[src], device_id=peer, device_id_type=MESH_ID),
            pltpu.make_async_remote_copy(
                src_ref=prev, dst_ref=prev_out.at[src], send_sem=pv_send.at[i],
                recv_sem=pv_recv.at[src], device_id=peer, device_id_type=MESH_ID),
        )

    def start_inner(i, carry):
        inner_copy(i, w).start()
        return carry

    def start_group(i, carry):
        for cp in group_copies(i, c):
            cp.start()
        return carry

    lax.fori_loop(0, g - 1, start_inner, 0)
    lax.fori_loop(0, g - 1, start_group, 0)

    def wait_inner(i, carry):
        inner_copy(i, w).wait_send()
        inner_copy(i, lax.rem(w + 2 * g - 1 - i, g)).wait_recv()
        return carry

    lax.fori_loop(0, g - 1, wait_inner, 0)
    own[0].wait()

    def start_outer(i, carry):
        outer_copy(i, q).start()
        return carry

    lax.fori_loop(0, g - 1, start_outer, 0)

    def wait_group(i, carry):
        for cp in group_copies(i, c):
            cp.wait_send()
        for cp in group_copies(i, lax.rem(c + 2 * g - 1 - i, g)):
            cp.wait_recv()
        return carry

    def wait_outer(i, carry):
        outer_copy(i, q).wait_send()
        outer_copy(i, lax.rem(q + 2 * g - 1 - i, g)).wait_recv()
        return carry

    lax.fori_loop(0, g - 1, wait_group, 0)
    lax.fori_loop(0, g - 1, wait_outer, 0)
    own[1].wait()
    own[2].wait()


def gather_all(picked, pts, prev, g):
    dma = pltpu.SemaphoreType.DMA
    return pl.pallas_call(
        functools.partial(gather_kernel, g),
        out_shape=(
            jax.ShapeDtypeStruct((g, g) + picked.shape, picked.dtype),
            jax.ShapeDtypeStruct((g,) + pts.shape, pts.dtype),
            jax.ShapeDtypeStruct((g,) + prev.shape, prev.dtype),
        ),
        in_specs=[ANY, ANY, ANY],
        out_specs=(ANY, ANY, ANY),
        scratch_shapes=[dma((g,)) for _ in range(8)] + [dma((3,))],
        compiler_params=pltpu.CompilerParams(has_side_effects=True, collective_id=0),
    )(picked, pts, prev)


def scatter_kernel(g, part, total_out, stage1, mid, stage2,
                   out_send, out_recv, in_send, in_recv, local_sem):
    c, q, w = coords()
    barrier = pltpu.get_barrier_semaphore()
    n = greet_all(barrier, lambda i: dev(c, q, lax.rem(w + 1 + i, g)), g - 1, 0)
    n = greet_all(barrier, lambda i: dev(c, lax.rem(q + 1 + i, g), w), g - 1, n)
    pl.semaphore_wait(barrier, n)
    own1 = pltpu.make_async_copy(part.at[q], stage1.at[q], local_sem.at[0])
    own1.start()

    def outer_copy(i, src):
        peer = lax.rem(q + 1 + i, g)
        return pltpu.make_async_remote_copy(
            src_ref=part.at[peer], dst_ref=stage1.at[src], send_sem=out_send.at[i],
            recv_sem=out_recv.at[src], device_id=dev(c, peer, w), device_id_type=MESH_ID)

    def inner_copy(i, src):
        peer = lax.rem(w + 1 + i, g)
        return pltpu.make_async_remote_copy(
            src_ref=mid.at[peer], dst_ref=stage2.at[src], send_sem=in_send.at[i],
            recv_sem=in_recv.at[src], device_id=dev(c, q, peer), device_id_type=MESH_ID)

    def start_outer(i, carry):
        outer_copy(i, q).start()
        return carry

    lax.fori_loop(0, g - 1, start_outer, 0)

    def wait_outer(i, carry):
        outer_copy(i, q).wait_send()
        outer_copy(i, lax.rem(q + 2 * g - 1 - i, g)).wait_recv()
        return carry

    lax.fori_loop(0, g - 1, wait_outer, 0)
    own1.wait()
    mid[...] = jnp.sum(stage1[...], axis=0)[:, None, :]
    own2 = pltpu.make_async_copy(mid.at[w], stage2.at[w], local_sem.at[1])
    own2.start()

    def start_inner(i, carry):
        inner_copy(i, w).start()
        return carry

    lax.fori_loop(0, g - 1, start_inner, 0)

    def wait_inner(i, carry):
        inner_copy(i, w).wait_send()
        inner_copy(i, lax.rem(w + 2 * g - 1 - i, g)).wait_recv()
        return carry

    lax.fori_loop(0, g - 1, wait_inner, 0)
    own2.wait()
    total_out[...] = jnp.sum(stage2[...], axis=0)


def scatter_all(part, g):
    dma = pltpu.SemaphoreType.DMA
    vmem = pl.BlockSpec(memory_space=pltpu.VMEM)
    width = part.shape[-1]
    return pl.pallas_call(
        functools.partial(scatter_kernel, g),
        out_shape=jax.ShapeDtypeStruct((1, width), part.dtype),
        in_specs=[vmem],
        out_specs=vmem,
        scratch_shapes=[
            pltpu.VMEM((g, g, width), jnp.float32),
            pltpu.VMEM((g, 1, width), jnp.float32),
            pltpu.VMEM((g, 1, width), jnp.float32),
            dma((g,)), dma((g,)), dma((g,)), dma((g,)), dma((2,)),
        ],
        compiler_params=pltpu.CompilerParams(has_side_effects=True, collective_id=1),
    )(part)


def tile_kernel(rows_ref, pts_ref, coef_ref, out_ref):
    row_chunk, col_chunk, lanes = 64, 512, 128
    n_cols = pts_ref.shape[0]

    def body(r, carry):
        r0 = pl.multiple_of(r * row_chunk, row_chunk)
        rows = rows_ref[pl.ds(r0, row_chunk), :]
        acc = jnp.zeros((row_chunk, lanes), jnp.float32)
        for cj in range(n_cols // col_chunk):
            cols = slice(cj * col_chunk, (cj + 1) * col_chunk)
            sq = lax.dot_general(
                rows, pts_ref[cols, :], (((1,), (1,)), ((), ())),
                preferred_element_type=jnp.float32)
            dist = jnp.where(sq > 0.0, sq * lax.rsqrt(sq), 0.0)
            m = dist * (-KERNEL_RATE)
            term = ((1.0 - m) * jnp.exp(m)) * coef_ref[:, cols]
            for l in range(col_chunk // lanes):
                acc = acc + term[:, l * lanes:(l + 1) * lanes]
        out_ref[pl.ds(r0, row_chunk), :] = jnp.sum(acc, axis=1, keepdims=True)
        return carry

    lax.fori_loop(0, rows_ref.shape[0] // row_chunk, body, 0)


def split3(v):
    hi = lax.reduce_precision(v, exponent_bits=8, mantissa_bits=7)
    rest = v - hi
    mid = lax.reduce_precision(rest, exponent_bits=8, mantissa_bits=7)
    lo = rest - mid
    return jnp.stack([hi, mid, lo], axis=1).astype(jnp.bfloat16)


def column_sums(row_feats, piece_points, every_coef):
    n_rows, n_cols = row_feats.shape[0], piece_points.shape[0]
    depth = row_feats.shape[1]
    width = 128 * ((depth + 6 + 127) // 128)
    row_sq = jnp.sum(jnp.square(row_feats.astype(jnp.float32)), axis=1)
    col_sq = jnp.sum(jnp.square(piece_points.astype(jnp.float32)), axis=1)
    one = jnp.bfloat16
    rows_aug = jnp.concatenate([
        row_feats * jnp.asarray(-2.0, one), jnp.ones((n_rows, 3), one), split3(row_sq),
        jnp.zeros((n_rows, width - depth - 6), one)], axis=1)
    pts_aug = jnp.concatenate([
        piece_points, split3(col_sq), jnp.ones((n_cols, 3), one),
        jnp.zeros((n_cols, width - depth - 6), one)], axis=1)
    block = math.gcd(n_rows, 512)
    full = lambda i: (0, 0)
    return pl.pallas_call(
        tile_kernel,
        out_shape=jax.ShapeDtypeStruct((n_rows, 1), jnp.float32),
        grid=(n_rows // block,),
        in_specs=[
            pl.BlockSpec((block, width), lambda i: (i, 0)),
            pl.BlockSpec((n_cols, width), full),
            pl.BlockSpec((1, n_cols), full),
        ],
        out_specs=pl.BlockSpec((block, 1), lambda i: (i, 0)),
        cost_estimate=pl.CostEstimate(
            flops=n_rows * n_cols * (2 * width + 10),
            transcendentals=2 * n_rows * n_cols,
            bytes_accessed=2 * (n_rows + n_cols) * width + 4 * (n_rows + n_cols)),
    )(rows_aug, pts_aug, every_coef[None, :]).reshape(-1)


def per_device(n_blk, n_str, points, coefficients, velocity, targets, batch_rows, counts):
    preview = coefficients + MOMENTUM * velocity
    slot_total = batch_rows.shape[0]
    local_size = points.shape[0]
    slot_ids = jnp.arange(slot_total, dtype=jnp.int32)
    count_here = counts.reshape((1,))
    in_count = slot_ids < count_here[0]
    picked = jnp.take(points, batch_rows, axis=0)
    g = 8
    rows_all, pts_all, prev_all = gather_all(picked, points, preview.reshape(1, -1), g)
    group_rows = rows_all.reshape(-1, points.shape[1])
    piece_points = pts_all.reshape(-1, points.shape[1])
    every_coef = prev_all.reshape(-1)
    partial_value = column_sums(group_rows, piece_points, every_coef)
    kernel_rows = scatter_all(partial_value.reshape(g, g, slot_total), g).reshape(-1)
    residual = jnp.where(
        in_count,
        kernel_rows + NOISE_VAR * jnp.take(preview, batch_rows) - jnp.take(targets, batch_rows),
        0.0,
    )
    scatter_rows = (batch_rows[:, None] == jnp.arange(local_size, dtype=jnp.int32)[None, :]).astype(
        jnp.float32
    )
    update_sum = jnp.dot(residual, scatter_rows, precision=lax.Precision.HIGHEST)
    new_velocity = MOMENTUM * velocity - STEP_SIZE * update_sum
    new_coefficients = coefficients + new_velocity
    return (new_coefficients, new_velocity)


def solution(mesh):
    n_blk = mesh.shape["blk"]
    n_str = mesh.shape["stripe"]
    in_specs = (
        P(("blk", "stripe"), None),
        P(("blk", "stripe")),
        P(("blk", "stripe")),
        P(("blk", "stripe")),
        P(("blk", "stripe")),
        P("blk", "stripe"),
    )
    out_specs = (P(("blk", "stripe")), P(("blk", "stripe")))
    return jax.shard_map(
        functools.partial(per_device, n_blk, n_str), mesh=mesh, in_specs=in_specs,
        out_specs=out_specs, check_vma=False
    )
```

```python
import functools
import math

import jax
import jax.numpy as jnp
from jax import lax
from jax.experimental import pallas as pl
from jax.experimental.pallas import tpu as pltpu
from jax.sharding import PartitionSpec as P

MOMENTUM = 0.9
STEP_SIZE = 1.0
NOISE_VAR = 8.0
KERNEL_RATE = 3.0**0.5 / 6.0

MESH_ID = pl.DeviceIdType.MESH
ANY = pl.BlockSpec(memory_space=pl.ANY)


def coords():
    b = lax.axis_index("blk")
    s = lax.axis_index("stripe")
    core = lax.rem(s, 2)
    z_hi = lax.rem(s // 2, 2)
    x = lax.rem(s // 4, 4)
    y = s // 16
    c = lax.rem(b, 2) * 4 + lax.rem(x, 2) * 2 + core
    q = y * 2 + x // 2
    w = (b // 2) * 2 + z_hi
    return c, q, w


def dev(c, q, w):
    b = (w // 2) * 2 + c // 4
    z_hi = lax.rem(w, 2)
    y = q // 2
    x = lax.rem(q, 2) * 2 + lax.rem(c // 2, 2)
    core = lax.rem(c, 2)
    return (b, ((y * 4 + x) * 2 + z_hi) * 2 + core)


def greet_all(barrier, peers_of, n, total):
    def greet(i, carry):
        pl.semaphore_signal(barrier, 1, device_id=peers_of(i), device_id_type=MESH_ID)
        return carry

    lax.fori_loop(0, n, greet, 0)
    return total + n


def gather_kernel(g, picked, pts, prev, rows_out, pts_out, prev_out,
                  in_send, in_recv, out_send, out_recv, pt_send, pt_recv, pv_send, pv_recv,
                  local_sem):
    c, q, w = coords()
    barrier = pltpu.get_barrier_semaphore()
    n = greet_all(barrier, lambda i: dev(c, q, lax.rem(w + 1 + i, g)), g - 1, 0)
    n = greet_all(barrier, lambda i: dev(c, lax.rem(q + 1 + i, g), w), g - 1, n)
    n = greet_all(barrier, lambda i: dev(lax.rem(c + 1 + i, g), q, w), g - 1, n)
    pl.semaphore_wait(barrier, n)
    own = [
        pltpu.make_async_copy(picked, rows_out.at[q, w], local_sem.at[0]),
        pltpu.make_async_copy(pts, pts_out.at[c], local_sem.at[1]),
        pltpu.make_async_copy(prev, prev_out.at[c], local_sem.at[2]),
    ]
    for cp in own:
        cp.start()

    def inner_copy(i, src):
        return pltpu.make_async_remote_copy(
            src_ref=picked, dst_ref=rows_out.at[q, src], send_sem=in_send.at[i],
            recv_sem=in_recv.at[src], device_id=dev(c, q, lax.rem(w + 1 + i, g)),
            device_id_type=MESH_ID)

    def outer_copy(i, src):
        return pltpu.make_async_remote_copy(
            src_ref=rows_out.at[q], dst_ref=rows_out.at[src], send_sem=out_send.at[i],
            recv_sem=out_recv.at[src], device_id=dev(c, lax.rem(q + 1 + i, g), w),
            device_id_type=MESH_ID)

    def group_copies(i, src):
        peer = dev(lax.rem(c + 1 + i, g), q, w)
        return (
            pltpu.make_async_remote_copy(
                src_ref=pts, dst_ref=pts_out.at[src], send_sem=pt_send.at[i],
                recv_sem=pt_recv.at[src], device_id=peer, device_id_type=MESH_ID),
            pltpu.make_async_remote_copy(
                src_ref=prev, dst_ref=prev_out.at[src], send_sem=pv_send.at[i],
                recv_sem=pv_recv.at[src], device_id=peer, device_id_type=MESH_ID),
        )

    def start_inner(i, carry):
        inner_copy(i, w).start()
        return carry

    def start_group(i, carry):
        for cp in group_copies(i, c):
            cp.start()
        return carry

    lax.fori_loop(0, g - 1, start_inner, 0)
    lax.fori_loop(0, g - 1, start_group, 0)

    def wait_inner(i, carry):
        inner_copy(i, w).wait_send()
        inner_copy(i, lax.rem(w + 2 * g - 1 - i, g)).wait_recv()
        return carry

    lax.fori_loop(0, g - 1, wait_inner, 0)
    own[0].wait()

    def start_outer(i, carry):
        outer_copy(i, q).start()
        return carry

    lax.fori_loop(0, g - 1, start_outer, 0)

    def wait_group(i, carry):
        for cp in group_copies(i, c):
            cp.wait_send()
        for cp in group_copies(i, lax.rem(c + 2 * g - 1 - i, g)):
            cp.wait_recv()
        return carry

    def wait_outer(i, carry):
        outer_copy(i, q).wait_send()
        outer_copy(i, lax.rem(q + 2 * g - 1 - i, g)).wait_recv()
        return carry

    lax.fori_loop(0, g - 1, wait_group, 0)
    lax.fori_loop(0, g - 1, wait_outer, 0)
    own[1].wait()
    own[2].wait()


def gather_all(picked, pts, prev, g):
    dma = pltpu.SemaphoreType.DMA
    return pl.pallas_call(
        functools.partial(gather_kernel, g),
        out_shape=(
            jax.ShapeDtypeStruct((g, g) + picked.shape, picked.dtype),
            jax.ShapeDtypeStruct((g,) + pts.shape, pts.dtype),
            jax.ShapeDtypeStruct((g,) + prev.shape, prev.dtype),
        ),
        in_specs=[ANY, ANY, ANY],
        out_specs=(ANY, ANY, ANY),
        scratch_shapes=[dma((g,)) for _ in range(8)] + [dma((3,))],
        compiler_params=pltpu.CompilerParams(has_side_effects=True, collective_id=0),
    )(picked, pts, prev)


def scatter_kernel(g, part, total_out, stage1, mid, stage2,
                   out_send, out_recv, in_send, in_recv, local_sem):
    c, q, w = coords()
    barrier = pltpu.get_barrier_semaphore()
    n = greet_all(barrier, lambda i: dev(c, q, lax.rem(w + 1 + i, g)), g - 1, 0)
    n = greet_all(barrier, lambda i: dev(c, lax.rem(q + 1 + i, g), w), g - 1, n)
    pl.semaphore_wait(barrier, n)
    own1 = pltpu.make_async_copy(part.at[q], stage1.at[q], local_sem.at[0])
    own1.start()

    def outer_copy(i, src):
        peer = lax.rem(q + 1 + i, g)
        return pltpu.make_async_remote_copy(
            src_ref=part.at[peer], dst_ref=stage1.at[src], send_sem=out_send.at[i],
            recv_sem=out_recv.at[src], device_id=dev(c, peer, w), device_id_type=MESH_ID)

    def inner_copy(i, src):
        peer = lax.rem(w + 1 + i, g)
        return pltpu.make_async_remote_copy(
            src_ref=mid.at[peer], dst_ref=stage2.at[src], send_sem=in_send.at[i],
            recv_sem=in_recv.at[src], device_id=dev(c, q, peer), device_id_type=MESH_ID)

    def start_outer(i, carry):
        outer_copy(i, q).start()
        return carry

    lax.fori_loop(0, g - 1, start_outer, 0)

    def wait_outer(i, carry):
        outer_copy(i, q).wait_send()
        outer_copy(i, lax.rem(q + 2 * g - 1 - i, g)).wait_recv()
        return carry

    lax.fori_loop(0, g - 1, wait_outer, 0)
    own1.wait()
    mid[...] = jnp.sum(stage1[...], axis=0)[:, None, :]
    own2 = pltpu.make_async_copy(mid.at[w], stage2.at[w], local_sem.at[1])
    own2.start()

    def start_inner(i, carry):
        inner_copy(i, w).start()
        return carry

    lax.fori_loop(0, g - 1, start_inner, 0)

    def wait_inner(i, carry):
        inner_copy(i, w).wait_send()
        inner_copy(i, lax.rem(w + 2 * g - 1 - i, g)).wait_recv()
        return carry

    lax.fori_loop(0, g - 1, wait_inner, 0)
    own2.wait()
    total_out[...] = jnp.sum(stage2[...], axis=0)


def scatter_all(part, g):
    dma = pltpu.SemaphoreType.DMA
    vmem = pl.BlockSpec(memory_space=pltpu.VMEM)
    width = part.shape[-1]
    return pl.pallas_call(
        functools.partial(scatter_kernel, g),
        out_shape=jax.ShapeDtypeStruct((1, width), part.dtype),
        in_specs=[vmem],
        out_specs=vmem,
        scratch_shapes=[
            pltpu.VMEM((g, g, width), jnp.float32),
            pltpu.VMEM((g, 1, width), jnp.float32),
            pltpu.VMEM((g, 1, width), jnp.float32),
            dma((g,)), dma((g,)), dma((g,)), dma((g,)), dma((2,)),
        ],
        compiler_params=pltpu.CompilerParams(has_side_effects=True, collective_id=1),
    )(part)


def matern_sums(row_feats, row_sq, col_points, col_coef):
    col_sq = jnp.sum(jnp.square(col_points.astype(jnp.float32)), axis=1)
    inner_prod = lax.dot_general(
        row_feats, col_points, (((1,), (1,)), ((), ())), preferred_element_type=jnp.float32
    )
    distance = jnp.sqrt(jnp.maximum(row_sq[:, None] + col_sq[None, :] - 2.0 * inner_prod, 0.0))
    scaled = KERNEL_RATE * distance
    kernel_tile = (1.0 + scaled) * jnp.exp(-scaled)
    return jnp.sum(kernel_tile * col_coef[None, :], axis=1)


def column_sums(row_feats, piece_points, every_coef):
    row_sq = jnp.sum(jnp.square(row_feats.astype(jnp.float32)), axis=1)
    zeros_init = jnp.zeros((row_feats.shape[0],), jnp.float32)
    piece_len = piece_points.shape[0]
    block_len = math.gcd(piece_len, 512)
    point_blocks = piece_points.reshape(-1, block_len, piece_points.shape[1])
    coef_blocks = every_coef.reshape(-1, block_len)

    def advance(partial_sum, column_block):
        return (
            partial_sum + matern_sums(row_feats, row_sq, column_block[0], column_block[1]),
            None,
        )

    result, unused = lax.scan(advance, zeros_init, (point_blocks, coef_blocks))
    return result


def per_device(n_blk, n_str, points, coefficients, velocity, targets, batch_rows, counts):
    preview = coefficients + MOMENTUM * velocity
    slot_total = batch_rows.shape[0]
    local_size = points.shape[0]
    slot_ids = jnp.arange(slot_total, dtype=jnp.int32)
    count_here = counts.reshape((1,))
    in_count = slot_ids < count_here[0]
    picked = jnp.take(points, batch_rows, axis=0)
    g = 8
    lanes = 128
    dense = lambda a: a.reshape(-1, lanes)
    rows_all, pts_all, prev_all = gather_all(
        dense(picked), dense(points), preview.reshape(1, -1), g)
    group_rows = rows_all.reshape(-1, points.shape[1])
    piece_points = pts_all.reshape(-1, points.shape[1])
    every_coef = prev_all.reshape(-1)
    partial_value = column_sums(group_rows, piece_points, every_coef)
    kernel_rows = scatter_all(partial_value.reshape(g, g, slot_total), g).reshape(-1)
    residual = jnp.where(
        in_count,
        kernel_rows + NOISE_VAR * jnp.take(preview, batch_rows) - jnp.take(targets, batch_rows),
        0.0,
    )
    scatter_rows = (batch_rows[:, None] == jnp.arange(local_size, dtype=jnp.int32)[None, :]).astype(
        jnp.float32
    )
    update_sum = jnp.dot(residual, scatter_rows, precision=lax.Precision.HIGHEST)
    new_velocity = MOMENTUM * velocity - STEP_SIZE * update_sum
    new_coefficients = coefficients + new_velocity
    return (new_coefficients, new_velocity)


def solution(mesh):
    n_blk = mesh.shape["blk"]
    n_str = mesh.shape["stripe"]
    in_specs = (
        P(("blk", "stripe"), None),
        P(("blk", "stripe")),
        P(("blk", "stripe")),
        P(("blk", "stripe")),
        P(("blk", "stripe")),
        P("blk", "stripe"),
    )
    out_specs = (P(("blk", "stripe")), P(("blk", "stripe")))
    return jax.shard_map(
        functools.partial(per_device, n_blk, n_str), mesh=mesh, in_specs=in_specs,
        out_specs=out_specs, check_vma=False
    )
```

```python
import functools
import math

import jax
import jax.numpy as jnp
from jax import lax
from jax.experimental import pallas as pl
from jax.experimental.pallas import tpu as pltpu
from jax.sharding import PartitionSpec as P

MOMENTUM = 0.9
STEP_SIZE = 1.0
NOISE_VAR = 8.0
KERNEL_RATE = 3.0**0.5 / 6.0

MESH_ID = pl.DeviceIdType.MESH
ANY = pl.BlockSpec(memory_space=pl.ANY)


def coords():
    b = lax.axis_index("blk")
    s = lax.axis_index("stripe")
    core = lax.rem(s, 2)
    z_hi = lax.rem(s // 2, 2)
    x = lax.rem(s // 4, 4)
    y = s // 16
    c = lax.rem(b, 2) * 4 + lax.rem(x, 2) * 2 + core
    q = y * 2 + x // 2
    w = (b // 2) * 2 + z_hi
    return c, q, w


def dev(c, q, w):
    b = (w // 2) * 2 + c // 4
    z_hi = lax.rem(w, 2)
    y = q // 2
    x = lax.rem(q, 2) * 2 + lax.rem(c // 2, 2)
    core = lax.rem(c, 2)
    return (b, ((y * 4 + x) * 2 + z_hi) * 2 + core)


def greet_all(barrier, peers_of, n, total):
    def greet(i, carry):
        pl.semaphore_signal(barrier, 1, device_id=peers_of(i), device_id_type=MESH_ID)
        return carry

    lax.fori_loop(0, n, greet, 0)
    return total + n


def gather_kernel(g, picked, pts, prev, rows_out, pts_out, prev_out,
                  in_send, in_recv, out_send, out_recv, pt_send, pt_recv, pv_send, pv_recv,
                  local_sem):
    c, q, w = coords()
    barrier = pltpu.get_barrier_semaphore()
    n = greet_all(barrier, lambda i: dev(c, q, lax.rem(w + 1 + i, g)), g - 1, 0)
    n = greet_all(barrier, lambda i: dev(c, lax.rem(q + 1 + i, g), w), g - 1, n)
    n = greet_all(barrier, lambda i: dev(lax.rem(c + 1 + i, g), q, w), g - 1, n)
    pl.semaphore_wait(barrier, n)
    own = [
        pltpu.make_async_copy(picked, rows_out.at[q, w], local_sem.at[0]),
        pltpu.make_async_copy(pts, pts_out.at[c], local_sem.at[1]),
        pltpu.make_async_copy(prev, prev_out.at[c], local_sem.at[2]),
    ]
    for cp in own:
        cp.start()

    def inner_copy(i, src):
        return pltpu.make_async_remote_copy(
            src_ref=picked, dst_ref=rows_out.at[q, src], send_sem=in_send.at[i],
            recv_sem=in_recv.at[src], device_id=dev(c, q, lax.rem(w + 1 + i, g)),
            device_id_type=MESH_ID)

    def outer_copy(i, src):
        return pltpu.make_async_remote_copy(
            src_ref=rows_out.at[q], dst_ref=rows_out.at[src], send_sem=out_send.at[i],
            recv_sem=out_recv.at[src], device_id=dev(c, lax.rem(q + 1 + i, g), w),
            device_id_type=MESH_ID)

    def group_copies(i, src):
        peer = dev(lax.rem(c + 1 + i, g), q, w)
        return (
            pltpu.make_async_remote_copy(
                src_ref=pts, dst_ref=pts_out.at[src], send_sem=pt_send.at[i],
                recv_sem=pt_recv.at[src], device_id=peer, device_id_type=MESH_ID),
            pltpu.make_async_remote_copy(
                src_ref=prev, dst_ref=prev_out.at[src], send_sem=pv_send.at[i],
                recv_sem=pv_recv.at[src], device_id=peer, device_id_type=MESH_ID),
        )

    def start_inner(i, carry):
        inner_copy(i, w).start()
        return carry

    def start_group(i, carry):
        for cp in group_copies(i, c):
            cp.start()
        return carry

    lax.fori_loop(0, g - 1, start_inner, 0)
    lax.fori_loop(0, g - 1, start_group, 0)

    def wait_inner(i, carry):
        inner_copy(i, w).wait_send()
        inner_copy(i, lax.rem(w + 2 * g - 1 - i, g)).wait_recv()
        return carry

    lax.fori_loop(0, g - 1, wait_inner, 0)
    own[0].wait()

    def start_outer(i, carry):
        outer_copy(i, q).start()
        return carry

    lax.fori_loop(0, g - 1, start_outer, 0)

    def wait_group(i, carry):
        for cp in group_copies(i, c):
            cp.wait_send()
        for cp in group_copies(i, lax.rem(c + 2 * g - 1 - i, g)):
            cp.wait_recv()
        return carry

    def wait_outer(i, carry):
        outer_copy(i, q).wait_send()
        outer_copy(i, lax.rem(q + 2 * g - 1 - i, g)).wait_recv()
        return carry

    lax.fori_loop(0, g - 1, wait_group, 0)
    lax.fori_loop(0, g - 1, wait_outer, 0)
    own[1].wait()
    own[2].wait()


def gather_all(picked, pts, prev, g):
    dma = pltpu.SemaphoreType.DMA
    return pl.pallas_call(
        functools.partial(gather_kernel, g),
        out_shape=(
            jax.ShapeDtypeStruct((g, g) + picked.shape, picked.dtype),
            jax.ShapeDtypeStruct((g,) + pts.shape, pts.dtype),
            jax.ShapeDtypeStruct((g,) + prev.shape, prev.dtype),
        ),
        in_specs=[ANY, ANY, ANY],
        out_specs=(ANY, ANY, ANY),
        scratch_shapes=[dma((g,)) for _ in range(8)] + [dma((3,))],
        compiler_params=pltpu.CompilerParams(has_side_effects=True, collective_id=0),
    )(picked, pts, prev)


def scatter_kernel(g, part, total_out, stage1, mid, stage2,
                   out_send, out_recv, in_send, in_recv, local_sem):
    c, q, w = coords()
    barrier = pltpu.get_barrier_semaphore()
    n = greet_all(barrier, lambda i: dev(c, q, lax.rem(w + 1 + i, g)), g - 1, 0)
    n = greet_all(barrier, lambda i: dev(c, lax.rem(q + 1 + i, g), w), g - 1, n)
    pl.semaphore_wait(barrier, n)
    own1 = pltpu.make_async_copy(part.at[q], stage1.at[q], local_sem.at[0])
    own1.start()

    def outer_copy(i, src):
        peer = lax.rem(q + 1 + i, g)
        return pltpu.make_async_remote_copy(
            src_ref=part.at[peer], dst_ref=stage1.at[src], send_sem=out_send.at[i],
            recv_sem=out_recv.at[src], device_id=dev(c, peer, w), device_id_type=MESH_ID)

    def inner_copy(i, src):
        peer = lax.rem(w + 1 + i, g)
        return pltpu.make_async_remote_copy(
            src_ref=mid.at[peer], dst_ref=stage2.at[src], send_sem=in_send.at[i],
            recv_sem=in_recv.at[src], device_id=dev(c, q, peer), device_id_type=MESH_ID)

    def start_outer(i, carry):
        outer_copy(i, q).start()
        return carry

    lax.fori_loop(0, g - 1, start_outer, 0)

    def wait_outer(i, carry):
        outer_copy(i, q).wait_send()
        outer_copy(i, lax.rem(q + 2 * g - 1 - i, g)).wait_recv()
        return carry

    lax.fori_loop(0, g - 1, wait_outer, 0)
    own1.wait()
    mid[...] = jnp.sum(stage1[...], axis=0)[:, None, :]
    own2 = pltpu.make_async_copy(mid.at[w], stage2.at[w], local_sem.at[1])
    own2.start()

    def start_inner(i, carry):
        inner_copy(i, w).start()
        return carry

    lax.fori_loop(0, g - 1, start_inner, 0)

    def wait_inner(i, carry):
        inner_copy(i, w).wait_send()
        inner_copy(i, lax.rem(w + 2 * g - 1 - i, g)).wait_recv()
        return carry

    lax.fori_loop(0, g - 1, wait_inner, 0)
    own2.wait()
    total_out[...] = jnp.sum(stage2[...], axis=0)


def scatter_all(part, g):
    dma = pltpu.SemaphoreType.DMA
    vmem = pl.BlockSpec(memory_space=pltpu.VMEM)
    width = part.shape[-1]
    return pl.pallas_call(
        functools.partial(scatter_kernel, g),
        out_shape=jax.ShapeDtypeStruct((1, width), part.dtype),
        in_specs=[vmem],
        out_specs=vmem,
        scratch_shapes=[
            pltpu.VMEM((g, g, width), jnp.float32),
            pltpu.VMEM((g, 1, width), jnp.float32),
            pltpu.VMEM((g, 1, width), jnp.float32),
            dma((g,)), dma((g,)), dma((g,)), dma((g,)), dma((2,)),
        ],
        compiler_params=pltpu.CompilerParams(has_side_effects=True, collective_id=1),
    )(part)


def matern_sums(neg_two_rows, row_sq, col_points, col_coef):
    col_sq = jnp.sum(jnp.square(col_points.astype(jnp.float32)), axis=1)
    neg_two_dot = lax.dot_general(
        neg_two_rows, col_points, (((1,), (1,)), ((), ())), preferred_element_type=jnp.float32
    )
    sq = (row_sq[:, None] + col_sq[None, :]) + neg_two_dot
    distance = jnp.where(sq > 0.0, sq * lax.rsqrt(sq), 0.0)
    m = distance * (-KERNEL_RATE)
    kernel_tile = (1.0 - m) * jnp.exp(m)
    return jnp.sum(kernel_tile * col_coef[None, :], axis=1)


def column_sums(row_feats, piece_points, every_coef):
    row_sq = jnp.sum(jnp.square(row_feats.astype(jnp.float32)), axis=1)
    neg_two_rows = row_feats * jnp.asarray(-2.0, row_feats.dtype)
    zeros_init = jnp.zeros((row_feats.shape[0],), jnp.float32)
    piece_len = piece_points.shape[0]
    block_len = math.gcd(piece_len, 512)
    point_blocks = piece_points.reshape(-1, block_len, piece_points.shape[1])
    coef_blocks = every_coef.reshape(-1, block_len)

    def advance(partial_sum, column_block):
        return (
            partial_sum + matern_sums(neg_two_rows, row_sq, column_block[0], column_block[1]),
            None,
        )

    result, unused = lax.scan(advance, zeros_init, (point_blocks, coef_blocks))
    return result


def per_device(n_blk, n_str, points, coefficients, velocity, targets, batch_rows, counts):
    preview = coefficients + MOMENTUM * velocity
    slot_total = batch_rows.shape[0]
    local_size = points.shape[0]
    slot_ids = jnp.arange(slot_total, dtype=jnp.int32)
    count_here = counts.reshape((1,))
    in_count = slot_ids < count_here[0]
    picked = jnp.take(points, batch_rows, axis=0)
    g = 8
    lanes = 128
    dense = lambda a: a.reshape(-1, lanes)
    rows_all, pts_all, prev_all = gather_all(
        dense(picked), dense(points), preview.reshape(1, -1), g)
    group_rows = rows_all.reshape(-1, points.shape[1])
    piece_points = pts_all.reshape(-1, points.shape[1])
    every_coef = prev_all.reshape(-1)
    partial_value = column_sums(group_rows, piece_points, every_coef)
    kernel_rows = scatter_all(partial_value.reshape(g, g, slot_total), g).reshape(-1)
    residual = jnp.where(
        in_count,
        kernel_rows + NOISE_VAR * jnp.take(preview, batch_rows) - jnp.take(targets, batch_rows),
        0.0,
    )
    scatter_rows = (batch_rows[:, None] == jnp.arange(local_size, dtype=jnp.int32)[None, :]).astype(
        jnp.float32
    )
    update_sum = jnp.dot(residual, scatter_rows, precision=lax.Precision.HIGHEST)
    new_velocity = MOMENTUM * velocity - STEP_SIZE * update_sum
    new_coefficients = coefficients + new_velocity
    return (new_coefficients, new_velocity)


def solution(mesh):
    n_blk = mesh.shape["blk"]
    n_str = mesh.shape["stripe"]
    in_specs = (
        P(("blk", "stripe"), None),
        P(("blk", "stripe")),
        P(("blk", "stripe")),
        P(("blk", "stripe")),
        P(("blk", "stripe")),
        P("blk", "stripe"),
    )
    out_specs = (P(("blk", "stripe")), P(("blk", "stripe")))
    return jax.shard_map(
        functools.partial(per_device, n_blk, n_str), mesh=mesh, in_specs=in_specs,
        out_specs=out_specs, check_vma=False
    )
```

```python
import functools
import math

import jax
import jax.numpy as jnp
from jax import lax
from jax.experimental import pallas as pl
from jax.experimental.pallas import tpu as pltpu
from jax.sharding import PartitionSpec as P

MOMENTUM = 0.9
STEP_SIZE = 1.0
NOISE_VAR = 8.0
KERNEL_RATE = 3.0**0.5 / 6.0

MESH_ID = pl.DeviceIdType.MESH
ANY = pl.BlockSpec(memory_space=pl.ANY)


def coords():
    b = lax.axis_index("blk")
    s = lax.axis_index("stripe")
    core = lax.rem(s, 2)
    z_hi = lax.rem(s // 2, 2)
    x = lax.rem(s // 4, 4)
    y = s // 16
    c = lax.rem(b, 2) * 4 + lax.rem(x, 2) * 2 + core
    q = y * 2 + x // 2
    w = (b // 2) * 2 + z_hi
    return c, q, w


def dev(c, q, w):
    b = (w // 2) * 2 + c // 4
    z_hi = lax.rem(w, 2)
    y = q // 2
    x = lax.rem(q, 2) * 2 + lax.rem(c // 2, 2)
    core = lax.rem(c, 2)
    return (b, ((y * 4 + x) * 2 + z_hi) * 2 + core)


def greet_all(barrier, peers_of, n, total):
    def greet(i, carry):
        pl.semaphore_signal(barrier, 1, device_id=peers_of(i), device_id_type=MESH_ID)
        return carry

    lax.fori_loop(0, n, greet, 0)
    return total + n


def gather_kernel(g, picked, pts, prev, rows_out, pts_out, prev_out,
                  in_send, in_recv, out_send, out_recv, pt_send, pt_recv, pv_send, pv_recv,
                  local_sem):
    c, q, w = coords()
    barrier = pltpu.get_barrier_semaphore()
    n = greet_all(barrier, lambda i: dev(c, q, lax.rem(w + 1 + i, g)), g - 1, 0)
    n = greet_all(barrier, lambda i: dev(c, lax.rem(q + 1 + i, g), w), g - 1, n)
    n = greet_all(barrier, lambda i: dev(lax.rem(c + 1 + i, g), q, w), g - 1, n)
    pl.semaphore_wait(barrier, n)
    own = [
        pltpu.make_async_copy(picked, rows_out.at[q, w], local_sem.at[0]),
        pltpu.make_async_copy(pts, pts_out.at[c], local_sem.at[1]),
        pltpu.make_async_copy(prev, prev_out.at[c], local_sem.at[2]),
    ]
    for cp in own:
        cp.start()

    def inner_copy(i, src):
        return pltpu.make_async_remote_copy(
            src_ref=picked, dst_ref=rows_out.at[q, src], send_sem=in_send.at[i],
            recv_sem=in_recv.at[src], device_id=dev(c, q, lax.rem(w + 1 + i, g)),
            device_id_type=MESH_ID)

    def outer_copy(i, src):
        return pltpu.make_async_remote_copy(
            src_ref=rows_out.at[q], dst_ref=rows_out.at[src], send_sem=out_send.at[i],
            recv_sem=out_recv.at[src], device_id=dev(c, lax.rem(q + 1 + i, g), w),
            device_id_type=MESH_ID)

    def group_copies(i, src):
        peer = dev(lax.rem(c + 1 + i, g), q, w)
        return (
            pltpu.make_async_remote_copy(
                src_ref=pts, dst_ref=pts_out.at[src], send_sem=pt_send.at[i],
                recv_sem=pt_recv.at[src], device_id=peer, device_id_type=MESH_ID),
            pltpu.make_async_remote_copy(
                src_ref=prev, dst_ref=prev_out.at[src], send_sem=pv_send.at[i],
                recv_sem=pv_recv.at[src], device_id=peer, device_id_type=MESH_ID),
        )

    def start_inner(i, carry):
        inner_copy(i, w).start()
        return carry

    def start_group(i, carry):
        for cp in group_copies(i, c):
            cp.start()
        return carry

    lax.fori_loop(0, g - 1, start_inner, 0)

    def wait_inner(i, carry):
        inner_copy(i, w).wait_send()
        inner_copy(i, lax.rem(w + 2 * g - 1 - i, g)).wait_recv()
        return carry

    lax.fori_loop(0, g - 1, wait_inner, 0)
    own[0].wait()

    def start_outer(i, carry):
        outer_copy(i, q).start()
        return carry

    lax.fori_loop(0, g - 1, start_outer, 0)
    lax.fori_loop(0, g - 1, start_group, 0)

    def wait_group(i, carry):
        for cp in group_copies(i, c):
            cp.wait_send()
        for cp in group_copies(i, lax.rem(c + 2 * g - 1 - i, g)):
            cp.wait_recv()
        return carry

    def wait_outer(i, carry):
        outer_copy(i, q).wait_send()
        outer_copy(i, lax.rem(q + 2 * g - 1 - i, g)).wait_recv()
        return carry

    lax.fori_loop(0, g - 1, wait_group, 0)
    lax.fori_loop(0, g - 1, wait_outer, 0)
    own[1].wait()
    own[2].wait()


def gather_all(picked, pts, prev, g):
    dma = pltpu.SemaphoreType.DMA
    return pl.pallas_call(
        functools.partial(gather_kernel, g),
        out_shape=(
            jax.ShapeDtypeStruct((g, g) + picked.shape, picked.dtype),
            jax.ShapeDtypeStruct((g,) + pts.shape, pts.dtype),
            jax.ShapeDtypeStruct((g,) + prev.shape, prev.dtype),
        ),
        in_specs=[ANY, ANY, ANY],
        out_specs=(ANY, ANY, ANY),
        scratch_shapes=[dma((g,)) for _ in range(8)] + [dma((3,))],
        compiler_params=pltpu.CompilerParams(has_side_effects=True, collective_id=0),
    )(picked, pts, prev)


def scatter_kernel(g, part, total_out, stage1, mid, stage2,
                   out_send, out_recv, in_send, in_recv, local_sem):
    c, q, w = coords()
    barrier = pltpu.get_barrier_semaphore()
    n = greet_all(barrier, lambda i: dev(c, q, lax.rem(w + 1 + i, g)), g - 1, 0)
    n = greet_all(barrier, lambda i: dev(c, lax.rem(q + 1 + i, g), w), g - 1, n)
    pl.semaphore_wait(barrier, n)
    own1 = pltpu.make_async_copy(part.at[q], stage1.at[q], local_sem.at[0])
    own1.start()

    def outer_copy(i, src):
        peer = lax.rem(q + 1 + i, g)
        return pltpu.make_async_remote_copy(
            src_ref=part.at[peer], dst_ref=stage1.at[src], send_sem=out_send.at[i],
            recv_sem=out_recv.at[src], device_id=dev(c, peer, w), device_id_type=MESH_ID)

    def inner_copy(i, src):
        peer = lax.rem(w + 1 + i, g)
        return pltpu.make_async_remote_copy(
            src_ref=mid.at[peer], dst_ref=stage2.at[src], send_sem=in_send.at[i],
            recv_sem=in_recv.at[src], device_id=dev(c, q, peer), device_id_type=MESH_ID)

    def start_outer(i, carry):
        outer_copy(i, q).start()
        return carry

    lax.fori_loop(0, g - 1, start_outer, 0)

    def wait_outer(i, carry):
        outer_copy(i, q).wait_send()
        outer_copy(i, lax.rem(q + 2 * g - 1 - i, g)).wait_recv()
        return carry

    lax.fori_loop(0, g - 1, wait_outer, 0)
    own1.wait()
    mid[...] = jnp.sum(stage1[...], axis=0)[:, None, :]
    own2 = pltpu.make_async_copy(mid.at[w], stage2.at[w], local_sem.at[1])
    own2.start()

    def start_inner(i, carry):
        inner_copy(i, w).start()
        return carry

    lax.fori_loop(0, g - 1, start_inner, 0)

    def wait_inner(i, carry):
        inner_copy(i, w).wait_send()
        inner_copy(i, lax.rem(w + 2 * g - 1 - i, g)).wait_recv()
        return carry

    lax.fori_loop(0, g - 1, wait_inner, 0)
    own2.wait()
    total_out[...] = jnp.sum(stage2[...], axis=0)


def scatter_all(part, g):
    dma = pltpu.SemaphoreType.DMA
    vmem = pl.BlockSpec(memory_space=pltpu.VMEM)
    width = part.shape[-1]
    return pl.pallas_call(
        functools.partial(scatter_kernel, g),
        out_shape=jax.ShapeDtypeStruct((1, width), part.dtype),
        in_specs=[vmem],
        out_specs=vmem,
        scratch_shapes=[
            pltpu.VMEM((g, g, width), jnp.float32),
            pltpu.VMEM((g, 1, width), jnp.float32),
            pltpu.VMEM((g, 1, width), jnp.float32),
            dma((g,)), dma((g,)), dma((g,)), dma((g,)), dma((2,)),
        ],
        compiler_params=pltpu.CompilerParams(has_side_effects=True, collective_id=1),
    )(part)


def matern_sums(neg_two_rows, row_sq, col_points, col_coef):
    col_sq = jnp.sum(jnp.square(col_points.astype(jnp.float32)), axis=1)
    neg_two_dot = lax.dot_general(
        neg_two_rows, col_points, (((1,), (1,)), ((), ())), preferred_element_type=jnp.float32
    )
    sq = (row_sq[:, None] + col_sq[None, :]) + neg_two_dot
    distance = jnp.where(sq > 0.0, sq * lax.rsqrt(sq), 0.0)
    m = distance * (-KERNEL_RATE)
    kernel_tile = (1.0 - m) * jnp.exp(m)
    return jnp.sum(kernel_tile * col_coef[None, :], axis=1)


def column_sums(row_feats, piece_points, every_coef):
    row_sq = jnp.sum(jnp.square(row_feats.astype(jnp.float32)), axis=1)
    neg_two_rows = row_feats * jnp.asarray(-2.0, row_feats.dtype)
    zeros_init = jnp.zeros((row_feats.shape[0],), jnp.float32)
    piece_len = piece_points.shape[0]
    block_len = math.gcd(piece_len, 512)
    point_blocks = piece_points.reshape(-1, block_len, piece_points.shape[1])
    coef_blocks = every_coef.reshape(-1, block_len)

    def advance(partial_sum, column_block):
        return (
            partial_sum + matern_sums(neg_two_rows, row_sq, column_block[0], column_block[1]),
            None,
        )

    result, unused = lax.scan(advance, zeros_init, (point_blocks, coef_blocks))
    return result


def per_device(n_blk, n_str, points, coefficients, velocity, targets, batch_rows, counts):
    preview = coefficients + MOMENTUM * velocity
    slot_total = batch_rows.shape[0]
    local_size = points.shape[0]
    slot_ids = jnp.arange(slot_total, dtype=jnp.int32)
    count_here = counts.reshape((1,))
    in_count = slot_ids < count_here[0]
    picked = jnp.take(points, batch_rows, axis=0)
    g = 8
    lanes = 128
    dense = lambda a: a.reshape(-1, lanes)
    rows_all, pts_all, prev_all = gather_all(
        dense(picked), dense(points), preview.reshape(1, -1), g)
    group_rows = rows_all.reshape(-1, points.shape[1])
    piece_points = pts_all.reshape(-1, points.shape[1])
    every_coef = prev_all.reshape(-1)
    partial_value = column_sums(group_rows, piece_points, every_coef)
    kernel_rows = scatter_all(partial_value.reshape(g, g, slot_total), g).reshape(-1)
    residual = jnp.where(
        in_count,
        kernel_rows + NOISE_VAR * jnp.take(preview, batch_rows) - jnp.take(targets, batch_rows),
        0.0,
    )
    scatter_rows = (batch_rows[:, None] == jnp.arange(local_size, dtype=jnp.int32)[None, :]).astype(
        jnp.float32
    )
    update_sum = jnp.dot(residual, scatter_rows, precision=lax.Precision.HIGHEST)
    new_velocity = MOMENTUM * velocity - STEP_SIZE * update_sum
    new_coefficients = coefficients + new_velocity
    return (new_coefficients, new_velocity)


def solution(mesh):
    n_blk = mesh.shape["blk"]
    n_str = mesh.shape["stripe"]
    in_specs = (
        P(("blk", "stripe"), None),
        P(("blk", "stripe")),
        P(("blk", "stripe")),
        P(("blk", "stripe")),
        P(("blk", "stripe")),
        P("blk", "stripe"),
    )
    out_specs = (P(("blk", "stripe")), P(("blk", "stripe")))
    return jax.shard_map(
        functools.partial(per_device, n_blk, n_str), mesh=mesh, in_specs=in_specs,
        out_specs=out_specs, check_vma=False
    )
```

```python
import functools
import math

import jax
import jax.numpy as jnp
from jax import lax
from jax.experimental import pallas as pl
from jax.experimental.pallas import tpu as pltpu
from jax.sharding import PartitionSpec as P

MOMENTUM = 0.9
STEP_SIZE = 1.0
NOISE_VAR = 8.0
KERNEL_RATE = 3.0**0.5 / 6.0

MESH_ID = pl.DeviceIdType.MESH
ANY = pl.BlockSpec(memory_space=pl.ANY)


def coords():
    b = lax.axis_index("blk")
    s = lax.axis_index("stripe")
    core = lax.rem(s, 2)
    z_hi = lax.rem(s // 2, 2)
    x = lax.rem(s // 4, 4)
    y = s // 16
    c = lax.rem(b, 2) * 4 + lax.rem(x, 2) * 2 + core
    q = y * 2 + x // 2
    w = (b // 2) * 2 + z_hi
    return c, q, w


def dev(c, q, w):
    b = (w // 2) * 2 + c // 4
    z_hi = lax.rem(w, 2)
    y = q // 2
    x = lax.rem(q, 2) * 2 + lax.rem(c // 2, 2)
    core = lax.rem(c, 2)
    return (b, ((y * 4 + x) * 2 + z_hi) * 2 + core)


def greet_all(barrier, peers_of, n, total):
    def greet(i, carry):
        pl.semaphore_signal(barrier, 1, device_id=peers_of(i), device_id_type=MESH_ID)
        return carry

    lax.fori_loop(0, n, greet, 0)
    return total + n


def gather_kernel(g, picked, pts, prev, rows_out, pts_out, prev_out,
                  in_send, in_recv, out_send, out_recv, pt_send, pt_recv, pv_send, pv_recv,
                  local_sem):
    c, q, w = coords()
    barrier = pltpu.get_barrier_semaphore()
    n = greet_all(barrier, lambda i: dev(c, q, lax.rem(w + 1 + i, g)), g - 1, 0)
    n = greet_all(barrier, lambda i: dev(c, lax.rem(q + 1 + i, g), w), g - 1, n)
    n = greet_all(barrier, lambda i: dev(lax.rem(c + 1 + i, g), q, w), g - 1, n)
    pl.semaphore_wait(barrier, n)
    own = [
        pltpu.make_async_copy(picked, rows_out.at[q, w], local_sem.at[0]),
        pltpu.make_async_copy(pts, pts_out.at[c], local_sem.at[1]),
        pltpu.make_async_copy(prev, prev_out.at[c], local_sem.at[2]),
    ]
    for cp in own:
        cp.start()

    def inner_copy(i, src):
        return pltpu.make_async_remote_copy(
            src_ref=picked, dst_ref=rows_out.at[q, src], send_sem=in_send.at[i],
            recv_sem=in_recv.at[src], device_id=dev(c, q, lax.rem(w + 1 + i, g)),
            device_id_type=MESH_ID)

    def outer_copy(i, src):
        return pltpu.make_async_remote_copy(
            src_ref=rows_out.at[q], dst_ref=rows_out.at[src], send_sem=out_send.at[i],
            recv_sem=out_recv.at[src], device_id=dev(c, lax.rem(q + 1 + i, g), w),
            device_id_type=MESH_ID)

    def group_copies(i, src):
        peer = dev(lax.rem(c + 1 + i, g), q, w)
        return (
            pltpu.make_async_remote_copy(
                src_ref=pts, dst_ref=pts_out.at[src], send_sem=pt_send.at[i],
                recv_sem=pt_recv.at[src], device_id=peer, device_id_type=MESH_ID),
            pltpu.make_async_remote_copy(
                src_ref=prev, dst_ref=prev_out.at[src], send_sem=pv_send.at[i],
                recv_sem=pv_recv.at[src], device_id=peer, device_id_type=MESH_ID),
        )

    def start_inner(i, carry):
        inner_copy(i, w).start()
        return carry

    def start_group(i, carry):
        for cp in group_copies(i, c):
            cp.start()
        return carry

    lax.fori_loop(0, g - 1, start_inner, 0)
    lax.fori_loop(0, g - 1, start_group, 0)

    def wait_inner(i, carry):
        inner_copy(i, w).wait_send()
        inner_copy(i, lax.rem(w + 2 * g - 1 - i, g)).wait_recv()
        return carry

    lax.fori_loop(0, g - 1, wait_inner, 0)
    own[0].wait()

    def start_outer(i, carry):
        outer_copy(i, q).start()
        return carry

    lax.fori_loop(0, g - 1, start_outer, 0)

    def wait_group(i, carry):
        for cp in group_copies(i, c):
            cp.wait_send()
        for cp in group_copies(i, lax.rem(c + 2 * g - 1 - i, g)):
            cp.wait_recv()
        return carry

    def wait_outer(i, carry):
        outer_copy(i, q).wait_send()
        outer_copy(i, lax.rem(q + 2 * g - 1 - i, g)).wait_recv()
        return carry

    lax.fori_loop(0, g - 1, wait_group, 0)
    lax.fori_loop(0, g - 1, wait_outer, 0)
    own[1].wait()
    own[2].wait()


def gather_all(picked, pts, prev, g):
    dma = pltpu.SemaphoreType.DMA
    return pl.pallas_call(
        functools.partial(gather_kernel, g),
        out_shape=(
            jax.ShapeDtypeStruct((g, g) + picked.shape, picked.dtype),
            jax.ShapeDtypeStruct((g,) + pts.shape, pts.dtype),
            jax.ShapeDtypeStruct((g,) + prev.shape, prev.dtype),
        ),
        in_specs=[ANY, ANY, ANY],
        out_specs=(ANY, ANY, ANY),
        scratch_shapes=[dma((g,)) for _ in range(8)] + [dma((3,))],
        compiler_params=pltpu.CompilerParams(has_side_effects=True, collective_id=0),
    )(picked, pts, prev)


def scatter_kernel(g, part, total_out, stage1, mid, stage2,
                   out_send, out_recv, in_send, in_recv, local_sem):
    c, q, w = coords()
    barrier = pltpu.get_barrier_semaphore()
    n = greet_all(barrier, lambda i: dev(c, q, lax.rem(w + 1 + i, g)), g - 1, 0)
    n = greet_all(barrier, lambda i: dev(c, lax.rem(q + 1 + i, g), w), g - 1, n)
    pl.semaphore_wait(barrier, n)
    own1 = pltpu.make_async_copy(part.at[q], stage1.at[q], local_sem.at[0])
    own1.start()

    def outer_copy(i, src):
        peer = lax.rem(q + 1 + i, g)
        return pltpu.make_async_remote_copy(
            src_ref=part.at[peer], dst_ref=stage1.at[src], send_sem=out_send.at[i],
            recv_sem=out_recv.at[src], device_id=dev(c, peer, w), device_id_type=MESH_ID)

    def inner_copy(i, src):
        peer = lax.rem(w + 1 + i, g)
        return pltpu.make_async_remote_copy(
            src_ref=mid.at[peer], dst_ref=stage2.at[src], send_sem=in_send.at[i],
            recv_sem=in_recv.at[src], device_id=dev(c, q, peer), device_id_type=MESH_ID)

    def start_outer(i, carry):
        outer_copy(i, q).start()
        return carry

    lax.fori_loop(0, g - 1, start_outer, 0)

    def wait_outer(i, carry):
        outer_copy(i, q).wait_send()
        outer_copy(i, lax.rem(q + 2 * g - 1 - i, g)).wait_recv()
        return carry

    lax.fori_loop(0, g - 1, wait_outer, 0)
    own1.wait()
    mid[...] = jnp.sum(stage1[...], axis=0)[:, None, :]
    own2 = pltpu.make_async_copy(mid.at[w], stage2.at[w], local_sem.at[1])
    own2.start()

    def start_inner(i, carry):
        inner_copy(i, w).start()
        return carry

    lax.fori_loop(0, g - 1, start_inner, 0)

    def wait_inner(i, carry):
        inner_copy(i, w).wait_send()
        inner_copy(i, lax.rem(w + 2 * g - 1 - i, g)).wait_recv()
        return carry

    lax.fori_loop(0, g - 1, wait_inner, 0)
    own2.wait()
    total_out[...] = jnp.sum(stage2[...], axis=0)


def scatter_all(part, g):
    dma = pltpu.SemaphoreType.DMA
    vmem = pl.BlockSpec(memory_space=pltpu.VMEM)
    width = part.shape[-1]
    return pl.pallas_call(
        functools.partial(scatter_kernel, g),
        out_shape=jax.ShapeDtypeStruct((1, width), part.dtype),
        in_specs=[vmem],
        out_specs=vmem,
        scratch_shapes=[
            pltpu.VMEM((g, g, width), jnp.float32),
            pltpu.VMEM((g, 1, width), jnp.float32),
            pltpu.VMEM((g, 1, width), jnp.float32),
            dma((g,)), dma((g,)), dma((g,)), dma((g,)), dma((2,)),
        ],
        compiler_params=pltpu.CompilerParams(has_side_effects=True, collective_id=1),
    )(part)


def matern_sums(neg_two_rows, row_sq, col_points, col_coef):
    col_sq = jnp.sum(jnp.square(col_points.astype(jnp.float32)), axis=1)
    neg_two_dot = lax.dot_general(
        neg_two_rows, col_points, (((1,), (1,)), ((), ())), preferred_element_type=jnp.float32
    )
    sq = (row_sq[:, None] + col_sq[None, :]) + neg_two_dot
    distance = jnp.where(sq > 0.0, sq * lax.rsqrt(sq), 0.0)
    m = distance * (-KERNEL_RATE)
    kernel_tile = (1.0 - m) * jnp.exp(m)
    return jnp.sum(kernel_tile * col_coef[None, :], axis=1)


def column_sums(row_feats, piece_points, every_coef):
    row_sq = jnp.sum(jnp.square(row_feats.astype(jnp.float32)), axis=1)
    neg_two_rows = row_feats * jnp.asarray(-2.0, row_feats.dtype)
    zeros_init = jnp.zeros((row_feats.shape[0],), jnp.float32)
    piece_len = piece_points.shape[0]
    block_len = math.gcd(piece_len, 2048)
    point_blocks = piece_points.reshape(-1, block_len, piece_points.shape[1])
    coef_blocks = every_coef.reshape(-1, block_len)

    def advance(partial_sum, column_block):
        return (
            partial_sum + matern_sums(neg_two_rows, row_sq, column_block[0], column_block[1]),
            None,
        )

    result, unused = lax.scan(advance, zeros_init, (point_blocks, coef_blocks))
    return result


def per_device(n_blk, n_str, points, coefficients, velocity, targets, batch_rows, counts):
    preview = coefficients + MOMENTUM * velocity
    slot_total = batch_rows.shape[0]
    local_size = points.shape[0]
    slot_ids = jnp.arange(slot_total, dtype=jnp.int32)
    count_here = counts.reshape((1,))
    in_count = slot_ids < count_here[0]
    picked = jnp.take(points, batch_rows, axis=0)
    g = 8
    lanes = 128
    dense = lambda a: a.reshape(-1, lanes)
    rows_all, pts_all, prev_all = gather_all(
        dense(picked), dense(points), preview.reshape(1, -1), g)
    group_rows = rows_all.reshape(-1, points.shape[1])
    piece_points = pts_all.reshape(-1, points.shape[1])
    every_coef = prev_all.reshape(-1)
    partial_value = column_sums(group_rows, piece_points, every_coef)
    kernel_rows = scatter_all(partial_value.reshape(g, g, slot_total), g).reshape(-1)
    residual = jnp.where(
        in_count,
        kernel_rows + NOISE_VAR * jnp.take(preview, batch_rows) - jnp.take(targets, batch_rows),
        0.0,
    )
    scatter_rows = (batch_rows[:, None] == jnp.arange(local_size, dtype=jnp.int32)[None, :]).astype(
        jnp.float32
    )
    update_sum = jnp.dot(residual, scatter_rows, precision=lax.Precision.HIGHEST)
    new_velocity = MOMENTUM * velocity - STEP_SIZE * update_sum
    new_coefficients = coefficients + new_velocity
    return (new_coefficients, new_velocity)


def solution(mesh):
    n_blk = mesh.shape["blk"]
    n_str = mesh.shape["stripe"]
    in_specs = (
        P(("blk", "stripe"), None),
        P(("blk", "stripe")),
        P(("blk", "stripe")),
        P(("blk", "stripe")),
        P(("blk", "stripe")),
        P("blk", "stripe"),
    )
    out_specs = (P(("blk", "stripe")), P(("blk", "stripe")))
    return jax.shard_map(
        functools.partial(per_device, n_blk, n_str), mesh=mesh, in_specs=in_specs,
        out_specs=out_specs, check_vma=False
    )
```

```python
import functools
import math

import jax
import jax.numpy as jnp
from jax import lax
from jax.experimental import pallas as pl
from jax.experimental.pallas import tpu as pltpu
from jax.sharding import PartitionSpec as P

MOMENTUM = 0.9
STEP_SIZE = 1.0
NOISE_VAR = 8.0
KERNEL_RATE = 3.0**0.5 / 6.0

MESH_ID = pl.DeviceIdType.MESH
ANY = pl.BlockSpec(memory_space=pl.ANY)


def coords():
    b = lax.axis_index("blk")
    s = lax.axis_index("stripe")
    core = lax.rem(s, 2)
    z_hi = lax.rem(s // 2, 2)
    x = lax.rem(s // 4, 4)
    y = s // 16
    c = lax.rem(b, 2) * 4 + lax.rem(x, 2) * 2 + core
    q = y * 2 + x // 2
    w = (b // 2) * 2 + z_hi
    return c, q, w


def dev(c, q, w):
    b = (w // 2) * 2 + c // 4
    z_hi = lax.rem(w, 2)
    y = q // 2
    x = lax.rem(q, 2) * 2 + lax.rem(c // 2, 2)
    core = lax.rem(c, 2)
    return (b, ((y * 4 + x) * 2 + z_hi) * 2 + core)


def greet_all(barrier, peers_of, n, total):
    def greet(i, carry):
        pl.semaphore_signal(barrier, 1, device_id=peers_of(i), device_id_type=MESH_ID)
        return carry

    lax.fori_loop(0, n, greet, 0)
    return total + n


def gather_kernel(g, picked, pts, prev, rows_out, pts_out, prev_out,
                  in_send, in_recv, out_send, out_recv, pt_send, pt_recv, pv_send, pv_recv,
                  local_sem):
    c, q, w = coords()
    barrier = pltpu.get_barrier_semaphore()
    n = greet_all(barrier, lambda i: dev(c, q, lax.rem(w + 1 + i, g)), g - 1, 0)
    n = greet_all(barrier, lambda i: dev(c, lax.rem(q + 1 + i, g), w), g - 1, n)
    n = greet_all(barrier, lambda i: dev(lax.rem(c + 1 + i, g), q, w), g - 1, n)
    pl.semaphore_wait(barrier, n)
    own = [
        pltpu.make_async_copy(picked, rows_out.at[q, w], local_sem.at[0]),
        pltpu.make_async_copy(pts, pts_out.at[c], local_sem.at[1]),
        pltpu.make_async_copy(prev, prev_out.at[c], local_sem.at[2]),
    ]
    for cp in own:
        cp.start()

    def inner_copy(i, src):
        return pltpu.make_async_remote_copy(
            src_ref=picked, dst_ref=rows_out.at[q, src], send_sem=in_send.at[i],
            recv_sem=in_recv.at[src], device_id=dev(c, q, lax.rem(w + 1 + i, g)),
            device_id_type=MESH_ID)

    def outer_copy(i, src):
        return pltpu.make_async_remote_copy(
            src_ref=rows_out.at[q], dst_ref=rows_out.at[src], send_sem=out_send.at[i],
            recv_sem=out_recv.at[src], device_id=dev(c, lax.rem(q + 1 + i, g), w),
            device_id_type=MESH_ID)

    def group_copies(i, src):
        peer = dev(lax.rem(c + 1 + i, g), q, w)
        return (
            pltpu.make_async_remote_copy(
                src_ref=pts, dst_ref=pts_out.at[src], send_sem=pt_send.at[i],
                recv_sem=pt_recv.at[src], device_id=peer, device_id_type=MESH_ID),
            pltpu.make_async_remote_copy(
                src_ref=prev, dst_ref=prev_out.at[src], send_sem=pv_send.at[i],
                recv_sem=pv_recv.at[src], device_id=peer, device_id_type=MESH_ID),
        )

    def start_inner(i, carry):
        inner_copy(i, w).start()
        return carry

    def start_group(i, carry):
        for cp in group_copies(i, c):
            cp.start()
        return carry

    lax.fori_loop(0, g - 1, start_inner, 0)
    lax.fori_loop(0, g - 1, start_group, 0)

    def wait_inner(i, carry):
        inner_copy(i, w).wait_send()
        inner_copy(i, lax.rem(w + 2 * g - 1 - i, g)).wait_recv()
        return carry

    lax.fori_loop(0, g - 1, wait_inner, 0)
    own[0].wait()

    def start_outer(i, carry):
        outer_copy(i, q).start()
        return carry

    lax.fori_loop(0, g - 1, start_outer, 0)

    def wait_group(i, carry):
        for cp in group_copies(i, c):
            cp.wait_send()
        for cp in group_copies(i, lax.rem(c + 2 * g - 1 - i, g)):
            cp.wait_recv()
        return carry

    def wait_outer(i, carry):
        outer_copy(i, q).wait_send()
        outer_copy(i, lax.rem(q + 2 * g - 1 - i, g)).wait_recv()
        return carry

    lax.fori_loop(0, g - 1, wait_group, 0)
    lax.fori_loop(0, g - 1, wait_outer, 0)
    own[1].wait()
    own[2].wait()


def gather_all(picked, pts, prev, g):
    dma = pltpu.SemaphoreType.DMA
    return pl.pallas_call(
        functools.partial(gather_kernel, g),
        out_shape=(
            jax.ShapeDtypeStruct((g, g) + picked.shape, picked.dtype),
            jax.ShapeDtypeStruct((g,) + pts.shape, pts.dtype),
            jax.ShapeDtypeStruct((g,) + prev.shape, prev.dtype),
        ),
        in_specs=[ANY, ANY, ANY],
        out_specs=(ANY, ANY, ANY),
        scratch_shapes=[dma((g,)) for _ in range(8)] + [dma((3,))],
        compiler_params=pltpu.CompilerParams(has_side_effects=True, collective_id=0),
    )(picked, pts, prev)


def scatter_kernel(g, part, total_out, stage1, mid, stage2,
                   out_send, out_recv, in_send, in_recv, local_sem):
    c, q, w = coords()
    barrier = pltpu.get_barrier_semaphore()
    n = greet_all(barrier, lambda i: dev(c, q, lax.rem(w + 1 + i, g)), g - 1, 0)
    n = greet_all(barrier, lambda i: dev(c, lax.rem(q + 1 + i, g), w), g - 1, n)
    pl.semaphore_wait(barrier, n)
    own1 = pltpu.make_async_copy(part.at[q], stage1.at[q], local_sem.at[0])
    own1.start()

    def outer_copy(i, src):
        peer = lax.rem(q + 1 + i, g)
        return pltpu.make_async_remote_copy(
            src_ref=part.at[peer], dst_ref=stage1.at[src], send_sem=out_send.at[i],
            recv_sem=out_recv.at[src], device_id=dev(c, peer, w), device_id_type=MESH_ID)

    def inner_copy(i, src):
        peer = lax.rem(w + 1 + i, g)
        return pltpu.make_async_remote_copy(
            src_ref=mid.at[peer], dst_ref=stage2.at[src], send_sem=in_send.at[i],
            recv_sem=in_recv.at[src], device_id=dev(c, q, peer), device_id_type=MESH_ID)

    def start_outer(i, carry):
        outer_copy(i, q).start()
        return carry

    lax.fori_loop(0, g - 1, start_outer, 0)

    def wait_outer(i, carry):
        outer_copy(i, q).wait_send()
        outer_copy(i, lax.rem(q + 2 * g - 1 - i, g)).wait_recv()
        return carry

    lax.fori_loop(0, g - 1, wait_outer, 0)
    own1.wait()
    mid[...] = jnp.sum(stage1[...], axis=0)[:, None, :]
    own2 = pltpu.make_async_copy(mid.at[w], stage2.at[w], local_sem.at[1])
    own2.start()

    def start_inner(i, carry):
        inner_copy(i, w).start()
        return carry

    lax.fori_loop(0, g - 1, start_inner, 0)

    def wait_inner(i, carry):
        inner_copy(i, w).wait_send()
        inner_copy(i, lax.rem(w + 2 * g - 1 - i, g)).wait_recv()
        return carry

    lax.fori_loop(0, g - 1, wait_inner, 0)
    own2.wait()
    total_out[...] = jnp.sum(stage2[...], axis=0)


def scatter_all(part, g):
    dma = pltpu.SemaphoreType.DMA
    vmem = pl.BlockSpec(memory_space=pltpu.VMEM)
    width = part.shape[-1]
    return pl.pallas_call(
        functools.partial(scatter_kernel, g),
        out_shape=jax.ShapeDtypeStruct((1, width), part.dtype),
        in_specs=[vmem],
        out_specs=vmem,
        scratch_shapes=[
            pltpu.VMEM((g, g, width), jnp.float32),
            pltpu.VMEM((g, 1, width), jnp.float32),
            pltpu.VMEM((g, 1, width), jnp.float32),
            dma((g,)), dma((g,)), dma((g,)), dma((g,)), dma((2,)),
        ],
        compiler_params=pltpu.CompilerParams(has_side_effects=True, collective_id=1),
    )(part)


def matern_sums(neg_two_rows, row_sq, col_points, col_coef):
    col_sq = jnp.sum(jnp.square(col_points.astype(jnp.float32)), axis=1)
    neg_two_dot = lax.dot_general(
        neg_two_rows, col_points, (((1,), (1,)), ((), ())), preferred_element_type=jnp.float32
    )
    sq = (row_sq[:, None] + col_sq[None, :]) + neg_two_dot
    distance = jnp.where(sq > 0.0, sq * lax.rsqrt(sq), 0.0)
    m = distance * (-KERNEL_RATE)
    kernel_tile = (1.0 - m) * jnp.exp(m)
    return jnp.sum(kernel_tile * col_coef[None, :], axis=1)


def column_sums(row_feats, piece_points, every_coef):
    row_sq = jnp.sum(jnp.square(row_feats.astype(jnp.float32)), axis=1)
    neg_two_rows = row_feats * jnp.asarray(-2.0, row_feats.dtype)
    zeros_init = jnp.zeros((row_feats.shape[0],), jnp.float32)
    piece_len = piece_points.shape[0]
    block_len = math.gcd(piece_len, 2048)
    point_blocks = piece_points.reshape(-1, block_len, piece_points.shape[1])
    coef_blocks = every_coef.reshape(-1, block_len)

    def advance(partial_sum, column_block):
        return (
            partial_sum + matern_sums(neg_two_rows, row_sq, column_block[0], column_block[1]),
            None,
        )

    result, unused = lax.scan(advance, zeros_init, (point_blocks, coef_blocks))
    return result


def per_device(n_blk, n_str, points, coefficients, velocity, targets, batch_rows, counts):
    preview = coefficients + MOMENTUM * velocity
    slot_total = batch_rows.shape[0]
    local_size = points.shape[0]
    picked = points.at[batch_rows].get(mode="promise_in_bounds")
    g = 8
    lanes = 128
    dense = lambda a: a.reshape(-1, lanes)
    rows_all, pts_all, prev_all = gather_all(
        dense(picked), dense(points), preview.reshape(1, -1), g)
    rows_all, batch_rows, counts = lax.optimization_barrier((rows_all, batch_rows, counts))
    slot_ids = jnp.arange(slot_total, dtype=jnp.int32)
    count_here = counts.reshape((1,))
    in_count = slot_ids < count_here[0]
    group_rows = rows_all.reshape(-1, points.shape[1])
    piece_points = pts_all.reshape(-1, points.shape[1])
    every_coef = prev_all.reshape(-1)
    partial_value = column_sums(group_rows, piece_points, every_coef)
    kernel_rows = scatter_all(partial_value.reshape(g, g, slot_total), g).reshape(-1)
    residual = jnp.where(
        in_count,
        kernel_rows + NOISE_VAR * preview.at[batch_rows].get(mode="promise_in_bounds") - targets.at[batch_rows].get(mode="promise_in_bounds"),
        0.0,
    )
    scatter_rows = (batch_rows[:, None] == jnp.arange(local_size, dtype=jnp.int32)[None, :]).astype(
        jnp.float32
    )
    update_sum = jnp.dot(residual, scatter_rows, precision=lax.Precision.HIGHEST)
    new_velocity = MOMENTUM * velocity - STEP_SIZE * update_sum
    new_coefficients = coefficients + new_velocity
    return (new_coefficients, new_velocity)


def solution(mesh):
    n_blk = mesh.shape["blk"]
    n_str = mesh.shape["stripe"]
    in_specs = (
        P(("blk", "stripe"), None),
        P(("blk", "stripe")),
        P(("blk", "stripe")),
        P(("blk", "stripe")),
        P(("blk", "stripe")),
        P("blk", "stripe"),
    )
    out_specs = (P(("blk", "stripe")), P(("blk", "stripe")))
    return jax.shard_map(
        functools.partial(per_device, n_blk, n_str), mesh=mesh, in_specs=in_specs,
        out_specs=out_specs, check_vma=False
    )
```

```python
import functools
import math

import jax
import jax.numpy as jnp
from jax import lax
from jax.experimental import pallas as pl
from jax.experimental.pallas import tpu as pltpu
from jax.sharding import PartitionSpec as P

MOMENTUM = 0.9
STEP_SIZE = 1.0
NOISE_VAR = 8.0
KERNEL_RATE = 3.0**0.5 / 6.0

MESH_ID = pl.DeviceIdType.MESH
ANY = pl.BlockSpec(memory_space=pl.ANY)


def coords():
    b = lax.axis_index("blk")
    s = lax.axis_index("stripe")
    core = lax.rem(s, 2)
    z_hi = lax.rem(s // 2, 2)
    x = lax.rem(s // 4, 4)
    y = s // 16
    c = lax.rem(b, 2) * 4 + lax.rem(x, 2) * 2 + core
    q = y * 2 + x // 2
    w = (b // 2) * 2 + z_hi
    return c, q, w


def dev(c, q, w):
    b = (w // 2) * 2 + c // 4
    z_hi = lax.rem(w, 2)
    y = q // 2
    x = lax.rem(q, 2) * 2 + lax.rem(c // 2, 2)
    core = lax.rem(c, 2)
    return (b, ((y * 4 + x) * 2 + z_hi) * 2 + core)


def greet_all(barrier, peers_of, n, total):
    def greet(i, carry):
        pl.semaphore_signal(barrier, 1, device_id=peers_of(i), device_id_type=MESH_ID)
        return carry

    lax.fori_loop(0, n, greet, 0)
    return total + n


def gather_kernel(g, picked, pts, rows_out, pts_out,
                  in_send, in_recv, out_send, out_recv, pt_send, pt_recv, local_sem):
    c, q, w = coords()
    barrier = pltpu.get_barrier_semaphore()
    n = greet_all(barrier, lambda i: dev(c, q, lax.rem(w + 1 + i, g)), g - 1, 0)
    n = greet_all(barrier, lambda i: dev(c, lax.rem(q + 1 + i, g), w), g - 1, n)
    n = greet_all(barrier, lambda i: dev(lax.rem(c + 1 + i, g), q, w), g - 1, n)
    pl.semaphore_wait(barrier, n)
    own = [
        pltpu.make_async_copy(picked, rows_out.at[q, w], local_sem.at[0]),
        pltpu.make_async_copy(pts, pts_out.at[c], local_sem.at[1]),
    ]
    for cp in own:
        cp.start()

    def inner_copy(i, src):
        return pltpu.make_async_remote_copy(
            src_ref=picked, dst_ref=rows_out.at[q, src], send_sem=in_send.at[i],
            recv_sem=in_recv.at[src], device_id=dev(c, q, lax.rem(w + 1 + i, g)),
            device_id_type=MESH_ID)

    def outer_copy(i, src):
        return pltpu.make_async_remote_copy(
            src_ref=rows_out.at[q], dst_ref=rows_out.at[src], send_sem=out_send.at[i],
            recv_sem=out_recv.at[src], device_id=dev(c, lax.rem(q + 1 + i, g), w),
            device_id_type=MESH_ID)

    def group_copies(i, src):
        peer = dev(lax.rem(c + 1 + i, g), q, w)
        return (
            pltpu.make_async_remote_copy(
                src_ref=pts, dst_ref=pts_out.at[src], send_sem=pt_send.at[i],
                recv_sem=pt_recv.at[src], device_id=peer, device_id_type=MESH_ID),
        )

    def start_inner(i, carry):
        inner_copy(i, w).start()
        return carry

    def start_group(i, carry):
        for cp in group_copies(i, c):
            cp.start()
        return carry

    lax.fori_loop(0, g - 1, start_inner, 0)
    lax.fori_loop(0, g - 1, start_group, 0)

    def wait_inner(i, carry):
        inner_copy(i, w).wait_send()
        inner_copy(i, lax.rem(w + 2 * g - 1 - i, g)).wait_recv()
        return carry

    lax.fori_loop(0, g - 1, wait_inner, 0)
    own[0].wait()

    def start_outer(i, carry):
        outer_copy(i, q).start()
        return carry

    lax.fori_loop(0, g - 1, start_outer, 0)

    def wait_group(i, carry):
        for cp in group_copies(i, c):
            cp.wait_send()
        for cp in group_copies(i, lax.rem(c + 2 * g - 1 - i, g)):
            cp.wait_recv()
        return carry

    def wait_outer(i, carry):
        outer_copy(i, q).wait_send()
        outer_copy(i, lax.rem(q + 2 * g - 1 - i, g)).wait_recv()
        return carry

    lax.fori_loop(0, g - 1, wait_group, 0)
    lax.fori_loop(0, g - 1, wait_outer, 0)
    own[1].wait()


def gather_all(picked, pts, g):
    dma = pltpu.SemaphoreType.DMA
    return pl.pallas_call(
        functools.partial(gather_kernel, g),
        out_shape=(
            jax.ShapeDtypeStruct((g, g) + picked.shape, picked.dtype),
            jax.ShapeDtypeStruct((g,) + pts.shape, pts.dtype),
        ),
        in_specs=[ANY, ANY],
        out_specs=(ANY, ANY),
        scratch_shapes=[dma((g,)) for _ in range(6)] + [dma((2,))],
        compiler_params=pltpu.CompilerParams(has_side_effects=True, collective_id=0),
    )(picked, pts)


def split3(v):
    hi = lax.reduce_precision(v, exponent_bits=8, mantissa_bits=7)
    rest = v - hi
    mid = lax.reduce_precision(rest, exponent_bits=8, mantissa_bits=7)
    lo = rest - mid
    return jnp.stack([hi, mid, lo]).astype(jnp.bfloat16)


def scatter_kernel(g, part, total_out, stage1, mid, stage2,
                   out_send, out_recv, in_send, in_recv, local_sem):
    c, q, w = coords()
    barrier = pltpu.get_barrier_semaphore()
    n = greet_all(barrier, lambda i: dev(c, q, lax.rem(w + 1 + i, g)), g - 1, 0)
    n = greet_all(barrier, lambda i: dev(c, lax.rem(q + 1 + i, g), w), g - 1, n)
    pl.semaphore_wait(barrier, n)
    own1 = pltpu.make_async_copy(part.at[q], stage1.at[q], local_sem.at[0])
    own1.start()

    def outer_copy(i, src):
        peer = lax.rem(q + 1 + i, g)
        return pltpu.make_async_remote_copy(
            src_ref=part.at[peer], dst_ref=stage1.at[src], send_sem=out_send.at[i],
            recv_sem=out_recv.at[src], device_id=dev(c, peer, w), device_id_type=MESH_ID)

    def inner_copy(i, src):
        peer = lax.rem(w + 1 + i, g)
        return pltpu.make_async_remote_copy(
            src_ref=mid.at[peer], dst_ref=stage2.at[src], send_sem=in_send.at[i],
            recv_sem=in_recv.at[src], device_id=dev(c, q, peer), device_id_type=MESH_ID)

    def start_outer(i, carry):
        outer_copy(i, q).start()
        return carry

    lax.fori_loop(0, g - 1, start_outer, 0)

    def wait_outer(i, carry):
        outer_copy(i, q).wait_send()
        outer_copy(i, lax.rem(q + 2 * g - 1 - i, g)).wait_recv()
        return carry

    lax.fori_loop(0, g - 1, wait_outer, 0)
    own1.wait()
    mid[...] = jnp.sum(stage1[...], axis=0)[:, None, :]
    own2 = pltpu.make_async_copy(mid.at[w], stage2.at[w], local_sem.at[1])
    own2.start()

    def start_inner(i, carry):
        inner_copy(i, w).start()
        return carry

    lax.fori_loop(0, g - 1, start_inner, 0)

    def wait_inner(i, carry):
        inner_copy(i, w).wait_send()
        inner_copy(i, lax.rem(w + 2 * g - 1 - i, g)).wait_recv()
        return carry

    lax.fori_loop(0, g - 1, wait_inner, 0)
    own2.wait()
    total_out[...] = jnp.sum(stage2[...], axis=0)


def scatter_all(part, g):
    dma = pltpu.SemaphoreType.DMA
    vmem = pl.BlockSpec(memory_space=pltpu.VMEM)
    width = part.shape[-1]
    return pl.pallas_call(
        functools.partial(scatter_kernel, g),
        out_shape=jax.ShapeDtypeStruct((1, width), part.dtype),
        in_specs=[vmem],
        out_specs=vmem,
        scratch_shapes=[
            pltpu.VMEM((g, g, width), jnp.float32),
            pltpu.VMEM((g, 1, width), jnp.float32),
            pltpu.VMEM((g, 1, width), jnp.float32),
            dma((g,)), dma((g,)), dma((g,)), dma((g,)), dma((2,)),
        ],
        compiler_params=pltpu.CompilerParams(has_side_effects=True, collective_id=1),
    )(part)


def matern_sums(neg_two_rows, row_sq, col_points, col_coef):
    col_sq = jnp.sum(jnp.square(col_points.astype(jnp.float32)), axis=1)
    neg_two_dot = lax.dot_general(
        neg_two_rows, col_points, (((1,), (1,)), ((), ())), preferred_element_type=jnp.float32
    )
    sq = (row_sq[:, None] + col_sq[None, :]) + neg_two_dot
    distance = jnp.where(sq > 0.0, sq * lax.rsqrt(sq), 0.0)
    m = distance * (-KERNEL_RATE)
    kernel_tile = (1.0 - m) * jnp.exp(m)
    return jnp.sum(kernel_tile * col_coef[None, :], axis=1)


def column_sums(row_feats, piece_points, every_coef):
    row_sq = jnp.sum(jnp.square(row_feats.astype(jnp.float32)), axis=1)
    neg_two_rows = row_feats * jnp.asarray(-2.0, row_feats.dtype)
    zeros_init = jnp.zeros((row_feats.shape[0],), jnp.float32)
    piece_len = piece_points.shape[0]
    block_len = math.gcd(piece_len, 2048)
    point_blocks = piece_points.reshape(-1, block_len, piece_points.shape[1])
    coef_blocks = every_coef.reshape(-1, block_len)

    def advance(partial_sum, column_block):
        return (
            partial_sum + matern_sums(neg_two_rows, row_sq, column_block[0], column_block[1]),
            None,
        )

    result, unused = lax.scan(advance, zeros_init, (point_blocks, coef_blocks))
    return result


def per_device(n_blk, n_str, points, coefficients, velocity, targets, batch_rows, counts):
    preview = coefficients + MOMENTUM * velocity
    slot_total = batch_rows.shape[0]
    local_size = points.shape[0]
    picked = points.at[batch_rows].get(mode="promise_in_bounds")
    g = 8
    lanes = 128
    dense = lambda a: a.reshape(-1, lanes)
    pt_rows = points.size // lanes
    pieces = split3(preview).reshape(-1, lanes)
    pad = (-(pt_rows + pieces.shape[0])) % 16
    block = jnp.concatenate(
        [dense(points), pieces, jnp.zeros((pad, lanes), points.dtype)], axis=0)
    rows_all, pts_all = gather_all(dense(picked), block, g)
    rows_all, batch_rows, counts = lax.optimization_barrier((rows_all, batch_rows, counts))
    prev_all = pts_all[:, pt_rows:pt_rows + pieces.shape[0], :].astype(jnp.float32)
    prev_all = prev_all.reshape(g, 3, -1)
    prev_all = (prev_all[:, 0] + prev_all[:, 1]) + prev_all[:, 2]
    pts_all = pts_all[:, :pt_rows, :]
    adjust = NOISE_VAR * preview - targets
    slot_ids = jnp.arange(slot_total, dtype=jnp.int32)
    count_here = counts.reshape((1,))
    in_count = slot_ids < count_here[0]
    group_rows = rows_all.reshape(-1, points.shape[1])
    piece_points = pts_all.reshape(-1, points.shape[1])
    every_coef = prev_all.reshape(-1)
    partial_value = column_sums(group_rows, piece_points, every_coef)
    kernel_rows = scatter_all(partial_value.reshape(g, g, slot_total), g).reshape(-1)
    residual = jnp.where(
        in_count,
        kernel_rows + adjust.at[batch_rows].get(mode="promise_in_bounds"),
        0.0,
    )
    scatter_rows = (batch_rows[:, None] == jnp.arange(local_size, dtype=jnp.int32)[None, :]).astype(
        jnp.float32
    )
    update_sum = jnp.dot(residual, scatter_rows, precision=lax.Precision.HIGHEST)
    new_velocity = MOMENTUM * velocity - STEP_SIZE * update_sum
    new_coefficients = coefficients + new_velocity
    return (new_coefficients, new_velocity)


def solution(mesh):
    n_blk = mesh.shape["blk"]
    n_str = mesh.shape["stripe"]
    in_specs = (
        P(("blk", "stripe"), None),
        P(("blk", "stripe")),
        P(("blk", "stripe")),
        P(("blk", "stripe")),
        P(("blk", "stripe")),
        P("blk", "stripe"),
    )
    out_specs = (P(("blk", "stripe")), P(("blk", "stripe")))
    return jax.shard_map(
        functools.partial(per_device, n_blk, n_str), mesh=mesh, in_specs=in_specs,
        out_specs=out_specs, check_vma=False
    )
```

```python
import functools
import math

import jax
import jax.numpy as jnp
from jax import lax
from jax.experimental import pallas as pl
from jax.experimental.pallas import tpu as pltpu
from jax.sharding import PartitionSpec as P

MOMENTUM = 0.9
STEP_SIZE = 1.0
NOISE_VAR = 8.0
KERNEL_RATE = 3.0**0.5 / 6.0

MESH_ID = pl.DeviceIdType.MESH
ANY = pl.BlockSpec(memory_space=pl.ANY)


def coords():
    b = lax.axis_index("blk")
    s = lax.axis_index("stripe")
    core = lax.rem(s, 2)
    z_hi = lax.rem(s // 2, 2)
    x = lax.rem(s // 4, 4)
    y = s // 16
    c = lax.rem(b, 2) * 4 + lax.rem(x, 2) * 2 + core
    q = y * 2 + x // 2
    w = (b // 2) * 2 + z_hi
    return c, q, w


def dev(c, q, w):
    b = (w // 2) * 2 + c // 4
    z_hi = lax.rem(w, 2)
    y = q // 2
    x = lax.rem(q, 2) * 2 + lax.rem(c // 2, 2)
    core = lax.rem(c, 2)
    return (b, ((y * 4 + x) * 2 + z_hi) * 2 + core)


def greet_all(barrier, peers_of, n, total):
    def greet(i, carry):
        pl.semaphore_signal(barrier, 1, device_id=peers_of(i), device_id_type=MESH_ID)
        return carry

    lax.fori_loop(0, n, greet, 0)
    return total + n


def gather_kernel(g, picked, pts, prev, rows_out, pts_out, prev_out,
                  in_send, in_recv, out_send, out_recv, pt_send, pt_recv, pv_send, pv_recv,
                  local_sem):
    c, q, w = coords()
    barrier = pltpu.get_barrier_semaphore()
    n = greet_all(barrier, lambda i: dev(c, q, lax.rem(w + 1 + i, g)), g - 1, 0)
    n = greet_all(barrier, lambda i: dev(c, lax.rem(q + 1 + i, g), w), g - 1, n)
    n = greet_all(barrier, lambda i: dev(lax.rem(c + 1 + i, g), q, w), g - 1, n)
    pl.semaphore_wait(barrier, n)
    own = [
        pltpu.make_async_copy(picked, rows_out.at[q, w], local_sem.at[0]),
        pltpu.make_async_copy(pts, pts_out.at[c], local_sem.at[1]),
        pltpu.make_async_copy(prev, prev_out.at[c], local_sem.at[2]),
    ]
    for cp in own:
        cp.start()

    def inner_copy(i, src):
        return pltpu.make_async_remote_copy(
            src_ref=picked, dst_ref=rows_out.at[q, src], send_sem=in_send.at[i],
            recv_sem=in_recv.at[src], device_id=dev(c, q, lax.rem(w + 1 + i, g)),
            device_id_type=MESH_ID)

    def outer_copy(i, src):
        return pltpu.make_async_remote_copy(
            src_ref=rows_out.at[q], dst_ref=rows_out.at[src], send_sem=out_send.at[i],
            recv_sem=out_recv.at[src], device_id=dev(c, lax.rem(q + 1 + i, g), w),
            device_id_type=MESH_ID)

    def group_copies(i, src):
        peer = dev(lax.rem(c + 1 + i, g), q, w)
        return (
            pltpu.make_async_remote_copy(
                src_ref=pts, dst_ref=pts_out.at[src], send_sem=pt_send.at[i],
                recv_sem=pt_recv.at[src], device_id=peer, device_id_type=MESH_ID),
            pltpu.make_async_remote_copy(
                src_ref=prev, dst_ref=prev_out.at[src], send_sem=pv_send.at[i],
                recv_sem=pv_recv.at[src], device_id=peer, device_id_type=MESH_ID),
        )

    def start_inner(i, carry):
        inner_copy(i, w).start()
        return carry

    def start_group(i, carry):
        for cp in group_copies(i, c):
            cp.start()
        return carry

    lax.fori_loop(0, g - 1, start_inner, 0)
    lax.fori_loop(0, g - 1, start_group, 0)

    def wait_inner(i, carry):
        inner_copy(i, w).wait_send()
        inner_copy(i, lax.rem(w + 2 * g - 1 - i, g)).wait_recv()
        return carry

    lax.fori_loop(0, g - 1, wait_inner, 0)
    own[0].wait()

    def start_outer(i, carry):
        outer_copy(i, q).start()
        return carry

    lax.fori_loop(0, g - 1, start_outer, 0)

    def wait_group(i, carry):
        for cp in group_copies(i, c):
            cp.wait_send()
        for cp in group_copies(i, lax.rem(c + 2 * g - 1 - i, g)):
            cp.wait_recv()
        return carry

    def wait_outer(i, carry):
        outer_copy(i, q).wait_send()
        outer_copy(i, lax.rem(q + 2 * g - 1 - i, g)).wait_recv()
        return carry

    lax.fori_loop(0, g - 1, wait_group, 0)
    lax.fori_loop(0, g - 1, wait_outer, 0)
    own[1].wait()
    own[2].wait()


def gather_all(picked, pts, prev, g):
    dma = pltpu.SemaphoreType.DMA
    return pl.pallas_call(
        functools.partial(gather_kernel, g),
        out_shape=(
            jax.ShapeDtypeStruct((g, g) + picked.shape, picked.dtype),
            jax.ShapeDtypeStruct((g,) + pts.shape, pts.dtype),
            jax.ShapeDtypeStruct((g,) + prev.shape, prev.dtype),
        ),
        in_specs=[ANY, ANY, ANY],
        out_specs=(ANY, ANY, ANY),
        scratch_shapes=[dma((g,)) for _ in range(8)] + [dma((3,))],
        compiler_params=pltpu.CompilerParams(has_side_effects=True, collective_id=0),
    )(picked, pts, prev)


def scatter_kernel(g, part, total_out, stage1, mid, stage2,
                   out_send, out_recv, in_send, in_recv, local_sem):
    c, q, w = coords()
    barrier = pltpu.get_barrier_semaphore()
    n = greet_all(barrier, lambda i: dev(c, q, lax.rem(w + 1 + i, g)), g - 1, 0)
    n = greet_all(barrier, lambda i: dev(c, lax.rem(q + 1 + i, g), w), g - 1, n)
    pl.semaphore_wait(barrier, n)
    own1 = pltpu.make_async_copy(part.at[q], stage1.at[q], local_sem.at[0])
    own1.start()

    def outer_copy(i, src):
        peer = lax.rem(q + 1 + i, g)
        return pltpu.make_async_remote_copy(
            src_ref=part.at[peer], dst_ref=stage1.at[src], send_sem=out_send.at[i],
            recv_sem=out_recv.at[src], device_id=dev(c, peer, w), device_id_type=MESH_ID)

    def inner_copy(i, src):
        peer = lax.rem(w + 1 + i, g)
        return pltpu.make_async_remote_copy(
            src_ref=mid.at[peer], dst_ref=stage2.at[src], send_sem=in_send.at[i],
            recv_sem=in_recv.at[src], device_id=dev(c, q, peer), device_id_type=MESH_ID)

    def start_outer(i, carry):
        outer_copy(i, q).start()
        return carry

    lax.fori_loop(0, g - 1, start_outer, 0)

    def wait_outer(i, carry):
        outer_copy(i, q).wait_send()
        outer_copy(i, lax.rem(q + 2 * g - 1 - i, g)).wait_recv()
        return carry

    lax.fori_loop(0, g - 1, wait_outer, 0)
    own1.wait()
    mid[...] = jnp.sum(stage1[...], axis=0)[:, None, :]
    own2 = pltpu.make_async_copy(mid.at[w], stage2.at[w], local_sem.at[1])
    own2.start()

    def start_inner(i, carry):
        inner_copy(i, w).start()
        return carry

    lax.fori_loop(0, g - 1, start_inner, 0)

    def wait_inner(i, carry):
        inner_copy(i, w).wait_send()
        inner_copy(i, lax.rem(w + 2 * g - 1 - i, g)).wait_recv()
        return carry

    lax.fori_loop(0, g - 1, wait_inner, 0)
    own2.wait()
    total_out[...] = jnp.sum(stage2[...], axis=0)


def scatter_all(part, g):
    dma = pltpu.SemaphoreType.DMA
    vmem = pl.BlockSpec(memory_space=pltpu.VMEM)
    width = part.shape[-1]
    return pl.pallas_call(
        functools.partial(scatter_kernel, g),
        out_shape=jax.ShapeDtypeStruct((1, width), part.dtype),
        in_specs=[vmem],
        out_specs=vmem,
        scratch_shapes=[
            pltpu.VMEM((g, g, width), jnp.float32),
            pltpu.VMEM((g, 1, width), jnp.float32),
            pltpu.VMEM((g, 1, width), jnp.float32),
            dma((g,)), dma((g,)), dma((g,)), dma((g,)), dma((2,)),
        ],
        compiler_params=pltpu.CompilerParams(has_side_effects=True, collective_id=1),
    )(part)


def matern_sums(neg_two_rows, row_sq, col_points, col_coef):
    col_sq = jnp.sum(jnp.square(col_points.astype(jnp.float32)), axis=1)
    neg_two_dot = lax.dot_general(
        neg_two_rows, col_points, (((1,), (1,)), ((), ())), preferred_element_type=jnp.float32
    )
    sq = (row_sq[:, None] + col_sq[None, :]) + neg_two_dot
    distance = jnp.where(sq > 0.0, sq * lax.rsqrt(sq), 0.0)
    m = distance * (-KERNEL_RATE)
    kernel_tile = (1.0 - m) * jnp.exp(m)
    return jnp.sum(kernel_tile * col_coef[None, :], axis=1)


def column_sums(row_feats, piece_points, every_coef):
    neg_two_rows = row_feats
    row_sq = 0.25 * jnp.sum(jnp.square(neg_two_rows.astype(jnp.float32)), axis=1)
    zeros_init = jnp.zeros((row_feats.shape[0],), jnp.float32)
    piece_len = piece_points.shape[0]
    block_len = math.gcd(piece_len, 2048)
    point_blocks = piece_points.reshape(-1, block_len, piece_points.shape[1])
    coef_blocks = every_coef.reshape(-1, block_len)

    def advance(partial_sum, column_block):
        return (
            partial_sum + matern_sums(neg_two_rows, row_sq, column_block[0], column_block[1]),
            None,
        )

    result, unused = lax.scan(advance, zeros_init, (point_blocks, coef_blocks))
    return result


def per_device(n_blk, n_str, points, coefficients, velocity, targets, batch_rows, counts):
    preview = coefficients + MOMENTUM * velocity
    slot_total = batch_rows.shape[0]
    local_size = points.shape[0]
    picked = points.at[batch_rows].get(mode="promise_in_bounds") * jnp.asarray(-2.0, points.dtype)
    g = 8
    lanes = 128
    dense = lambda a: a.reshape(-1, lanes)
    rows_all, pts_all, prev_all = gather_all(
        dense(picked), dense(points), preview.reshape(1, -1), g)
    rows_all, batch_rows, counts = lax.optimization_barrier((rows_all, batch_rows, counts))
    slot_ids = jnp.arange(slot_total, dtype=jnp.int32)
    count_here = counts.reshape((1,))
    in_count = slot_ids < count_here[0]
    group_rows = rows_all.reshape(-1, points.shape[1])
    piece_points = pts_all.reshape(-1, points.shape[1])
    every_coef = prev_all.reshape(-1)
    partial_value = column_sums(group_rows, piece_points, every_coef)
    kernel_rows = scatter_all(partial_value.reshape(g, g, slot_total), g).reshape(-1)
    residual = jnp.where(
        in_count,
        kernel_rows + NOISE_VAR * preview.at[batch_rows].get(mode="promise_in_bounds") - targets.at[batch_rows].get(mode="promise_in_bounds"),
        0.0,
    )
    scatter_rows = (batch_rows[:, None] == jnp.arange(local_size, dtype=jnp.int32)[None, :]).astype(
        jnp.float32
    )
    update_sum = jnp.dot(residual, scatter_rows, precision=lax.Precision.HIGHEST)
    new_velocity = MOMENTUM * velocity - STEP_SIZE * update_sum
    new_coefficients = coefficients + new_velocity
    return (new_coefficients, new_velocity)


def solution(mesh):
    n_blk = mesh.shape["blk"]
    n_str = mesh.shape["stripe"]
    in_specs = (
        P(("blk", "stripe"), None),
        P(("blk", "stripe")),
        P(("blk", "stripe")),
        P(("blk", "stripe")),
        P(("blk", "stripe")),
        P("blk", "stripe"),
    )
    out_specs = (P(("blk", "stripe")), P(("blk", "stripe")))
    return jax.shard_map(
        functools.partial(per_device, n_blk, n_str), mesh=mesh, in_specs=in_specs,
        out_specs=out_specs, check_vma=False
    )
```

```python
import functools
import math

import jax
import jax.numpy as jnp
from jax import lax
from jax.experimental import pallas as pl
from jax.experimental.pallas import tpu as pltpu
from jax.sharding import PartitionSpec as P

MOMENTUM = 0.9
STEP_SIZE = 1.0
NOISE_VAR = 8.0
KERNEL_RATE = 3.0**0.5 / 6.0

MESH_ID = pl.DeviceIdType.MESH
ANY = pl.BlockSpec(memory_space=pl.ANY)


def coords():
    b = lax.axis_index("blk")
    s = lax.axis_index("stripe")
    core = lax.rem(s, 2)
    z_hi = lax.rem(s // 2, 2)
    x = lax.rem(s // 4, 4)
    y = s // 16
    c = lax.rem(b, 2) * 4 + lax.rem(x, 2) * 2 + core
    q = y * 2 + x // 2
    w = (b // 2) * 2 + z_hi
    return c, q, w


def dev(c, q, w):
    b = (w // 2) * 2 + c // 4
    z_hi = lax.rem(w, 2)
    y = q // 2
    x = lax.rem(q, 2) * 2 + lax.rem(c // 2, 2)
    core = lax.rem(c, 2)
    return (b, ((y * 4 + x) * 2 + z_hi) * 2 + core)


def greet_all(barrier, peers_of, n, total):
    def greet(i, carry):
        pl.semaphore_signal(barrier, 1, device_id=peers_of(i), device_id_type=MESH_ID)
        return carry

    lax.fori_loop(0, n, greet, 0)
    return total + n


def gather_kernel(g, picked, pts, prev, rows_out, pts_out, prev_out,
                  in_send, in_recv, out_send, out_recv, pt_send, pt_recv, pv_send, pv_recv,
                  local_sem):
    c, q, w = coords()
    barrier = pltpu.get_barrier_semaphore()
    n = greet_all(barrier, lambda i: dev(c, q, lax.rem(w + 1 + i, g)), g - 1, 0)
    n = greet_all(barrier, lambda i: dev(c, lax.rem(q + 1 + i, g), w), g - 1, n)
    n = greet_all(barrier, lambda i: dev(lax.rem(c + 1 + i, g), q, w), g - 1, n)
    pl.semaphore_wait(barrier, n)
    own = [
        pltpu.make_async_copy(picked, rows_out.at[q, w], local_sem.at[0]),
        pltpu.make_async_copy(pts, pts_out.at[c], local_sem.at[1]),
        pltpu.make_async_copy(prev, prev_out.at[c], local_sem.at[2]),
    ]
    for cp in own:
        cp.start()

    def inner_copy(i, src):
        return pltpu.make_async_remote_copy(
            src_ref=picked, dst_ref=rows_out.at[q, src], send_sem=in_send.at[i],
            recv_sem=in_recv.at[src], device_id=dev(c, q, lax.rem(w + 1 + i, g)),
            device_id_type=MESH_ID)

    def outer_copy(i, src):
        return pltpu.make_async_remote_copy(
            src_ref=rows_out.at[q], dst_ref=rows_out.at[src], send_sem=out_send.at[i],
            recv_sem=out_recv.at[src], device_id=dev(c, lax.rem(q + 1 + i, g), w),
            device_id_type=MESH_ID)

    def group_copies(i, src):
        peer = dev(lax.rem(c + 1 + i, g), q, w)
        return (
            pltpu.make_async_remote_copy(
                src_ref=pts, dst_ref=pts_out.at[src], send_sem=pt_send.at[i],
                recv_sem=pt_recv.at[src], device_id=peer, device_id_type=MESH_ID),
            pltpu.make_async_remote_copy(
                src_ref=prev, dst_ref=prev_out.at[src], send_sem=pv_send.at[i],
                recv_sem=pv_recv.at[src], device_id=peer, device_id_type=MESH_ID),
        )

    def start_inner(i, carry):
        inner_copy(i, w).start()
        return carry

    def start_group(i, carry):
        for cp in group_copies(i, c):
            cp.start()
        return carry

    lax.fori_loop(0, g - 1, start_inner, 0)
    lax.fori_loop(0, g - 1, start_group, 0)

    def wait_inner(i, carry):
        inner_copy(i, w).wait_send()
        inner_copy(i, lax.rem(w + 2 * g - 1 - i, g)).wait_recv()
        return carry

    lax.fori_loop(0, g - 1, wait_inner, 0)
    own[0].wait()

    def start_outer(i, carry):
        outer_copy(i, q).start()
        return carry

    lax.fori_loop(0, g - 1, start_outer, 0)

    def wait_group(i, carry):
        for cp in group_copies(i, c):
            cp.wait_send()
        for cp in group_copies(i, lax.rem(c + 2 * g - 1 - i, g)):
            cp.wait_recv()
        return carry

    def wait_outer(i, carry):
        outer_copy(i, q).wait_send()
        outer_copy(i, lax.rem(q + 2 * g - 1 - i, g)).wait_recv()
        return carry

    lax.fori_loop(0, g - 1, wait_group, 0)
    lax.fori_loop(0, g - 1, wait_outer, 0)
    own[1].wait()
    own[2].wait()


def gather_all(picked, pts, prev, g):
    dma = pltpu.SemaphoreType.DMA
    return pl.pallas_call(
        functools.partial(gather_kernel, g),
        out_shape=(
            jax.ShapeDtypeStruct((g, g) + picked.shape, picked.dtype),
            jax.ShapeDtypeStruct((g,) + pts.shape, pts.dtype),
            jax.ShapeDtypeStruct((g,) + prev.shape, prev.dtype),
        ),
        in_specs=[ANY, ANY, ANY],
        out_specs=(ANY, ANY, ANY),
        scratch_shapes=[dma((g,)) for _ in range(8)] + [dma((3,))],
        compiler_params=pltpu.CompilerParams(has_side_effects=True, collective_id=0),
    )(picked, pts, prev)


def scatter_kernel(g, part, total_out, stage1, mid, stage2,
                   out_send, out_recv, in_send, in_recv, local_sem):
    c, q, w = coords()
    barrier = pltpu.get_barrier_semaphore()
    n = greet_all(barrier, lambda i: dev(c, q, lax.rem(w + 1 + i, g)), g - 1, 0)
    n = greet_all(barrier, lambda i: dev(c, lax.rem(q + 1 + i, g), w), g - 1, n)
    pl.semaphore_wait(barrier, n)
    own1 = pltpu.make_async_copy(part.at[q], stage1.at[q], local_sem.at[0])
    own1.start()

    def outer_copy(i, src):
        peer = lax.rem(q + 1 + i, g)
        return pltpu.make_async_remote_copy(
            src_ref=part.at[peer], dst_ref=stage1.at[src], send_sem=out_send.at[i],
            recv_sem=out_recv.at[src], device_id=dev(c, peer, w), device_id_type=MESH_ID)

    def inner_copy(i, src):
        peer = lax.rem(w + 1 + i, g)
        return pltpu.make_async_remote_copy(
            src_ref=mid.at[peer], dst_ref=stage2.at[src], send_sem=in_send.at[i],
            recv_sem=in_recv.at[src], device_id=dev(c, q, peer), device_id_type=MESH_ID)

    def start_outer(i, carry):
        outer_copy(i, q).start()
        return carry

    lax.fori_loop(0, g - 1, start_outer, 0)

    def wait_outer(i, carry):
        outer_copy(i, q).wait_send()
        outer_copy(i, lax.rem(q + 2 * g - 1 - i, g)).wait_recv()
        return carry

    lax.fori_loop(0, g - 1, wait_outer, 0)
    own1.wait()
    mid[...] = jnp.sum(stage1[...], axis=0)[:, None, :]
    own2 = pltpu.make_async_copy(mid.at[w], stage2.at[w], local_sem.at[1])
    own2.start()

    def start_inner(i, carry):
        inner_copy(i, w).start()
        return carry

    lax.fori_loop(0, g - 1, start_inner, 0)

    def wait_inner(i, carry):
        inner_copy(i, w).wait_send()
        inner_copy(i, lax.rem(w + 2 * g - 1 - i, g)).wait_recv()
        return carry

    lax.fori_loop(0, g - 1, wait_inner, 0)
    own2.wait()
    total_out[...] = jnp.sum(stage2[...], axis=0)


def scatter_all(part, g):
    dma = pltpu.SemaphoreType.DMA
    vmem = pl.BlockSpec(memory_space=pltpu.VMEM)
    width = part.shape[-1]
    return pl.pallas_call(
        functools.partial(scatter_kernel, g),
        out_shape=jax.ShapeDtypeStruct((1, width), part.dtype),
        in_specs=[vmem],
        out_specs=vmem,
        scratch_shapes=[
            pltpu.VMEM((g, g, width), jnp.float32),
            pltpu.VMEM((g, 1, width), jnp.float32),
            pltpu.VMEM((g, 1, width), jnp.float32),
            dma((g,)), dma((g,)), dma((g,)), dma((g,)), dma((2,)),
        ],
        compiler_params=pltpu.CompilerParams(has_side_effects=True, collective_id=1),
    )(part)


def matern_sums(neg_two_rows, row_sq, col_points, col_coef):
    col_sq = jnp.sum(jnp.square(col_points.astype(jnp.float32)), axis=1)
    neg_two_dot = lax.dot_general(
        neg_two_rows, col_points, (((1,), (1,)), ((), ())), preferred_element_type=jnp.float32
    )
    sq = (row_sq[:, None] + col_sq[None, :]) + neg_two_dot
    distance = jnp.where(sq > 0.0, sq * lax.rsqrt(sq), 0.0)
    m = distance * (-KERNEL_RATE)
    kernel_tile = (1.0 - m) * jnp.exp(m)
    return jnp.sum(kernel_tile * col_coef[None, :], axis=1)


def column_sums(row_feats, piece_points, every_coef):
    neg_two_rows = row_feats
    row_sq = 0.25 * jnp.sum(jnp.square(neg_two_rows.astype(jnp.float32)), axis=1)
    zeros_init = jnp.zeros((row_feats.shape[0],), jnp.float32)
    piece_len = piece_points.shape[0]
    block_len = math.gcd(piece_len, 2048)
    point_blocks = piece_points.reshape(-1, block_len, piece_points.shape[1])
    coef_blocks = every_coef.reshape(-1, block_len)

    def advance(partial_sum, column_block):
        return (
            partial_sum + matern_sums(neg_two_rows, row_sq, column_block[0], column_block[1]),
            None,
        )

    result, unused = lax.scan(advance, zeros_init, (point_blocks, coef_blocks))
    return result


def per_device(n_blk, n_str, points, coefficients, velocity, targets, batch_rows, counts):
    preview = coefficients + MOMENTUM * velocity
    slot_total = batch_rows.shape[0]
    local_size = points.shape[0]
    choose = (batch_rows[:, None] == jnp.arange(local_size, dtype=jnp.int32)[None, :])
    choose = jnp.where(choose, -2.0, 0.0).astype(points.dtype)
    picked = jnp.dot(choose, points, preferred_element_type=jnp.float32).astype(points.dtype)
    g = 8
    lanes = 128
    dense = lambda a: a.reshape(-1, lanes)
    rows_all, pts_all, prev_all = gather_all(
        dense(picked), dense(points), preview.reshape(1, -1), g)
    rows_all, batch_rows, counts = lax.optimization_barrier((rows_all, batch_rows, counts))
    slot_ids = jnp.arange(slot_total, dtype=jnp.int32)
    count_here = counts.reshape((1,))
    in_count = slot_ids < count_here[0]
    group_rows = rows_all.reshape(-1, points.shape[1])
    piece_points = pts_all.reshape(-1, points.shape[1])
    every_coef = prev_all.reshape(-1)
    partial_value = column_sums(group_rows, piece_points, every_coef)
    kernel_rows = scatter_all(partial_value.reshape(g, g, slot_total), g).reshape(-1)
    residual = jnp.where(
        in_count,
        kernel_rows + NOISE_VAR * preview.at[batch_rows].get(mode="promise_in_bounds") - targets.at[batch_rows].get(mode="promise_in_bounds"),
        0.0,
    )
    scatter_rows = (batch_rows[:, None] == jnp.arange(local_size, dtype=jnp.int32)[None, :]).astype(
        jnp.float32
    )
    update_sum = jnp.dot(residual, scatter_rows, precision=lax.Precision.HIGHEST)
    new_velocity = MOMENTUM * velocity - STEP_SIZE * update_sum
    new_coefficients = coefficients + new_velocity
    return (new_coefficients, new_velocity)


def solution(mesh):
    n_blk = mesh.shape["blk"]
    n_str = mesh.shape["stripe"]
    in_specs = (
        P(("blk", "stripe"), None),
        P(("blk", "stripe")),
        P(("blk", "stripe")),
        P(("blk", "stripe")),
        P(("blk", "stripe")),
        P("blk", "stripe"),
    )
    out_specs = (P(("blk", "stripe")), P(("blk", "stripe")))
    return jax.shard_map(
        functools.partial(per_device, n_blk, n_str), mesh=mesh, in_specs=in_specs,
        out_specs=out_specs, check_vma=False
    )
```

```python
import functools
import math

import jax
import jax.numpy as jnp
from jax import lax
from jax.experimental import pallas as pl
from jax.experimental.pallas import tpu as pltpu
from jax.sharding import PartitionSpec as P

MOMENTUM = 0.9
STEP_SIZE = 1.0
NOISE_VAR = 8.0
KERNEL_RATE = 3.0**0.5 / 6.0

MESH_ID = pl.DeviceIdType.MESH
ANY = pl.BlockSpec(memory_space=pl.ANY)


def coords():
    b = lax.axis_index("blk")
    s = lax.axis_index("stripe")
    core = lax.rem(s, 2)
    z_hi = lax.rem(s // 2, 2)
    x = lax.rem(s // 4, 4)
    y = s // 16
    c = lax.rem(b, 2) * 4 + lax.rem(x, 2) * 2 + core
    q = y * 2 + x // 2
    w = (b // 2) * 2 + z_hi
    return c, q, w


def dev(c, q, w):
    b = (w // 2) * 2 + c // 4
    z_hi = lax.rem(w, 2)
    y = q // 2
    x = lax.rem(q, 2) * 2 + lax.rem(c // 2, 2)
    core = lax.rem(c, 2)
    return (b, ((y * 4 + x) * 2 + z_hi) * 2 + core)


def greet_all(barrier, peers_of, n, total):
    def greet(i, carry):
        pl.semaphore_signal(barrier, 1, device_id=peers_of(i), device_id_type=MESH_ID)
        return carry

    lax.fori_loop(0, n, greet, 0)
    return total + n


def gather_kernel(g, picked, pts, prev, rows_out, pts_out, prev_out,
                  in_send, in_recv, out_send, out_recv, pt_send, pt_recv, pv_send, pv_recv,
                  local_sem):
    c, q, w = coords()
    barrier = pltpu.get_barrier_semaphore()
    n = greet_all(barrier, lambda i: dev(c, q, lax.rem(w + 1 + i, g)), g - 1, 0)
    n = greet_all(barrier, lambda i: dev(c, lax.rem(q + 1 + i, g), w), g - 1, n)
    n = greet_all(barrier, lambda i: dev(lax.rem(c + 1 + i, g), q, w), g - 1, n)
    pl.semaphore_wait(barrier, n)
    own = [
        pltpu.make_async_copy(picked, rows_out.at[q, w], local_sem.at[0]),
        pltpu.make_async_copy(pts, pts_out.at[c], local_sem.at[1]),
        pltpu.make_async_copy(prev, prev_out.at[c], local_sem.at[2]),
    ]
    for cp in own:
        cp.start()

    def inner_copy(i, src):
        return pltpu.make_async_remote_copy(
            src_ref=picked, dst_ref=rows_out.at[q, src], send_sem=in_send.at[i],
            recv_sem=in_recv.at[src], device_id=dev(c, q, lax.rem(w + 1 + i, g)),
            device_id_type=MESH_ID)

    def outer_copy(i, src):
        return pltpu.make_async_remote_copy(
            src_ref=rows_out.at[q], dst_ref=rows_out.at[src], send_sem=out_send.at[i],
            recv_sem=out_recv.at[src], device_id=dev(c, lax.rem(q + 1 + i, g), w),
            device_id_type=MESH_ID)

    def group_copies(i, src):
        peer = dev(lax.rem(c + 1 + i, g), q, w)
        return (
            pltpu.make_async_remote_copy(
                src_ref=pts, dst_ref=pts_out.at[src], send_sem=pt_send.at[i],
                recv_sem=pt_recv.at[src], device_id=peer, device_id_type=MESH_ID),
            pltpu.make_async_remote_copy(
                src_ref=prev, dst_ref=prev_out.at[src], send_sem=pv_send.at[i],
                recv_sem=pv_recv.at[src], device_id=peer, device_id_type=MESH_ID),
        )

    def start_inner(i, carry):
        inner_copy(i, w).start()
        return carry

    def start_group(i, carry):
        for cp in group_copies(i, c):
            cp.start()
        return carry

    lax.fori_loop(0, g - 1, start_inner, 0)
    lax.fori_loop(0, g - 1, start_group, 0)

    def wait_inner(i, carry):
        inner_copy(i, w).wait_send()
        inner_copy(i, lax.rem(w + 2 * g - 1 - i, g)).wait_recv()
        return carry

    lax.fori_loop(0, g - 1, wait_inner, 0)
    own[0].wait()

    def start_outer(i, carry):
        outer_copy(i, q).start()
        return carry

    lax.fori_loop(0, g - 1, start_outer, 0)

    def wait_group(i, carry):
        for cp in group_copies(i, c):
            cp.wait_send()
        for cp in group_copies(i, lax.rem(c + 2 * g - 1 - i, g)):
            cp.wait_recv()
        return carry

    def wait_outer(i, carry):
        outer_copy(i, q).wait_send()
        outer_copy(i, lax.rem(q + 2 * g - 1 - i, g)).wait_recv()
        return carry

    lax.fori_loop(0, g - 1, wait_group, 0)
    lax.fori_loop(0, g - 1, wait_outer, 0)
    own[1].wait()
    own[2].wait()


def gather_all(picked, pts, prev, g):
    dma = pltpu.SemaphoreType.DMA
    return pl.pallas_call(
        functools.partial(gather_kernel, g),
        out_shape=(
            jax.ShapeDtypeStruct((g, g) + picked.shape, picked.dtype),
            jax.ShapeDtypeStruct((g,) + pts.shape, pts.dtype),
            jax.ShapeDtypeStruct((g,) + prev.shape, prev.dtype),
        ),
        in_specs=[ANY, ANY, ANY],
        out_specs=(ANY, ANY, ANY),
        scratch_shapes=[dma((g,)) for _ in range(8)] + [dma((3,))],
        compiler_params=pltpu.CompilerParams(has_side_effects=True, collective_id=0),
    )(picked, pts, prev)


def scatter_kernel(g, part, total_out, stage1, mid, stage2,
                   out_send, out_recv, in_send, in_recv, local_sem):
    c, q, w = coords()
    barrier = pltpu.get_barrier_semaphore()
    n = greet_all(barrier, lambda i: dev(c, q, lax.rem(w + 1 + i, g)), g - 1, 0)
    n = greet_all(barrier, lambda i: dev(c, lax.rem(q + 1 + i, g), w), g - 1, n)
    pl.semaphore_wait(barrier, n)
    own1 = pltpu.make_async_copy(part.at[q], stage1.at[q], local_sem.at[0])
    own1.start()

    def outer_copy(i, src):
        peer = lax.rem(q + 1 + i, g)
        return pltpu.make_async_remote_copy(
            src_ref=part.at[peer], dst_ref=stage1.at[src], send_sem=out_send.at[i],
            recv_sem=out_recv.at[src], device_id=dev(c, peer, w), device_id_type=MESH_ID)

    def inner_copy(i, src):
        peer = lax.rem(w + 1 + i, g)
        return pltpu.make_async_remote_copy(
            src_ref=mid.at[peer], dst_ref=stage2.at[src], send_sem=in_send.at[i],
            recv_sem=in_recv.at[src], device_id=dev(c, q, peer), device_id_type=MESH_ID)

    def start_outer(i, carry):
        outer_copy(i, q).start()
        return carry

    lax.fori_loop(0, g - 1, start_outer, 0)

    def wait_outer(i, carry):
        outer_copy(i, q).wait_send()
        outer_copy(i, lax.rem(q + 2 * g - 1 - i, g)).wait_recv()
        return carry

    lax.fori_loop(0, g - 1, wait_outer, 0)
    own1.wait()
    mid[...] = jnp.sum(stage1[...], axis=0)[:, None, :]
    own2 = pltpu.make_async_copy(mid.at[w], stage2.at[w], local_sem.at[1])
    own2.start()

    def start_inner(i, carry):
        inner_copy(i, w).start()
        return carry

    lax.fori_loop(0, g - 1, start_inner, 0)

    def wait_inner(i, carry):
        inner_copy(i, w).wait_send()
        inner_copy(i, lax.rem(w + 2 * g - 1 - i, g)).wait_recv()
        return carry

    lax.fori_loop(0, g - 1, wait_inner, 0)
    own2.wait()
    total_out[...] = jnp.sum(stage2[...], axis=0)


def scatter_all(part, g):
    dma = pltpu.SemaphoreType.DMA
    vmem = pl.BlockSpec(memory_space=pltpu.VMEM)
    width = part.shape[-1]
    return pl.pallas_call(
        functools.partial(scatter_kernel, g),
        out_shape=jax.ShapeDtypeStruct((1, width), part.dtype),
        in_specs=[vmem],
        out_specs=vmem,
        scratch_shapes=[
            pltpu.VMEM((g, g, width), jnp.float32),
            pltpu.VMEM((g, 1, width), jnp.float32),
            pltpu.VMEM((g, 1, width), jnp.float32),
            dma((g,)), dma((g,)), dma((g,)), dma((g,)), dma((2,)),
        ],
        compiler_params=pltpu.CompilerParams(has_side_effects=True, collective_id=1),
    )(part)


def matern_sums(neg_two_rows, row_sq, col_points, col_coef):
    col_sq = jnp.sum(jnp.square(col_points.astype(jnp.float32)), axis=1)
    neg_two_dot = lax.dot_general(
        neg_two_rows, col_points, (((1,), (1,)), ((), ())), preferred_element_type=jnp.float32
    )
    sq = (row_sq[:, None] + col_sq[None, :]) + neg_two_dot
    distance = jnp.where(sq > 0.0, sq * lax.rsqrt(sq), 0.0)
    m = distance * (-KERNEL_RATE)
    kernel_tile = (1.0 - m) * jnp.exp(m)
    return jnp.sum(kernel_tile * col_coef[None, :], axis=1)


def column_sums(row_feats, piece_points, every_coef):
    neg_two_rows = row_feats
    row_sq = 0.25 * jnp.sum(jnp.square(neg_two_rows.astype(jnp.float32)), axis=1)
    zeros_init = jnp.zeros((row_feats.shape[0],), jnp.float32)
    piece_len = piece_points.shape[0]
    block_len = math.gcd(piece_len, 2048)
    point_blocks = piece_points.reshape(-1, block_len, piece_points.shape[1])
    coef_blocks = every_coef.reshape(-1, block_len)

    def advance(partial_sum, column_block):
        return (
            partial_sum + matern_sums(neg_two_rows, row_sq, column_block[0], column_block[1]),
            None,
        )

    result, unused = lax.scan(advance, zeros_init, (point_blocks, coef_blocks))
    return result


def per_device(n_blk, n_str, points, coefficients, velocity, targets, batch_rows, counts):
    preview = coefficients + MOMENTUM * velocity
    slot_total = batch_rows.shape[0]
    local_size = points.shape[0]
    choose = (batch_rows[:, None] == jnp.arange(local_size, dtype=jnp.int32)[None, :])
    choose = jnp.where(choose, -2.0, 0.0).astype(points.dtype)
    picked = jnp.dot(choose, points, preferred_element_type=jnp.float32).astype(points.dtype)
    g = 8
    lanes = 128
    dense = lambda a: a.reshape(-1, lanes)
    rows_all, pts_all, prev_all = gather_all(
        dense(picked), dense(points), preview.reshape(1, -1), g)
    rows_all, batch_rows, counts = lax.optimization_barrier((rows_all, batch_rows, counts))
    slot_ids = jnp.arange(slot_total, dtype=jnp.int32)
    count_here = counts.reshape((1,))
    in_count = slot_ids < count_here[0]
    group_rows = rows_all.reshape(-1, points.shape[1])
    piece_points = pts_all.reshape(-1, points.shape[1])
    every_coef = prev_all.reshape(-1)
    partial_value = column_sums(group_rows, piece_points, every_coef)
    kernel_rows = scatter_all(partial_value.reshape(g, g, slot_total), g).reshape(-1)
    scatter_rows = (batch_rows[:, None] == jnp.arange(local_size, dtype=jnp.int32)[None, :]).astype(
        jnp.float32
    )
    adjust = NOISE_VAR * preview - targets
    looked_up = jnp.dot(scatter_rows, adjust, precision=lax.Precision.HIGHEST)
    residual = jnp.where(in_count, kernel_rows + looked_up, 0.0)
    update_sum = jnp.dot(residual, scatter_rows, precision=lax.Precision.HIGHEST)
    new_velocity = MOMENTUM * velocity - STEP_SIZE * update_sum
    new_coefficients = coefficients + new_velocity
    return (new_coefficients, new_velocity)


def solution(mesh):
    n_blk = mesh.shape["blk"]
    n_str = mesh.shape["stripe"]
    in_specs = (
        P(("blk", "stripe"), None),
        P(("blk", "stripe")),
        P(("blk", "stripe")),
        P(("blk", "stripe")),
        P(("blk", "stripe")),
        P("blk", "stripe"),
    )
    out_specs = (P(("blk", "stripe")), P(("blk", "stripe")))
    return jax.shard_map(
        functools.partial(per_device, n_blk, n_str), mesh=mesh, in_specs=in_specs,
        out_specs=out_specs, check_vma=False
    )
```

```python
import functools
import math

import jax
import jax.numpy as jnp
from jax import lax
from jax.experimental import pallas as pl
from jax.experimental.pallas import tpu as pltpu
from jax.sharding import PartitionSpec as P

MOMENTUM = 0.9
STEP_SIZE = 1.0
NOISE_VAR = 8.0
KERNEL_RATE = 3.0**0.5 / 6.0

MESH_ID = pl.DeviceIdType.MESH
ANY = pl.BlockSpec(memory_space=pl.ANY)


def coords():
    b = lax.axis_index("blk")
    s = lax.axis_index("stripe")
    core = lax.rem(s, 2)
    z_hi = lax.rem(s // 2, 2)
    x = lax.rem(s // 4, 4)
    y = s // 16
    c = lax.rem(b, 2) * 4 + lax.rem(x, 2) * 2 + core
    q = y * 2 + x // 2
    w = (b // 2) * 2 + z_hi
    return c, q, w


def dev(c, q, w):
    b = (w // 2) * 2 + c // 4
    z_hi = lax.rem(w, 2)
    y = q // 2
    x = lax.rem(q, 2) * 2 + lax.rem(c // 2, 2)
    core = lax.rem(c, 2)
    return (b, ((y * 4 + x) * 2 + z_hi) * 2 + core)


def greet_all(barrier, peers_of, n, total):
    def greet(i, carry):
        pl.semaphore_signal(barrier, 1, device_id=peers_of(i), device_id_type=MESH_ID)
        return carry

    lax.fori_loop(0, n, greet, 0)
    return total + n


def gather_kernel(g, picked, pts, prev, rows_out, pts_out, prev_out,
                  in_send, in_recv, out_send, out_recv, pt_send, pt_recv, pv_send, pv_recv,
                  local_sem):
    c, q, w = coords()
    barrier = pltpu.get_barrier_semaphore()
    n = greet_all(barrier, lambda i: dev(c, q, lax.rem(w + 1 + i, g)), g - 1, 0)
    n = greet_all(barrier, lambda i: dev(c, lax.rem(q + 1 + i, g), w), g - 1, n)
    n = greet_all(barrier, lambda i: dev(lax.rem(c + 1 + i, g), q, w), g - 1, n)
    pl.semaphore_wait(barrier, n)
    own = [
        pltpu.make_async_copy(picked, rows_out.at[q, w], local_sem.at[0]),
        pltpu.make_async_copy(pts, pts_out.at[c], local_sem.at[1]),
        pltpu.make_async_copy(prev, prev_out.at[c], local_sem.at[2]),
    ]
    for cp in own:
        cp.start()

    def inner_copy(i, src):
        return pltpu.make_async_remote_copy(
            src_ref=picked, dst_ref=rows_out.at[q, src], send_sem=in_send.at[i],
            recv_sem=in_recv.at[src], device_id=dev(c, q, lax.rem(w + 1 + i, g)),
            device_id_type=MESH_ID)

    def outer_copy(i, src):
        return pltpu.make_async_remote_copy(
            src_ref=rows_out.at[q], dst_ref=rows_out.at[src], send_sem=out_send.at[i],
            recv_sem=out_recv.at[src], device_id=dev(c, lax.rem(q + 1 + i, g), w),
            device_id_type=MESH_ID)

    def group_copies(i, src):
        peer = dev(lax.rem(c + 1 + i, g), q, w)
        return (
            pltpu.make_async_remote_copy(
                src_ref=pts, dst_ref=pts_out.at[src], send_sem=pt_send.at[i],
                recv_sem=pt_recv.at[src], device_id=peer, device_id_type=MESH_ID),
            pltpu.make_async_remote_copy(
                src_ref=prev, dst_ref=prev_out.at[src], send_sem=pv_send.at[i],
                recv_sem=pv_recv.at[src], device_id=peer, device_id_type=MESH_ID),
        )

    def start_inner(i, carry):
        inner_copy(i, w).start()
        return carry

    def start_group(i, carry):
        for cp in group_copies(i, c):
            cp.start()
        return carry

    lax.fori_loop(0, g - 1, start_inner, 0)
    lax.fori_loop(0, g - 1, start_group, 0)

    def wait_inner(i, carry):
        inner_copy(i, lax.rem(w + 2 * g - 1 - i, g)).wait_recv()
        return carry

    def wait_inner_sent(i, carry):
        inner_copy(i, w).wait_send()
        return carry

    lax.fori_loop(0, g - 1, wait_inner, 0)
    own[0].wait()

    def start_outer(i, carry):
        outer_copy(i, q).start()
        return carry

    lax.fori_loop(0, g - 1, start_outer, 0)

    def wait_group(i, carry):
        for cp in group_copies(i, c):
            cp.wait_send()
        for cp in group_copies(i, lax.rem(c + 2 * g - 1 - i, g)):
            cp.wait_recv()
        return carry

    def wait_outer(i, carry):
        outer_copy(i, q).wait_send()
        outer_copy(i, lax.rem(q + 2 * g - 1 - i, g)).wait_recv()
        return carry

    lax.fori_loop(0, g - 1, wait_group, 0)
    lax.fori_loop(0, g - 1, wait_outer, 0)
    lax.fori_loop(0, g - 1, wait_inner_sent, 0)
    own[1].wait()
    own[2].wait()


def gather_all(picked, pts, prev, g):
    dma = pltpu.SemaphoreType.DMA
    return pl.pallas_call(
        functools.partial(gather_kernel, g),
        out_shape=(
            jax.ShapeDtypeStruct((g, g) + picked.shape, picked.dtype),
            jax.ShapeDtypeStruct((g,) + pts.shape, pts.dtype),
            jax.ShapeDtypeStruct((g,) + prev.shape, prev.dtype),
        ),
        in_specs=[ANY, ANY, ANY],
        out_specs=(ANY, ANY, ANY),
        scratch_shapes=[dma((g,)) for _ in range(8)] + [dma((3,))],
        compiler_params=pltpu.CompilerParams(has_side_effects=True, collective_id=0),
    )(picked, pts, prev)


def scatter_kernel(g, part, total_out, stage1, mid, stage2,
                   out_send, out_recv, in_send, in_recv, local_sem):
    c, q, w = coords()
    barrier = pltpu.get_barrier_semaphore()
    n = greet_all(barrier, lambda i: dev(c, q, lax.rem(w + 1 + i, g)), g - 1, 0)
    n = greet_all(barrier, lambda i: dev(c, lax.rem(q + 1 + i, g), w), g - 1, n)
    pl.semaphore_wait(barrier, n)
    own1 = pltpu.make_async_copy(part.at[q], stage1.at[q], local_sem.at[0])
    own1.start()

    def outer_copy(i, src):
        peer = lax.rem(q + 1 + i, g)
        return pltpu.make_async_remote_copy(
            src_ref=part.at[peer], dst_ref=stage1.at[src], send_sem=out_send.at[i],
            recv_sem=out_recv.at[src], device_id=dev(c, peer, w), device_id_type=MESH_ID)

    def inner_copy(i, src):
        peer = lax.rem(w + 1 + i, g)
        return pltpu.make_async_remote_copy(
            src_ref=mid.at[peer], dst_ref=stage2.at[src], send_sem=in_send.at[i],
            recv_sem=in_recv.at[src], device_id=dev(c, q, peer), device_id_type=MESH_ID)

    def start_outer(i, carry):
        outer_copy(i, q).start()
        return carry

    lax.fori_loop(0, g - 1, start_outer, 0)

    def wait_outer(i, carry):
        outer_copy(i, lax.rem(q + 2 * g - 1 - i, g)).wait_recv()
        return carry

    def wait_outer_sent(i, carry):
        outer_copy(i, q).wait_send()
        return carry

    lax.fori_loop(0, g - 1, wait_outer, 0)
    own1.wait()
    mid[...] = jnp.sum(stage1[...], axis=0)[:, None, :]
    own2 = pltpu.make_async_copy(mid.at[w], stage2.at[w], local_sem.at[1])
    own2.start()

    def start_inner(i, carry):
        inner_copy(i, w).start()
        return carry

    lax.fori_loop(0, g - 1, start_inner, 0)

    def wait_inner(i, carry):
        inner_copy(i, w).wait_send()
        inner_copy(i, lax.rem(w + 2 * g - 1 - i, g)).wait_recv()
        return carry

    lax.fori_loop(0, g - 1, wait_inner, 0)
    own2.wait()
    total_out[...] = jnp.sum(stage2[...], axis=0)
    lax.fori_loop(0, g - 1, wait_outer_sent, 0)


def scatter_all(part, g):
    dma = pltpu.SemaphoreType.DMA
    vmem = pl.BlockSpec(memory_space=pltpu.VMEM)
    width = part.shape[-1]
    return pl.pallas_call(
        functools.partial(scatter_kernel, g),
        out_shape=jax.ShapeDtypeStruct((1, width), part.dtype),
        in_specs=[vmem],
        out_specs=vmem,
        scratch_shapes=[
            pltpu.VMEM((g, g, width), jnp.float32),
            pltpu.VMEM((g, 1, width), jnp.float32),
            pltpu.VMEM((g, 1, width), jnp.float32),
            dma((g,)), dma((g,)), dma((g,)), dma((g,)), dma((2,)),
        ],
        compiler_params=pltpu.CompilerParams(has_side_effects=True, collective_id=1),
    )(part)


def matern_sums(neg_two_rows, row_sq, col_points, col_coef):
    col_sq = jnp.sum(jnp.square(col_points.astype(jnp.float32)), axis=1)
    neg_two_dot = lax.dot_general(
        neg_two_rows, col_points, (((1,), (1,)), ((), ())), preferred_element_type=jnp.float32
    )
    sq = (row_sq[:, None] + col_sq[None, :]) + neg_two_dot
    distance = jnp.where(sq > 0.0, sq * lax.rsqrt(sq), 0.0)
    m = distance * (-KERNEL_RATE)
    kernel_tile = (1.0 - m) * jnp.exp(m)
    return jnp.sum(kernel_tile * col_coef[None, :], axis=1)


def column_sums(row_feats, piece_points, every_coef):
    neg_two_rows = row_feats
    row_sq = 0.25 * jnp.sum(jnp.square(neg_two_rows.astype(jnp.float32)), axis=1)
    zeros_init = jnp.zeros((row_feats.shape[0],), jnp.float32)
    piece_len = piece_points.shape[0]
    block_len = math.gcd(piece_len, 2048)
    point_blocks = piece_points.reshape(-1, block_len, piece_points.shape[1])
    coef_blocks = every_coef.reshape(-1, block_len)

    def advance(partial_sum, column_block):
        return (
            partial_sum + matern_sums(neg_two_rows, row_sq, column_block[0], column_block[1]),
            None,
        )

    result, unused = lax.scan(advance, zeros_init, (point_blocks, coef_blocks))
    return result


def per_device(n_blk, n_str, points, coefficients, velocity, targets, batch_rows, counts):
    preview = coefficients + MOMENTUM * velocity
    slot_total = batch_rows.shape[0]
    local_size = points.shape[0]
    choose = (batch_rows[:, None] == jnp.arange(local_size, dtype=jnp.int32)[None, :])
    choose = jnp.where(choose, -2.0, 0.0).astype(points.dtype)
    picked = jnp.dot(choose, points, preferred_element_type=jnp.float32).astype(points.dtype)
    g = 8
    lanes = 128
    dense = lambda a: a.reshape(-1, lanes)
    rows_all, pts_all, prev_all = gather_all(
        dense(picked), dense(points), preview.reshape(1, -1), g)
    rows_all, batch_rows, counts = lax.optimization_barrier((rows_all, batch_rows, counts))
    slot_ids = jnp.arange(slot_total, dtype=jnp.int32)
    count_here = counts.reshape((1,))
    in_count = slot_ids < count_here[0]
    group_rows = rows_all.reshape(-1, points.shape[1])
    piece_points = pts_all.reshape(-1, points.shape[1])
    every_coef = prev_all.reshape(-1)
    partial_value = column_sums(group_rows, piece_points, every_coef)
    kernel_rows = scatter_all(partial_value.reshape(g, g, slot_total), g).reshape(-1)
    scatter_rows = (batch_rows[:, None] == jnp.arange(local_size, dtype=jnp.int32)[None, :]).astype(
        jnp.float32
    )
    adjust = NOISE_VAR * preview - targets
    looked_up = jnp.dot(scatter_rows, adjust, precision=lax.Precision.HIGHEST)
    residual = jnp.where(in_count, kernel_rows + looked_up, 0.0)
    update_sum = jnp.dot(residual, scatter_rows, precision=lax.Precision.HIGHEST)
    new_velocity = MOMENTUM * velocity - STEP_SIZE * update_sum
    new_coefficients = coefficients + new_velocity
    return (new_coefficients, new_velocity)


def solution(mesh):
    n_blk = mesh.shape["blk"]
    n_str = mesh.shape["stripe"]
    in_specs = (
        P(("blk", "stripe"), None),
        P(("blk", "stripe")),
        P(("blk", "stripe")),
        P(("blk", "stripe")),
        P(("blk", "stripe")),
        P("blk", "stripe"),
    )
    out_specs = (P(("blk", "stripe")), P(("blk", "stripe")))
    return jax.shard_map(
        functools.partial(per_device, n_blk, n_str), mesh=mesh, in_specs=in_specs,
        out_specs=out_specs, check_vma=False
    )
```

```python
import functools
import math

import jax
import jax.numpy as jnp
from jax import lax
from jax.experimental import pallas as pl
from jax.experimental.pallas import tpu as pltpu
from jax.sharding import PartitionSpec as P

MOMENTUM = 0.9
STEP_SIZE = 1.0
NOISE_VAR = 8.0
KERNEL_RATE = 3.0**0.5 / 6.0

MESH_ID = pl.DeviceIdType.MESH
ANY = pl.BlockSpec(memory_space=pl.ANY)


def coords():
    b = lax.axis_index("blk")
    s = lax.axis_index("stripe")
    core = lax.rem(s, 2)
    z_hi = lax.rem(s // 2, 2)
    x = lax.rem(s // 4, 4)
    y = s // 16
    c = lax.rem(b, 2) * 4 + lax.rem(x, 2) * 2 + core
    q = y * 2 + x // 2
    w = (b // 2) * 2 + z_hi
    return c, q, w


def dev(c, q, w):
    b = (w // 2) * 2 + c // 4
    z_hi = lax.rem(w, 2)
    y = q // 2
    x = lax.rem(q, 2) * 2 + lax.rem(c // 2, 2)
    core = lax.rem(c, 2)
    return (b, ((y * 4 + x) * 2 + z_hi) * 2 + core)


def greet_all(barrier, peers_of, n, total):
    def greet(i, carry):
        pl.semaphore_signal(barrier, 1, device_id=peers_of(i), device_id_type=MESH_ID)
        return carry

    lax.fori_loop(0, n, greet, 0)
    return total + n


def gather_kernel(g, picked, pts, prev, rows_out, pts_out, prev_out,
                  in_send, in_recv, out_send, out_recv, pt_send, pt_recv, pv_send, pv_recv,
                  local_sem):
    c, q, w = coords()
    barrier = pltpu.get_barrier_semaphore()
    n = greet_all(barrier, lambda i: dev(c, q, lax.rem(w + 1 + i, g)), g - 1, 0)
    n = greet_all(barrier, lambda i: dev(c, lax.rem(q + 1 + i, g), w), g - 1, n)
    n = greet_all(barrier, lambda i: dev(lax.rem(c + 1 + i, g), q, w), g - 1, n)
    pl.semaphore_wait(barrier, n)
    own = [
        pltpu.make_async_copy(picked, rows_out.at[q, w], local_sem.at[0]),
        pltpu.make_async_copy(pts, pts_out.at[c], local_sem.at[1]),
        pltpu.make_async_copy(prev, prev_out.at[c], local_sem.at[2]),
    ]
    for cp in own:
        cp.start()

    def inner_copy(i, src):
        return pltpu.make_async_remote_copy(
            src_ref=picked, dst_ref=rows_out.at[q, src], send_sem=in_send.at[i],
            recv_sem=in_recv.at[src], device_id=dev(c, q, lax.rem(w + 1 + i, g)),
            device_id_type=MESH_ID)

    def outer_copy(i, src):
        return pltpu.make_async_remote_copy(
            src_ref=rows_out.at[q], dst_ref=rows_out.at[src], send_sem=out_send.at[i],
            recv_sem=out_recv.at[src], device_id=dev(c, lax.rem(q + 1 + i, g), w),
            device_id_type=MESH_ID)

    def group_copies(i, src):
        peer = dev(lax.rem(c + 1 + i, g), q, w)
        return (
            pltpu.make_async_remote_copy(
                src_ref=pts, dst_ref=pts_out.at[src], send_sem=pt_send.at[i],
                recv_sem=pt_recv.at[src], device_id=peer, device_id_type=MESH_ID),
            pltpu.make_async_remote_copy(
                src_ref=prev, dst_ref=prev_out.at[src], send_sem=pv_send.at[i],
                recv_sem=pv_recv.at[src], device_id=peer, device_id_type=MESH_ID),
        )

    def start_inner(i, carry):
        inner_copy(i, w).start()
        return carry

    def start_group(i, carry):
        for cp in group_copies(i, c):
            cp.start()
        return carry

    lax.fori_loop(0, g - 1, start_inner, 0)
    lax.fori_loop(0, g - 1, start_group, 0)

    def wait_inner(i, carry):
        inner_copy(i, w).wait_send()
        inner_copy(i, lax.rem(w + 2 * g - 1 - i, g)).wait_recv()
        return carry

    lax.fori_loop(0, g - 1, wait_inner, 0)
    own[0].wait()

    def start_outer(i, carry):
        outer_copy(i, q).start()
        return carry

    lax.fori_loop(0, g - 1, start_outer, 0)

    def wait_group(i, carry):
        for cp in group_copies(i, c):
            cp.wait_send()
        for cp in group_copies(i, lax.rem(c + 2 * g - 1 - i, g)):
            cp.wait_recv()
        return carry

    def wait_outer(i, carry):
        outer_copy(i, q).wait_send()
        outer_copy(i, lax.rem(q + 2 * g - 1 - i, g)).wait_recv()
        return carry

    lax.fori_loop(0, g - 1, wait_group, 0)
    lax.fori_loop(0, g - 1, wait_outer, 0)
    own[1].wait()
    own[2].wait()


def gather_all(picked, pts, prev, g):
    dma = pltpu.SemaphoreType.DMA
    return pl.pallas_call(
        functools.partial(gather_kernel, g),
        out_shape=(
            jax.ShapeDtypeStruct((g, g) + picked.shape, picked.dtype),
            jax.ShapeDtypeStruct((g,) + pts.shape, pts.dtype),
            jax.ShapeDtypeStruct((g,) + prev.shape, prev.dtype),
        ),
        in_specs=[pl.BlockSpec(memory_space=pltpu.VMEM)] * 2 + [ANY],
        out_specs=(ANY, ANY, ANY),
        scratch_shapes=[dma((g,)) for _ in range(8)] + [dma((3,))],
        compiler_params=pltpu.CompilerParams(has_side_effects=True, collective_id=0),
    )(picked, pts, prev)


def scatter_kernel(g, part, total_out, stage1, mid, stage2,
                   out_send, out_recv, in_send, in_recv, local_sem):
    c, q, w = coords()
    barrier = pltpu.get_barrier_semaphore()
    n = greet_all(barrier, lambda i: dev(c, q, lax.rem(w + 1 + i, g)), g - 1, 0)
    n = greet_all(barrier, lambda i: dev(c, lax.rem(q + 1 + i, g), w), g - 1, n)
    pl.semaphore_wait(barrier, n)
    own1 = pltpu.make_async_copy(part.at[q], stage1.at[q], local_sem.at[0])
    own1.start()

    def outer_copy(i, src):
        peer = lax.rem(q + 1 + i, g)
        return pltpu.make_async_remote_copy(
            src_ref=part.at[peer], dst_ref=stage1.at[src], send_sem=out_send.at[i],
            recv_sem=out_recv.at[src], device_id=dev(c, peer, w), device_id_type=MESH_ID)

    def inner_copy(i, src):
        peer = lax.rem(w + 1 + i, g)
        return pltpu.make_async_remote_copy(
            src_ref=mid.at[peer], dst_ref=stage2.at[src], send_sem=in_send.at[i],
            recv_sem=in_recv.at[src], device_id=dev(c, q, peer), device_id_type=MESH_ID)

    def start_outer(i, carry):
        outer_copy(i, q).start()
        return carry

    lax.fori_loop(0, g - 1, start_outer, 0)

    def wait_outer(i, carry):
        outer_copy(i, q).wait_send()
        outer_copy(i, lax.rem(q + 2 * g - 1 - i, g)).wait_recv()
        return carry

    lax.fori_loop(0, g - 1, wait_outer, 0)
    own1.wait()
    mid[...] = jnp.sum(stage1[...], axis=0)[:, None, :]
    own2 = pltpu.make_async_copy(mid.at[w], stage2.at[w], local_sem.at[1])
    own2.start()

    def start_inner(i, carry):
        inner_copy(i, w).start()
        return carry

    lax.fori_loop(0, g - 1, start_inner, 0)

    def wait_inner(i, carry):
        inner_copy(i, w).wait_send()
        inner_copy(i, lax.rem(w + 2 * g - 1 - i, g)).wait_recv()
        return carry

    lax.fori_loop(0, g - 1, wait_inner, 0)
    own2.wait()
    total_out[...] = jnp.sum(stage2[...], axis=0)


def scatter_all(part, g):
    dma = pltpu.SemaphoreType.DMA
    vmem = pl.BlockSpec(memory_space=pltpu.VMEM)
    width = part.shape[-1]
    return pl.pallas_call(
        functools.partial(scatter_kernel, g),
        out_shape=jax.ShapeDtypeStruct((1, width), part.dtype),
        in_specs=[vmem],
        out_specs=vmem,
        scratch_shapes=[
            pltpu.VMEM((g, g, width), jnp.float32),
            pltpu.VMEM((g, 1, width), jnp.float32),
            pltpu.VMEM((g, 1, width), jnp.float32),
            dma((g,)), dma((g,)), dma((g,)), dma((g,)), dma((2,)),
        ],
        compiler_params=pltpu.CompilerParams(has_side_effects=True, collective_id=1),
    )(part)


def matern_sums(neg_two_rows, row_sq, col_points, col_coef):
    col_sq = jnp.sum(jnp.square(col_points.astype(jnp.float32)), axis=1)
    neg_two_dot = lax.dot_general(
        neg_two_rows, col_points, (((1,), (1,)), ((), ())), preferred_element_type=jnp.float32
    )
    sq = (row_sq[:, None] + col_sq[None, :]) + neg_two_dot
    distance = jnp.where(sq > 0.0, sq * lax.rsqrt(sq), 0.0)
    m = distance * (-KERNEL_RATE)
    kernel_tile = (1.0 - m) * jnp.exp(m)
    return jnp.sum(kernel_tile * col_coef[None, :], axis=1)


def column_sums(row_feats, piece_points, every_coef):
    neg_two_rows = row_feats
    row_sq = 0.25 * jnp.sum(jnp.square(neg_two_rows.astype(jnp.float32)), axis=1)
    zeros_init = jnp.zeros((row_feats.shape[0],), jnp.float32)
    piece_len = piece_points.shape[0]
    block_len = math.gcd(piece_len, 2048)
    point_blocks = piece_points.reshape(-1, block_len, piece_points.shape[1])
    coef_blocks = every_coef.reshape(-1, block_len)

    def advance(partial_sum, column_block):
        return (
            partial_sum + matern_sums(neg_two_rows, row_sq, column_block[0], column_block[1]),
            None,
        )

    result, unused = lax.scan(advance, zeros_init, (point_blocks, coef_blocks))
    return result


def per_device(n_blk, n_str, points, coefficients, velocity, targets, batch_rows, counts):
    preview = coefficients + MOMENTUM * velocity
    slot_total = batch_rows.shape[0]
    local_size = points.shape[0]
    choose = (batch_rows[:, None] == jnp.arange(local_size, dtype=jnp.int32)[None, :])
    choose = jnp.where(choose, -2.0, 0.0).astype(points.dtype)
    picked = jnp.dot(choose, points, preferred_element_type=jnp.float32).astype(points.dtype)
    g = 8
    lanes = 128
    dense = lambda a: a.reshape(-1, lanes)
    rows_all, pts_all, prev_all = gather_all(
        dense(picked), dense(points), preview.reshape(1, -1), g)
    rows_all, batch_rows, counts = lax.optimization_barrier((rows_all, batch_rows, counts))
    slot_ids = jnp.arange(slot_total, dtype=jnp.int32)
    count_here = counts.reshape((1,))
    in_count = slot_ids < count_here[0]
    group_rows = rows_all.reshape(-1, points.shape[1])
    piece_points = pts_all.reshape(-1, points.shape[1])
    every_coef = prev_all.reshape(-1)
    partial_value = column_sums(group_rows, piece_points, every_coef)
    kernel_rows = scatter_all(partial_value.reshape(g, g, slot_total), g).reshape(-1)
    scatter_rows = (batch_rows[:, None] == jnp.arange(local_size, dtype=jnp.int32)[None, :]).astype(
        jnp.float32
    )
    adjust = NOISE_VAR * preview - targets
    looked_up = jnp.dot(scatter_rows, adjust, precision=lax.Precision.HIGHEST)
    residual = jnp.where(in_count, kernel_rows + looked_up, 0.0)
    update_sum = jnp.dot(residual, scatter_rows, precision=lax.Precision.HIGHEST)
    new_velocity = MOMENTUM * velocity - STEP_SIZE * update_sum
    new_coefficients = coefficients + new_velocity
    return (new_coefficients, new_velocity)


def solution(mesh):
    n_blk = mesh.shape["blk"]
    n_str = mesh.shape["stripe"]
    in_specs = (
        P(("blk", "stripe"), None),
        P(("blk", "stripe")),
        P(("blk", "stripe")),
        P(("blk", "stripe")),
        P(("blk", "stripe")),
        P("blk", "stripe"),
    )
    out_specs = (P(("blk", "stripe")), P(("blk", "stripe")))
    return jax.shard_map(
        functools.partial(per_device, n_blk, n_str), mesh=mesh, in_specs=in_specs,
        out_specs=out_specs, check_vma=False
    )
```

```python
import functools
import math

import jax
import jax.numpy as jnp
from jax import lax
from jax.experimental import pallas as pl
from jax.experimental.pallas import tpu as pltpu
from jax.sharding import PartitionSpec as P

MOMENTUM = 0.9
STEP_SIZE = 1.0
NOISE_VAR = 8.0
KERNEL_RATE = 3.0**0.5 / 6.0

MESH_ID = pl.DeviceIdType.MESH
ANY = pl.BlockSpec(memory_space=pl.ANY)


def coords():
    b = lax.axis_index("blk")
    s = lax.axis_index("stripe")
    core = lax.rem(s, 2)
    z_hi = lax.rem(s // 2, 2)
    x = lax.rem(s // 4, 4)
    y = s // 16
    c = lax.rem(b, 2) * 4 + lax.rem(x, 2) * 2 + core
    q = y * 2 + x // 2
    w = (b // 2) * 2 + z_hi
    return c, q, w


def dev(c, q, w):
    b = (w // 2) * 2 + c // 4
    z_hi = lax.rem(w, 2)
    y = q // 2
    x = lax.rem(q, 2) * 2 + lax.rem(c // 2, 2)
    core = lax.rem(c, 2)
    return (b, ((y * 4 + x) * 2 + z_hi) * 2 + core)


def greet_all(barrier, peers_of, n, total):
    def greet(i, carry):
        pl.semaphore_signal(barrier, 1, device_id=peers_of(i), device_id_type=MESH_ID)
        return carry

    lax.fori_loop(0, n, greet, 0)
    return total + n


def gather_kernel(g, picked, pts, prev, rows_out, pts_out, prev_out,
                  in_send, in_recv, out_send, out_recv, pt_send, pt_recv, pv_send, pv_recv,
                  local_sem):
    c, q, w = coords()
    barrier = pltpu.get_barrier_semaphore()
    n = greet_all(barrier, lambda i: dev(c, q, lax.rem(w + 1 + i, g)), g - 1, 0)
    n = greet_all(barrier, lambda i: dev(c, lax.rem(q + 1 + i, g), w), g - 1, n)
    n = greet_all(barrier, lambda i: dev(lax.rem(c + 1 + i, g), q, w), g - 1, n)
    pl.semaphore_wait(barrier, n)
    own = [
        pltpu.make_async_copy(picked, rows_out.at[q, w], local_sem.at[0]),
        pltpu.make_async_copy(pts, pts_out.at[c], local_sem.at[1]),
        pltpu.make_async_copy(prev, prev_out.at[c], local_sem.at[2]),
    ]
    for cp in own:
        cp.start()

    def inner_copy(i, src):
        return pltpu.make_async_remote_copy(
            src_ref=picked, dst_ref=rows_out.at[q, src], send_sem=in_send.at[i],
            recv_sem=in_recv.at[src], device_id=dev(c, q, lax.rem(w + 1 + i, g)),
            device_id_type=MESH_ID)

    def outer_copy(i, src):
        return pltpu.make_async_remote_copy(
            src_ref=rows_out.at[q], dst_ref=rows_out.at[src], send_sem=out_send.at[i],
            recv_sem=out_recv.at[src], device_id=dev(c, lax.rem(q + 1 + i, g), w),
            device_id_type=MESH_ID)

    def group_copies(i, src):
        peer = dev(lax.rem(c + 1 + i, g), q, w)
        return (
            pltpu.make_async_remote_copy(
                src_ref=pts, dst_ref=pts_out.at[src], send_sem=pt_send.at[i],
                recv_sem=pt_recv.at[src], device_id=peer, device_id_type=MESH_ID),
            pltpu.make_async_remote_copy(
                src_ref=prev, dst_ref=prev_out.at[src], send_sem=pv_send.at[i],
                recv_sem=pv_recv.at[src], device_id=peer, device_id_type=MESH_ID),
        )

    def start_inner(i, carry):
        inner_copy(i, w).start()
        return carry

    def start_group(i, carry):
        for cp in group_copies(i, c):
            cp.start()
        return carry

    lax.fori_loop(0, g - 1, start_inner, 0)
    lax.fori_loop(0, g - 1, start_group, 0)

    def wait_inner(i, carry):
        inner_copy(i, w).wait_send()
        inner_copy(i, lax.rem(w + 2 * g - 1 - i, g)).wait_recv()
        return carry

    lax.fori_loop(0, g - 1, wait_inner, 0)
    own[0].wait()

    def start_outer(i, carry):
        outer_copy(i, q).start()
        return carry

    lax.fori_loop(0, g - 1, start_outer, 0)

    def wait_group(i, carry):
        for cp in group_copies(i, c):
            cp.wait_send()
        for cp in group_copies(i, lax.rem(c + 2 * g - 1 - i, g)):
            cp.wait_recv()
        return carry

    def wait_outer(i, carry):
        outer_copy(i, q).wait_send()
        outer_copy(i, lax.rem(q + 2 * g - 1 - i, g)).wait_recv()
        return carry

    lax.fori_loop(0, g - 1, wait_group, 0)
    lax.fori_loop(0, g - 1, wait_outer, 0)
    own[1].wait()
    own[2].wait()


def gather_all(picked, pts, prev, g):
    dma = pltpu.SemaphoreType.DMA
    return pl.pallas_call(
        functools.partial(gather_kernel, g),
        out_shape=(
            jax.ShapeDtypeStruct((g, g) + picked.shape, picked.dtype),
            jax.ShapeDtypeStruct((g,) + pts.shape, pts.dtype),
            jax.ShapeDtypeStruct((g,) + prev.shape, prev.dtype),
        ),
        in_specs=[ANY, ANY, ANY],
        out_specs=(ANY, ANY, ANY),
        scratch_shapes=[dma((g,)) for _ in range(8)] + [dma((3,))],
        compiler_params=pltpu.CompilerParams(has_side_effects=True, collective_id=0),
    )(picked, pts, prev)


def exchange(src_of, dst, my, n, peer_dev, send_sem, recv_sem, local_sem):
    own = pltpu.make_async_copy(src_of(my), dst.at[my], local_sem)
    own.start()

    def copy(i, src):
        peer = lax.rem(my + 1 + i, n)
        return pltpu.make_async_remote_copy(
            src_ref=src_of(peer), dst_ref=dst.at[src], send_sem=send_sem.at[i],
            recv_sem=recv_sem.at[src], device_id=peer_dev(peer), device_id_type=MESH_ID)

    def start(i, carry):
        copy(i, my).start()
        return carry

    lax.fori_loop(0, n - 1, start, 0)

    def wait(i, carry):
        copy(i, my).wait_send()
        copy(i, lax.rem(my + 2 * n - 1 - i, n)).wait_recv()
        return carry

    lax.fori_loop(0, n - 1, wait, 0)
    own.wait()


def scatter_kernel(n, part, total_out, s1, m1, s2, m2, s3, sems, local_sem):
    c, q, w = coords()
    a, bb, cc = q // 2, lax.rem(q, 2) * 2 + lax.rem(w, 2), w // 2
    at = lambda a2, b2, c2: dev(c, a2 * 2 + b2 // 2, c2 * 2 + lax.rem(b2, 2))
    barrier = pltpu.get_barrier_semaphore()
    k = greet_all(barrier, lambda i: at(lax.rem(a + 1 + i, n), bb, cc), n - 1, 0)
    k = greet_all(barrier, lambda i: at(a, lax.rem(bb + 1 + i, n), cc), n - 1, k)
    k = greet_all(barrier, lambda i: at(a, bb, lax.rem(cc + 1 + i, n)), n - 1, k)
    pl.semaphore_wait(barrier, k)
    exchange(lambda p: part.at[p], s1, a, n, lambda p: at(p, bb, cc),
             sems.at[0], sems.at[1], local_sem.at[0])
    m1[...] = jnp.sum(s1[...], axis=0)
    exchange(lambda p: m1.at[p], s2, bb, n, lambda p: at(a, p, cc),
             sems.at[2], sems.at[3], local_sem.at[1])
    m2[...] = jnp.sum(s2[...], axis=0)[:, None, :]
    exchange(lambda p: m2.at[p], s3, cc, n, lambda p: at(a, bb, p),
             sems.at[4], sems.at[5], local_sem.at[2])
    total_out[...] = jnp.sum(s3[...], axis=0)


def scatter_all(part, n):
    vmem = pl.BlockSpec(memory_space=pltpu.VMEM)
    width = part.shape[-1]
    f32 = jnp.float32
    return pl.pallas_call(
        functools.partial(scatter_kernel, n),
        out_shape=jax.ShapeDtypeStruct((1, width), part.dtype),
        in_specs=[vmem],
        out_specs=vmem,
        scratch_shapes=[
            pltpu.VMEM((n, n, n, width), f32),
            pltpu.VMEM((n, n, width), f32),
            pltpu.VMEM((n, n, width), f32),
            pltpu.VMEM((n, 1, width), f32),
            pltpu.VMEM((n, 1, width), f32),
            pltpu.SemaphoreType.DMA((6, n)),
            pltpu.SemaphoreType.DMA((3,)),
        ],
        compiler_params=pltpu.CompilerParams(has_side_effects=True, collective_id=1),
    )(part)


def matern_sums(neg_two_rows, row_sq, col_points, col_coef):
    col_sq = jnp.sum(jnp.square(col_points.astype(jnp.float32)), axis=1)
    neg_two_dot = lax.dot_general(
        neg_two_rows, col_points, (((1,), (1,)), ((), ())), preferred_element_type=jnp.float32
    )
    sq = (row_sq[:, None] + col_sq[None, :]) + neg_two_dot
    distance = jnp.where(sq > 0.0, sq * lax.rsqrt(sq), 0.0)
    m = distance * (-KERNEL_RATE)
    kernel_tile = (1.0 - m) * jnp.exp(m)
    return jnp.sum(kernel_tile * col_coef[None, :], axis=1)


def column_sums(row_feats, piece_points, every_coef):
    neg_two_rows = row_feats
    row_sq = 0.25 * jnp.sum(jnp.square(neg_two_rows.astype(jnp.float32)), axis=1)
    zeros_init = jnp.zeros((row_feats.shape[0],), jnp.float32)
    piece_len = piece_points.shape[0]
    block_len = math.gcd(piece_len, 2048)
    point_blocks = piece_points.reshape(-1, block_len, piece_points.shape[1])
    coef_blocks = every_coef.reshape(-1, block_len)

    def advance(partial_sum, column_block):
        return (
            partial_sum + matern_sums(neg_two_rows, row_sq, column_block[0], column_block[1]),
            None,
        )

    result, unused = lax.scan(advance, zeros_init, (point_blocks, coef_blocks))
    return result


def per_device(n_blk, n_str, points, coefficients, velocity, targets, batch_rows, counts):
    preview = coefficients + MOMENTUM * velocity
    slot_total = batch_rows.shape[0]
    local_size = points.shape[0]
    choose = (batch_rows[:, None] == jnp.arange(local_size, dtype=jnp.int32)[None, :])
    choose = jnp.where(choose, -2.0, 0.0).astype(points.dtype)
    picked = jnp.dot(choose, points, preferred_element_type=jnp.float32).astype(points.dtype)
    g = 8
    lanes = 128
    dense = lambda a: a.reshape(-1, lanes)
    rows_all, pts_all, prev_all = gather_all(
        dense(picked), dense(points), preview.reshape(1, -1), g)
    rows_all, batch_rows, counts = lax.optimization_barrier((rows_all, batch_rows, counts))
    slot_ids = jnp.arange(slot_total, dtype=jnp.int32)
    count_here = counts.reshape((1,))
    in_count = slot_ids < count_here[0]
    group_rows = rows_all.reshape(-1, points.shape[1])
    piece_points = pts_all.reshape(-1, points.shape[1])
    every_coef = prev_all.reshape(-1)
    partial_value = column_sums(group_rows, piece_points, every_coef)
    split = partial_value.reshape(4, 2, 4, 2, slot_total).transpose(0, 1, 3, 2, 4)
    kernel_rows = scatter_all(split.reshape(4, 4, 4, slot_total), 4).reshape(-1)
    scatter_rows = (batch_rows[:, None] == jnp.arange(local_size, dtype=jnp.int32)[None, :]).astype(
        jnp.float32
    )
    adjust = NOISE_VAR * preview - targets
    looked_up = jnp.dot(scatter_rows, adjust, precision=lax.Precision.HIGHEST)
    residual = jnp.where(in_count, kernel_rows + looked_up, 0.0)
    update_sum = jnp.dot(residual, scatter_rows, precision=lax.Precision.HIGHEST)
    new_velocity = MOMENTUM * velocity - STEP_SIZE * update_sum
    new_coefficients = coefficients + new_velocity
    return (new_coefficients, new_velocity)


def solution(mesh):
    n_blk = mesh.shape["blk"]
    n_str = mesh.shape["stripe"]
    in_specs = (
        P(("blk", "stripe"), None),
        P(("blk", "stripe")),
        P(("blk", "stripe")),
        P(("blk", "stripe")),
        P(("blk", "stripe")),
        P("blk", "stripe"),
    )
    out_specs = (P(("blk", "stripe")), P(("blk", "stripe")))
    return jax.shard_map(
        functools.partial(per_device, n_blk, n_str), mesh=mesh, in_specs=in_specs,
        out_specs=out_specs, check_vma=False
    )
```

```python
import functools
import math

import jax
import jax.numpy as jnp
from jax import lax
from jax.experimental import pallas as pl
from jax.experimental.pallas import tpu as pltpu
from jax.sharding import PartitionSpec as P

MOMENTUM = 0.9
STEP_SIZE = 1.0
NOISE_VAR = 8.0
KERNEL_RATE = 3.0**0.5 / 6.0

MESH_ID = pl.DeviceIdType.MESH
ANY = pl.BlockSpec(memory_space=pl.ANY)


def coords():
    b = lax.axis_index("blk")
    s = lax.axis_index("stripe")
    core = lax.rem(s, 2)
    z_hi = lax.rem(s // 2, 2)
    x = lax.rem(s // 4, 4)
    y = s // 16
    c = lax.rem(b, 2) * 4 + lax.rem(x, 2) * 2 + core
    q = y * 2 + x // 2
    w = (b // 2) * 2 + z_hi
    return c, q, w


def dev(c, q, w):
    b = (w // 2) * 2 + c // 4
    z_hi = lax.rem(w, 2)
    y = q // 2
    x = lax.rem(q, 2) * 2 + lax.rem(c // 2, 2)
    core = lax.rem(c, 2)
    return (b, ((y * 4 + x) * 2 + z_hi) * 2 + core)


def greet_all(barrier, peers_of, n, total):
    def greet(i, carry):
        pl.semaphore_signal(barrier, 1, device_id=peers_of(i), device_id_type=MESH_ID)
        return carry

    lax.fori_loop(0, n, greet, 0)
    return total + n


def gather_kernel(g, picked, pts, prev, rows_out, pts_out, prev_out,
                  in_send, in_recv, out_send, out_recv, pt_send, pt_recv, pv_send, pv_recv,
                  local_sem):
    c, q, w = coords()
    barrier = pltpu.get_barrier_semaphore()
    n = greet_all(barrier, lambda i: dev(c, q, lax.rem(w + 1 + i, g)), g - 1, 0)
    n = greet_all(barrier, lambda i: dev(c, lax.rem(q + 1 + i, g), w), g - 1, n)
    n = greet_all(barrier, lambda i: dev(lax.rem(c + 1 + i, g), q, w), g - 1, n)
    pl.semaphore_wait(barrier, n)
    own = [
        pltpu.make_async_copy(picked, rows_out.at[q, w], local_sem.at[0]),
        pltpu.make_async_copy(pts, pts_out.at[c], local_sem.at[1]),
        pltpu.make_async_copy(prev, prev_out.at[c], local_sem.at[2]),
    ]
    for cp in own:
        cp.start()

    def inner_copy(i, src):
        return pltpu.make_async_remote_copy(
            src_ref=picked, dst_ref=rows_out.at[q, src], send_sem=in_send.at[i],
            recv_sem=in_recv.at[src], device_id=dev(c, q, lax.rem(w + 1 + i, g)),
            device_id_type=MESH_ID)

    def outer_copy(i, src):
        return pltpu.make_async_remote_copy(
            src_ref=rows_out.at[q], dst_ref=rows_out.at[src], send_sem=out_send.at[i],
            recv_sem=out_recv.at[src], device_id=dev(c, lax.rem(q + 1 + i, g), w),
            device_id_type=MESH_ID)

    def group_copies(i, src):
        peer = dev(lax.rem(c + 1 + i, g), q, w)
        return (
            pltpu.make_async_remote_copy(
                src_ref=pts, dst_ref=pts_out.at[src], send_sem=pt_send.at[i],
                recv_sem=pt_recv.at[src], device_id=peer, device_id_type=MESH_ID),
            pltpu.make_async_remote_copy(
                src_ref=prev, dst_ref=prev_out.at[src], send_sem=pv_send.at[i],
                recv_sem=pv_recv.at[src], device_id=peer, device_id_type=MESH_ID),
        )

    def start_inner(i, carry):
        inner_copy(i, w).start()
        return carry

    def start_group(i, carry):
        for cp in group_copies(i, c):
            cp.start()
        return carry

    lax.fori_loop(0, g - 1, start_inner, 0)
    lax.fori_loop(0, g - 1, start_group, 0)

    def wait_inner(i, carry):
        inner_copy(i, w).wait_send()
        inner_copy(i, lax.rem(w + 2 * g - 1 - i, g)).wait_recv()
        return carry

    lax.fori_loop(0, g - 1, wait_inner, 0)
    own[0].wait()

    def start_outer(i, carry):
        outer_copy(i, q).start()
        return carry

    lax.fori_loop(0, g - 1, start_outer, 0)

    def wait_group(i, carry):
        for cp in group_copies(i, c):
            cp.wait_send()
        for cp in group_copies(i, lax.rem(c + 2 * g - 1 - i, g)):
            cp.wait_recv()
        return carry

    def wait_outer(i, carry):
        outer_copy(i, q).wait_send()
        outer_copy(i, lax.rem(q + 2 * g - 1 - i, g)).wait_recv()
        return carry

    lax.fori_loop(0, g - 1, wait_group, 0)
    lax.fori_loop(0, g - 1, wait_outer, 0)
    own[1].wait()
    own[2].wait()


def gather_all(picked, pts, prev, g):
    dma = pltpu.SemaphoreType.DMA
    return pl.pallas_call(
        functools.partial(gather_kernel, g),
        out_shape=(
            jax.ShapeDtypeStruct((g, g) + picked.shape, picked.dtype),
            jax.ShapeDtypeStruct((g,) + pts.shape, pts.dtype),
            jax.ShapeDtypeStruct((g,) + prev.shape, prev.dtype),
        ),
        in_specs=[ANY, ANY, ANY],
        out_specs=(ANY, ANY, ANY),
        scratch_shapes=[dma((g,)) for _ in range(8)] + [dma((3,))],
        compiler_params=pltpu.CompilerParams(has_side_effects=True, collective_id=0),
    )(picked, pts, prev)


def scatter_kernel(g, part, total_out, stage1, mid, stage2,
                   out_send, out_recv, in_send, in_recv, local_sem):
    c, q, w = coords()
    barrier = pltpu.get_barrier_semaphore()
    n = greet_all(barrier, lambda i: dev(c, q, lax.rem(w + 1 + i, g)), g - 1, 0)
    n = greet_all(barrier, lambda i: dev(c, lax.rem(q + 1 + i, g), w), g - 1, n)
    pl.semaphore_wait(barrier, n)
    own1 = pltpu.make_async_copy(part.at[q], stage1.at[q], local_sem.at[0])
    own1.start()

    def outer_copy(i, src):
        peer = lax.rem(q + 1 + i, g)
        return pltpu.make_async_remote_copy(
            src_ref=part.at[peer], dst_ref=stage1.at[src], send_sem=out_send.at[i],
            recv_sem=out_recv.at[src], device_id=dev(c, peer, w), device_id_type=MESH_ID)

    def inner_copy(i, src):
        peer = lax.rem(w + 1 + i, g)
        return pltpu.make_async_remote_copy(
            src_ref=mid.at[peer], dst_ref=stage2.at[src], send_sem=in_send.at[i],
            recv_sem=in_recv.at[src], device_id=dev(c, q, peer), device_id_type=MESH_ID)

    def start_outer(i, carry):
        outer_copy(i, q).start()
        return carry

    lax.fori_loop(0, g - 1, start_outer, 0)

    def wait_outer(i, carry):
        outer_copy(i, q).wait_send()
        outer_copy(i, lax.rem(q + 2 * g - 1 - i, g)).wait_recv()
        return carry

    lax.fori_loop(0, g - 1, wait_outer, 0)
    own1.wait()
    mid[...] = jnp.sum(stage1[...], axis=0)[:, None, :]
    own2 = pltpu.make_async_copy(mid.at[w], stage2.at[w], local_sem.at[1])
    own2.start()

    def start_inner(i, carry):
        inner_copy(i, w).start()
        return carry

    lax.fori_loop(0, g - 1, start_inner, 0)

    def wait_inner(i, carry):
        inner_copy(i, w).wait_send()
        inner_copy(i, lax.rem(w + 2 * g - 1 - i, g)).wait_recv()
        return carry

    lax.fori_loop(0, g - 1, wait_inner, 0)
    own2.wait()
    total_out[...] = jnp.sum(stage2[...], axis=0)


def scatter_all(part, g):
    dma = pltpu.SemaphoreType.DMA
    vmem = pl.BlockSpec(memory_space=pltpu.VMEM)
    width = part.shape[-1]
    return pl.pallas_call(
        functools.partial(scatter_kernel, g),
        out_shape=jax.ShapeDtypeStruct((1, width), part.dtype),
        in_specs=[vmem],
        out_specs=vmem,
        scratch_shapes=[
            pltpu.VMEM((g, g, width), jnp.float32),
            pltpu.VMEM((g, 1, width), jnp.float32),
            pltpu.VMEM((g, 1, width), jnp.float32),
            dma((g,)), dma((g,)), dma((g,)), dma((g,)), dma((2,)),
        ],
        compiler_params=pltpu.CompilerParams(has_side_effects=True, collective_id=1),
    )(part)


def matern_sums(neg_two_rows, row_sq, col_points, col_coef):
    col_sq = jnp.sum(jnp.square(col_points.astype(jnp.float32)), axis=1)
    neg_two_dot = lax.dot_general(
        neg_two_rows, col_points, (((1,), (1,)), ((), ())), preferred_element_type=jnp.float32
    )
    sq = (row_sq[:, None] + col_sq[None, :]) + neg_two_dot
    distance = jnp.where(sq > 0.0, sq * lax.rsqrt(sq), 0.0)
    m = distance * (-KERNEL_RATE)
    kernel_tile = (1.0 - m) * jnp.exp(m)
    return jnp.sum(kernel_tile * col_coef[None, :], axis=1)


def column_sums(row_feats, piece_points, every_coef):
    neg_two_rows = row_feats
    row_sq = 0.25 * jnp.sum(jnp.square(neg_two_rows.astype(jnp.float32)), axis=1)
    zeros_init = jnp.zeros((row_feats.shape[0],), jnp.float32)
    piece_len = piece_points.shape[0]
    block_len = math.gcd(piece_len, 2048)
    point_blocks = piece_points.reshape(-1, block_len, piece_points.shape[1])
    coef_blocks = every_coef.reshape(-1, block_len)

    def advance(partial_sum, column_block):
        return (
            partial_sum + matern_sums(neg_two_rows, row_sq, column_block[0], column_block[1]),
            None,
        )

    result, unused = lax.scan(advance, zeros_init, (point_blocks, coef_blocks), unroll=True)
    return result


def per_device(n_blk, n_str, points, coefficients, velocity, targets, batch_rows, counts):
    preview = coefficients + MOMENTUM * velocity
    slot_total = batch_rows.shape[0]
    local_size = points.shape[0]
    choose = (batch_rows[:, None] == jnp.arange(local_size, dtype=jnp.int32)[None, :])
    choose = jnp.where(choose, -2.0, 0.0).astype(points.dtype)
    picked = jnp.dot(choose, points, preferred_element_type=jnp.float32).astype(points.dtype)
    g = 8
    lanes = 128
    dense = lambda a: a.reshape(-1, lanes)
    rows_all, pts_all, prev_all = gather_all(
        dense(picked), dense(points), preview.reshape(1, -1), g)
    rows_all, batch_rows, counts = lax.optimization_barrier((rows_all, batch_rows, counts))
    slot_ids = jnp.arange(slot_total, dtype=jnp.int32)
    count_here = counts.reshape((1,))
    in_count = slot_ids < count_here[0]
    group_rows = rows_all.reshape(-1, points.shape[1])
    piece_points = pts_all.reshape(-1, points.shape[1])
    every_coef = prev_all.reshape(-1)
    partial_value = column_sums(group_rows, piece_points, every_coef)
    kernel_rows = scatter_all(partial_value.reshape(g, g, slot_total), g).reshape(-1)
    scatter_rows = (batch_rows[:, None] == jnp.arange(local_size, dtype=jnp.int32)[None, :]).astype(
        jnp.float32
    )
    adjust = NOISE_VAR * preview - targets
    looked_up = jnp.dot(scatter_rows, adjust, precision=lax.Precision.HIGHEST)
    residual = jnp.where(in_count, kernel_rows + looked_up, 0.0)
    update_sum = jnp.dot(residual, scatter_rows, precision=lax.Precision.HIGHEST)
    new_velocity = MOMENTUM * velocity - STEP_SIZE * update_sum
    new_coefficients = coefficients + new_velocity
    return (new_coefficients, new_velocity)


def solution(mesh):
    n_blk = mesh.shape["blk"]
    n_str = mesh.shape["stripe"]
    in_specs = (
        P(("blk", "stripe"), None),
        P(("blk", "stripe")),
        P(("blk", "stripe")),
        P(("blk", "stripe")),
        P(("blk", "stripe")),
        P("blk", "stripe"),
    )
    out_specs = (P(("blk", "stripe")), P(("blk", "stripe")))
    return jax.shard_map(
        functools.partial(per_device, n_blk, n_str), mesh=mesh, in_specs=in_specs,
        out_specs=out_specs, check_vma=False
    )
```

```python
import functools
import math

import jax
import jax.numpy as jnp
from jax import lax
from jax.experimental import pallas as pl
from jax.experimental.pallas import tpu as pltpu
from jax.sharding import PartitionSpec as P

MOMENTUM = 0.9
STEP_SIZE = 1.0
NOISE_VAR = 8.0
KERNEL_RATE = 3.0**0.5 / 6.0

MESH_ID = pl.DeviceIdType.MESH
ANY = pl.BlockSpec(memory_space=pl.ANY)


def coords():
    b = lax.axis_index("blk")
    s = lax.axis_index("stripe")
    core = lax.rem(s, 2)
    z_hi = lax.rem(s // 2, 2)
    x = lax.rem(s // 4, 4)
    y = s // 16
    c = lax.rem(b, 2) * 4 + lax.rem(x, 2) * 2 + core
    q = y * 2 + x // 2
    w = (b // 2) * 2 + z_hi
    return c, q, w


def dev(c, q, w):
    b = (w // 2) * 2 + c // 4
    z_hi = lax.rem(w, 2)
    y = q // 2
    x = lax.rem(q, 2) * 2 + lax.rem(c // 2, 2)
    core = lax.rem(c, 2)
    return (b, ((y * 4 + x) * 2 + z_hi) * 2 + core)


def greet_all(barrier, peers_of, n, total):
    def greet(i, carry):
        pl.semaphore_signal(barrier, 1, device_id=peers_of(i), device_id_type=MESH_ID)
        return carry

    lax.fori_loop(0, n, greet, 0)
    return total + n


def gather_kernel(g, picked, pts, prev, rows_out, pts_out, prev_out,
                  in_send, in_recv, out_send, out_recv, pt_send, pt_recv, pv_send, pv_recv,
                  local_sem):
    c, q, w = coords()
    barrier = pltpu.get_barrier_semaphore()
    n = greet_all(barrier, lambda i: dev(c, q, lax.rem(w + 1 + i, g)), g - 1, 0)
    n = greet_all(barrier, lambda i: dev(c, lax.rem(q + 1 + i, g), w), g - 1, n)
    n = greet_all(barrier, lambda i: dev(lax.rem(c + 1 + i, g), q, w), g - 1, n)
    pl.semaphore_wait(barrier, n)
    own = [
        pltpu.make_async_copy(picked, rows_out.at[q, w], local_sem.at[0]),
        pltpu.make_async_copy(pts, pts_out.at[c], local_sem.at[1]),
        pltpu.make_async_copy(prev, prev_out.at[c], local_sem.at[2]),
    ]
    for cp in own:
        cp.start()

    def inner_copy(i, src):
        return pltpu.make_async_remote_copy(
            src_ref=picked, dst_ref=rows_out.at[q, src], send_sem=in_send.at[i],
            recv_sem=in_recv.at[src], device_id=dev(c, q, lax.rem(w + 1 + i, g)),
            device_id_type=MESH_ID)

    def outer_copy(i, src):
        return pltpu.make_async_remote_copy(
            src_ref=rows_out.at[q], dst_ref=rows_out.at[src], send_sem=out_send.at[i],
            recv_sem=out_recv.at[src], device_id=dev(c, lax.rem(q + 1 + i, g), w),
            device_id_type=MESH_ID)

    def group_copies(i, src):
        peer = dev(lax.rem(c + 1 + i, g), q, w)
        return (
            pltpu.make_async_remote_copy(
                src_ref=pts, dst_ref=pts_out.at[src], send_sem=pt_send.at[i],
                recv_sem=pt_recv.at[src], device_id=peer, device_id_type=MESH_ID),
            pltpu.make_async_remote_copy(
                src_ref=prev, dst_ref=prev_out.at[src], send_sem=pv_send.at[i],
                recv_sem=pv_recv.at[src], device_id=peer, device_id_type=MESH_ID),
        )

    def start_inner(i, carry):
        inner_copy(i, w).start()
        return carry

    def start_group(i, carry):
        for cp in group_copies(i, c):
            cp.start()
        return carry

    lax.fori_loop(0, g - 1, start_inner, 0)
    lax.fori_loop(0, g - 1, start_group, 0)

    def wait_inner(i, carry):
        inner_copy(i, w).wait_send()
        inner_copy(i, lax.rem(w + 2 * g - 1 - i, g)).wait_recv()
        return carry

    lax.fori_loop(0, g - 1, wait_inner, 0)
    own[0].wait()

    def start_outer(i, carry):
        outer_copy(i, q).start()
        return carry

    lax.fori_loop(0, g - 1, start_outer, 0)

    def wait_group(i, carry):
        for cp in group_copies(i, c):
            cp.wait_send()
        for cp in group_copies(i, lax.rem(c + 2 * g - 1 - i, g)):
            cp.wait_recv()
        return carry

    def wait_outer(i, carry):
        outer_copy(i, q).wait_send()
        outer_copy(i, lax.rem(q + 2 * g - 1 - i, g)).wait_recv()
        return carry

    lax.fori_loop(0, g - 1, wait_group, 0)
    lax.fori_loop(0, g - 1, wait_outer, 0)
    own[1].wait()
    own[2].wait()


def gather_all(picked, pts, prev, g):
    dma = pltpu.SemaphoreType.DMA
    return pl.pallas_call(
        functools.partial(gather_kernel, g),
        out_shape=(
            jax.ShapeDtypeStruct((g, g) + picked.shape, picked.dtype),
            jax.ShapeDtypeStruct((g,) + pts.shape, pts.dtype),
            jax.ShapeDtypeStruct((g,) + prev.shape, prev.dtype),
        ),
        in_specs=[ANY, ANY, ANY],
        out_specs=(ANY, ANY, ANY),
        scratch_shapes=[dma((g,)) for _ in range(8)] + [dma((3,))],
        compiler_params=pltpu.CompilerParams(has_side_effects=True, collective_id=0),
    )(picked, pts, prev)


def scatter_kernel(g, part, total_out, stage1, mid, stage2,
                   out_send, out_recv, in_send, in_recv, local_sem):
    c, q, w = coords()
    barrier = pltpu.get_barrier_semaphore()
    n = greet_all(barrier, lambda i: dev(c, q, lax.rem(w + 1 + i, g)), g - 1, 0)
    n = greet_all(barrier, lambda i: dev(c, lax.rem(q + 1 + i, g), w), g - 1, n)
    pl.semaphore_wait(barrier, n)
    own1 = pltpu.make_async_copy(part.at[q], stage1.at[q], local_sem.at[0])
    own1.start()

    def outer_copy(i, src):
        peer = lax.rem(q + 1 + i, g)
        return pltpu.make_async_remote_copy(
            src_ref=part.at[peer], dst_ref=stage1.at[src], send_sem=out_send.at[i],
            recv_sem=out_recv.at[src], device_id=dev(c, peer, w), device_id_type=MESH_ID)

    def inner_copy(i, src):
        peer = lax.rem(w + 1 + i, g)
        return pltpu.make_async_remote_copy(
            src_ref=mid.at[peer], dst_ref=stage2.at[src], send_sem=in_send.at[i],
            recv_sem=in_recv.at[src], device_id=dev(c, q, peer), device_id_type=MESH_ID)

    def start_outer(i, carry):
        outer_copy(i, q).start()
        return carry

    lax.fori_loop(0, g - 1, start_outer, 0)

    def wait_outer(i, carry):
        outer_copy(i, q).wait_send()
        outer_copy(i, lax.rem(q + 2 * g - 1 - i, g)).wait_recv()
        return carry

    lax.fori_loop(0, g - 1, wait_outer, 0)
    own1.wait()
    mid[...] = jnp.sum(stage1[...], axis=0)[:, None, :]
    own2 = pltpu.make_async_copy(mid.at[w], stage2.at[w], local_sem.at[1])
    own2.start()

    def start_inner(i, carry):
        inner_copy(i, w).start()
        return carry

    lax.fori_loop(0, g - 1, start_inner, 0)

    def wait_inner(i, carry):
        inner_copy(i, w).wait_send()
        inner_copy(i, lax.rem(w + 2 * g - 1 - i, g)).wait_recv()
        return carry

    lax.fori_loop(0, g - 1, wait_inner, 0)
    own2.wait()
    total_out[...] = jnp.sum(stage2[...], axis=0)


def scatter_all(part, g):
    dma = pltpu.SemaphoreType.DMA
    vmem = pl.BlockSpec(memory_space=pltpu.VMEM)
    width = part.shape[-1]
    return pl.pallas_call(
        functools.partial(scatter_kernel, g),
        out_shape=jax.ShapeDtypeStruct((1, width), part.dtype),
        in_specs=[vmem],
        out_specs=vmem,
        scratch_shapes=[
            pltpu.VMEM((g, g, width), jnp.float32),
            pltpu.VMEM((g, 1, width), jnp.float32),
            pltpu.VMEM((g, 1, width), jnp.float32),
            dma((g,)), dma((g,)), dma((g,)), dma((g,)), dma((2,)),
        ],
        compiler_params=pltpu.CompilerParams(has_side_effects=True, collective_id=1),
    )(part)


def matern_sums(neg_two_rows, row_sq, col_points, col_coef, col_sq):
    neg_two_dot = lax.dot_general(
        neg_two_rows, col_points, (((1,), (1,)), ((), ())), preferred_element_type=jnp.float32
    )
    sq = (row_sq[:, None] + col_sq[None, :]) + neg_two_dot
    distance = jnp.where(sq > 0.0, sq * lax.rsqrt(sq), 0.0)
    m = distance * (-KERNEL_RATE)
    kernel_tile = (1.0 - m) * jnp.exp(m)
    return jnp.sum(kernel_tile * col_coef[None, :], axis=1)


def column_sums(row_feats, piece_points, every_coef):
    neg_two_rows = row_feats
    row_sq = 0.25 * jnp.sum(jnp.square(neg_two_rows.astype(jnp.float32)), axis=1)
    zeros_init = jnp.zeros((row_feats.shape[0],), jnp.float32)
    piece_len = piece_points.shape[0]
    block_len = math.gcd(piece_len, 2048)
    point_blocks = piece_points.reshape(-1, block_len, piece_points.shape[1])
    coef_blocks = every_coef.reshape(-1, block_len)
    sq_blocks = jnp.sum(jnp.square(piece_points.astype(jnp.float32)), axis=1).reshape(-1, block_len)

    def advance(partial_sum, column_block):
        return (
            partial_sum
            + matern_sums(neg_two_rows, row_sq, column_block[0], column_block[1], column_block[2]),
            None,
        )

    result, unused = lax.scan(advance, zeros_init, (point_blocks, coef_blocks, sq_blocks))
    return result


def per_device(n_blk, n_str, points, coefficients, velocity, targets, batch_rows, counts):
    preview = coefficients + MOMENTUM * velocity
    slot_total = batch_rows.shape[0]
    local_size = points.shape[0]
    choose = (batch_rows[:, None] == jnp.arange(local_size, dtype=jnp.int32)[None, :])
    choose = jnp.where(choose, -2.0, 0.0).astype(points.dtype)
    picked = jnp.dot(choose, points, preferred_element_type=jnp.float32).astype(points.dtype)
    g = 8
    lanes = 128
    dense = lambda a: a.reshape(-1, lanes)
    rows_all, pts_all, prev_all = gather_all(
        dense(picked), dense(points), preview.reshape(1, -1), g)
    rows_all, batch_rows, counts = lax.optimization_barrier((rows_all, batch_rows, counts))
    slot_ids = jnp.arange(slot_total, dtype=jnp.int32)
    count_here = counts.reshape((1,))
    in_count = slot_ids < count_here[0]
    group_rows = rows_all.reshape(-1, points.shape[1])
    piece_points = pts_all.reshape(-1, points.shape[1])
    every_coef = prev_all.reshape(-1)
    partial_value = column_sums(group_rows, piece_points, every_coef)
    kernel_rows = scatter_all(partial_value.reshape(g, g, slot_total), g).reshape(-1)
    scatter_rows = (batch_rows[:, None] == jnp.arange(local_size, dtype=jnp.int32)[None, :]).astype(
        jnp.float32
    )
    adjust = NOISE_VAR * preview - targets
    looked_up = jnp.dot(scatter_rows, adjust, precision=lax.Precision.HIGHEST)
    residual = jnp.where(in_count, kernel_rows + looked_up, 0.0)
    update_sum = jnp.dot(residual, scatter_rows, precision=lax.Precision.HIGHEST)
    new_velocity = MOMENTUM * velocity - STEP_SIZE * update_sum
    new_coefficients = coefficients + new_velocity
    return (new_coefficients, new_velocity)


def solution(mesh):
    n_blk = mesh.shape["blk"]
    n_str = mesh.shape["stripe"]
    in_specs = (
        P(("blk", "stripe"), None),
        P(("blk", "stripe")),
        P(("blk", "stripe")),
        P(("blk", "stripe")),
        P(("blk", "stripe")),
        P("blk", "stripe"),
    )
    out_specs = (P(("blk", "stripe")), P(("blk", "stripe")))
    return jax.shard_map(
        functools.partial(per_device, n_blk, n_str), mesh=mesh, in_specs=in_specs,
        out_specs=out_specs, check_vma=False
    )
```

```python
import functools
import math

import jax
import jax.numpy as jnp
from jax import lax
from jax.experimental import pallas as pl
from jax.experimental.pallas import tpu as pltpu
from jax.sharding import PartitionSpec as P

MOMENTUM = 0.9
STEP_SIZE = 1.0
NOISE_VAR = 8.0
KERNEL_RATE = 3.0**0.5 / 6.0

MESH_ID = pl.DeviceIdType.MESH
ANY = pl.BlockSpec(memory_space=pl.ANY)


def coords():
    b = lax.axis_index("blk")
    s = lax.axis_index("stripe")
    core = lax.rem(s, 2)
    z_hi = lax.rem(s // 2, 2)
    x = lax.rem(s // 4, 4)
    y = s // 16
    c = lax.rem(b, 2) * 4 + lax.rem(x, 2) * 2 + core
    q = y * 2 + x // 2
    w = (b // 2) * 2 + z_hi
    return c, q, w


def dev(c, q, w):
    b = (w // 2) * 2 + c // 4
    z_hi = lax.rem(w, 2)
    y = q // 2
    x = lax.rem(q, 2) * 2 + lax.rem(c // 2, 2)
    core = lax.rem(c, 2)
    return (b, ((y * 4 + x) * 2 + z_hi) * 2 + core)


def greet_all(barrier, peers_of, n, total):
    def greet(i, carry):
        pl.semaphore_signal(barrier, 1, device_id=peers_of(i), device_id_type=MESH_ID)
        return carry

    lax.fori_loop(0, n, greet, 0)
    return total + n


def gather_kernel(g, picked, pts, prev, rows_out, pts_out, prev_out,
                  in_send, in_recv, out_send, out_recv, pt_send, pt_recv, pv_send, pv_recv,
                  local_sem):
    c, q, w = coords()
    barrier = pltpu.get_barrier_semaphore()
    n = greet_all(barrier, lambda i: dev(c, q, lax.rem(w + 1 + i, g)), g - 1, 0)
    n = greet_all(barrier, lambda i: dev(c, lax.rem(q + 1 + i, g), w), g - 1, n)
    n = greet_all(barrier, lambda i: dev(lax.rem(c + 1 + i, g), q, w), g - 1, n)
    pl.semaphore_wait(barrier, n)
    own = [
        pltpu.make_async_copy(picked, rows_out.at[q, w], local_sem.at[0]),
        pltpu.make_async_copy(pts, pts_out.at[c], local_sem.at[1]),
        pltpu.make_async_copy(prev, prev_out.at[c], local_sem.at[2]),
    ]
    for cp in own:
        cp.start()

    def inner_copy(i, src):
        return pltpu.make_async_remote_copy(
            src_ref=picked, dst_ref=rows_out.at[q, src], send_sem=in_send.at[i],
            recv_sem=in_recv.at[src], device_id=dev(c, q, lax.rem(w + 1 + i, g)),
            device_id_type=MESH_ID)

    def outer_copy(i, src):
        return pltpu.make_async_remote_copy(
            src_ref=rows_out.at[q], dst_ref=rows_out.at[src], send_sem=out_send.at[i],
            recv_sem=out_recv.at[src], device_id=dev(c, lax.rem(q + 1 + i, g), w),
            device_id_type=MESH_ID)

    def group_copies(i, src):
        peer = dev(lax.rem(c + 1 + i, g), q, w)
        return (
            pltpu.make_async_remote_copy(
                src_ref=pts, dst_ref=pts_out.at[src], send_sem=pt_send.at[i],
                recv_sem=pt_recv.at[src], device_id=peer, device_id_type=MESH_ID),
            pltpu.make_async_remote_copy(
                src_ref=prev, dst_ref=prev_out.at[src], send_sem=pv_send.at[i],
                recv_sem=pv_recv.at[src], device_id=peer, device_id_type=MESH_ID),
        )

    def start_inner(i, carry):
        inner_copy(i, w).start()
        return carry

    def start_group(i, carry):
        for cp in group_copies(i, c):
            cp.start()
        return carry

    lax.fori_loop(0, g - 1, start_inner, 0)
    lax.fori_loop(0, g - 1, start_group, 0)

    def wait_inner(i, carry):
        inner_copy(i, w).wait_send()
        inner_copy(i, lax.rem(w + 2 * g - 1 - i, g)).wait_recv()
        return carry

    lax.fori_loop(0, g - 1, wait_inner, 0)
    own[0].wait()

    def start_outer(i, carry):
        outer_copy(i, q).start()
        return carry

    lax.fori_loop(0, g - 1, start_outer, 0)

    def wait_group(i, carry):
        for cp in group_copies(i, c):
            cp.wait_send()
        for cp in group_copies(i, lax.rem(c + 2 * g - 1 - i, g)):
            cp.wait_recv()
        return carry

    def wait_outer(i, carry):
        outer_copy(i, q).wait_send()
        outer_copy(i, lax.rem(q + 2 * g - 1 - i, g)).wait_recv()
        return carry

    lax.fori_loop(0, g - 1, wait_group, 0)
    lax.fori_loop(0, g - 1, wait_outer, 0)
    own[1].wait()
    own[2].wait()


def gather_all(picked, pts, prev, g):
    dma = pltpu.SemaphoreType.DMA
    return pl.pallas_call(
        functools.partial(gather_kernel, g),
        out_shape=(
            jax.ShapeDtypeStruct((g, g) + picked.shape, picked.dtype),
            jax.ShapeDtypeStruct((g,) + pts.shape, pts.dtype),
            jax.ShapeDtypeStruct((g,) + prev.shape, prev.dtype),
        ),
        in_specs=[ANY, ANY, ANY],
        out_specs=(ANY, ANY, ANY),
        scratch_shapes=[dma((g,)) for _ in range(8)] + [dma((3,))],
        compiler_params=pltpu.CompilerParams(has_side_effects=True, collective_id=0),
    )(picked, pts, prev)


def scatter_kernel(g, part, total_out, stage1, mid, stage2,
                   out_send, out_recv, in_send, in_recv, local_sem):
    c, q, w = coords()
    barrier = pltpu.get_barrier_semaphore()
    n = greet_all(barrier, lambda i: dev(c, q, lax.rem(w + 1 + i, g)), g - 1, 0)
    n = greet_all(barrier, lambda i: dev(c, lax.rem(q + 1 + i, g), w), g - 1, n)
    pl.semaphore_wait(barrier, n)
    own1 = pltpu.make_async_copy(part.at[w], stage1.at[w], local_sem.at[0])
    own1.start()

    def inner_copy(i, src):
        peer = lax.rem(w + 1 + i, g)
        return pltpu.make_async_remote_copy(
            src_ref=part.at[peer], dst_ref=stage1.at[src], send_sem=in_send.at[i],
            recv_sem=in_recv.at[src], device_id=dev(c, q, peer), device_id_type=MESH_ID)

    def outer_copy(i, src):
        peer = lax.rem(q + 1 + i, g)
        return pltpu.make_async_remote_copy(
            src_ref=mid.at[peer], dst_ref=stage2.at[src], send_sem=out_send.at[i],
            recv_sem=out_recv.at[src], device_id=dev(c, peer, w), device_id_type=MESH_ID)

    def start_inner(i, carry):
        inner_copy(i, w).start()
        return carry

    lax.fori_loop(0, g - 1, start_inner, 0)

    def wait_inner(i, carry):
        inner_copy(i, w).wait_send()
        inner_copy(i, lax.rem(w + 2 * g - 1 - i, g)).wait_recv()
        return carry

    lax.fori_loop(0, g - 1, wait_inner, 0)
    own1.wait()
    mid[...] = jnp.sum(stage1[...], axis=0)[:, None, :]
    own2 = pltpu.make_async_copy(mid.at[q], stage2.at[q], local_sem.at[1])
    own2.start()

    def start_outer(i, carry):
        outer_copy(i, q).start()
        return carry

    lax.fori_loop(0, g - 1, start_outer, 0)

    def wait_outer(i, carry):
        outer_copy(i, q).wait_send()
        outer_copy(i, lax.rem(q + 2 * g - 1 - i, g)).wait_recv()
        return carry

    lax.fori_loop(0, g - 1, wait_outer, 0)
    own2.wait()
    total_out[...] = jnp.sum(stage2[...], axis=0)


def scatter_all(part, g):
    dma = pltpu.SemaphoreType.DMA
    vmem = pl.BlockSpec(memory_space=pltpu.VMEM)
    width = part.shape[-1]
    return pl.pallas_call(
        functools.partial(scatter_kernel, g),
        out_shape=jax.ShapeDtypeStruct((1, width), part.dtype),
        in_specs=[vmem],
        out_specs=vmem,
        scratch_shapes=[
            pltpu.VMEM((g, g, width), jnp.float32),
            pltpu.VMEM((g, 1, width), jnp.float32),
            pltpu.VMEM((g, 1, width), jnp.float32),
            dma((g,)), dma((g,)), dma((g,)), dma((g,)), dma((2,)),
        ],
        compiler_params=pltpu.CompilerParams(has_side_effects=True, collective_id=1),
    )(part)


def matern_sums(neg_two_rows, row_sq, col_points, col_coef):
    col_sq = jnp.sum(jnp.square(col_points.astype(jnp.float32)), axis=1)
    neg_two_dot = lax.dot_general(
        neg_two_rows, col_points, (((1,), (1,)), ((), ())), preferred_element_type=jnp.float32
    )
    sq = (row_sq[:, None] + col_sq[None, :]) + neg_two_dot
    distance = jnp.where(sq > 0.0, sq * lax.rsqrt(sq), 0.0)
    m = distance * (-KERNEL_RATE)
    kernel_tile = (1.0 - m) * jnp.exp(m)
    return jnp.sum(kernel_tile * col_coef[None, :], axis=1)


def column_sums(row_feats, piece_points, every_coef):
    neg_two_rows = row_feats
    row_sq = 0.25 * jnp.sum(jnp.square(neg_two_rows.astype(jnp.float32)), axis=1)
    zeros_init = jnp.zeros((row_feats.shape[0],), jnp.float32)
    piece_len = piece_points.shape[0]
    block_len = math.gcd(piece_len, 2048)
    point_blocks = piece_points.reshape(-1, block_len, piece_points.shape[1])
    coef_blocks = every_coef.reshape(-1, block_len)

    def advance(partial_sum, column_block):
        return (
            partial_sum + matern_sums(neg_two_rows, row_sq, column_block[0], column_block[1]),
            None,
        )

    result, unused = lax.scan(advance, zeros_init, (point_blocks, coef_blocks))
    return result


def per_device(n_blk, n_str, points, coefficients, velocity, targets, batch_rows, counts):
    preview = coefficients + MOMENTUM * velocity
    slot_total = batch_rows.shape[0]
    local_size = points.shape[0]
    choose = (batch_rows[:, None] == jnp.arange(local_size, dtype=jnp.int32)[None, :])
    choose = jnp.where(choose, -2.0, 0.0).astype(points.dtype)
    picked = jnp.dot(choose, points, preferred_element_type=jnp.float32).astype(points.dtype)
    g = 8
    lanes = 128
    dense = lambda a: a.reshape(-1, lanes)
    rows_all, pts_all, prev_all = gather_all(
        dense(picked), dense(points), preview.reshape(1, -1), g)
    rows_all, batch_rows, counts = lax.optimization_barrier((rows_all, batch_rows, counts))
    slot_ids = jnp.arange(slot_total, dtype=jnp.int32)
    count_here = counts.reshape((1,))
    in_count = slot_ids < count_here[0]
    group_rows = rows_all.reshape(-1, points.shape[1])
    piece_points = pts_all.reshape(-1, points.shape[1])
    every_coef = prev_all.reshape(-1)
    partial_value = column_sums(group_rows, piece_points, every_coef)
    by_w = partial_value.reshape(g, g, slot_total).transpose(1, 0, 2)
    kernel_rows = scatter_all(by_w, g).reshape(-1)
    scatter_rows = (batch_rows[:, None] == jnp.arange(local_size, dtype=jnp.int32)[None, :]).astype(
        jnp.float32
    )
    adjust = NOISE_VAR * preview - targets
    looked_up = jnp.dot(scatter_rows, adjust, precision=lax.Precision.HIGHEST)
    residual = jnp.where(in_count, kernel_rows + looked_up, 0.0)
    update_sum = jnp.dot(residual, scatter_rows, precision=lax.Precision.HIGHEST)
    new_velocity = MOMENTUM * velocity - STEP_SIZE * update_sum
    new_coefficients = coefficients + new_velocity
    return (new_coefficients, new_velocity)


def solution(mesh):
    n_blk = mesh.shape["blk"]
    n_str = mesh.shape["stripe"]
    in_specs = (
        P(("blk", "stripe"), None),
        P(("blk", "stripe")),
        P(("blk", "stripe")),
        P(("blk", "stripe")),
        P(("blk", "stripe")),
        P("blk", "stripe"),
    )
    out_specs = (P(("blk", "stripe")), P(("blk", "stripe")))
    return jax.shard_map(
        functools.partial(per_device, n_blk, n_str), mesh=mesh, in_specs=in_specs,
        out_specs=out_specs, check_vma=False
    )
```
